32 devices in a mesh: section: 2 (over x), dp: 4 (over z), tensor: 4 (over y, core).
Axes of the slice: x: 2, y: 2, z: 4, core: 2. Of those that a mesh axis runs over, the one named last changes fastest.
Arguments:
- text_in: bfloat16 [2, 2048, 768], P(None, ('dp', 'tensor')), may hold values from -6 to 6
- layout_in: bfloat16 [2, 2048, 192], P(None, ('dp', 'tensor')), may hold values from -6 to 6
- text_cot: bfloat16 [2, 2048, 768], P(None, ('dp', 'tensor')), may hold values from -6 to 6
- layout_cot: bfloat16 [2, 2048, 192], P(None, ('dp', 'tensor')), may hold values from -6 to 6
- token_mask: int32 [2, 2048], P(None, ('dp', 'tensor')), may hold values 0 or 1
- box_mask: int32 [2, 2048], P(None, ('dp', 'tensor')), may hold values 0 or 1
- segments: int32 [2, 4, 512], P(None, 'dp'), may hold values from 0 to 3, never falling along the last dimension, each value on 1 to 256 neighbouring positions
- text_qkv: bfloat16 [2, 3, 768, 768], P('section', None, None, 'tensor'), may hold values from -0.21875 to 0.21875
- text_qv_bias: float32 [2, 2, 768], P('section', None, 'tensor'), may hold values from -1.5 to 1.5
- text_out_w: bfloat16 [2, 768, 768], P('section', 'tensor'), may hold values from -1.75 to 1.75
- text_ffn_in: bfloat16 [2, 768, 3072], P('section', None, 'tensor'), may hold values from -0.21875 to 0.21875
- text_ffn_bias: float32 [2, 3072], P('section', 'tensor'), may hold values from -1.5 to 1.5
- text_ffn_out: bfloat16 [2, 3072, 768], P('section', 'tensor'), may hold values from -0.21875 to 0.21875
- text_gains: float32 [2, 2, 768], P('section'), may hold values from 0.5 to 1.5
- text_biases: float32 [2, 4, 768], P('section'), may hold values from -1.5 to 1.5
- layout_qkv: bfloat16 [2, 3, 192, 192], P('section', None, None, 'tensor'), may hold values from -0.4375 to 0.4375
- layout_qv_bias: float32 [2, 2, 192], P('section', None, 'tensor'), may hold values from -1.5 to 1.5
- layout_out_w: bfloat16 [2, 192, 192], P('section', 'tensor'), may hold values from -3.5 to 3.5
- layout_ffn_in: bfloat16 [2, 192, 768], P('section', None, 'tensor'), may hold values from -0.4375 to 0.4375
- layout_ffn_bias: float32 [2, 768], P('section', 'tensor'), may hold values from -1.5 to 1.5
- layout_ffn_out: bfloat16 [2, 768, 192], P('section', 'tensor'), may hold values from -0.4375 to 0.4375
- layout_gains: float32 [2, 2, 192], P('section'), may hold values from 0.5 to 1.5
- layout_biases: float32 [2, 4, 192], P('section'), may hold values from -1.5 to 1.5
Outputs:
- text_hidden: bfloat16 [2, 2, 2048, 768], P('section', None, ('dp', 'tensor'))
- layout_hidden: bfloat16 [2, 2, 2048, 192], P('section', None, ('dp', 'tensor'))
- text_input_grad: bfloat16 [2, 2, 2048, 768], P('section', None, ('dp', 'tensor'))
- layout_input_grad: bfloat16 [2, 2, 2048, 192], P('section', None, ('dp', 'tensor'))
- grad_text_qkv: float32 [2, 3, 768, 768], P('section', None, 'dp', 'tensor')
- grad_text_qv_bias: float32 [2, 2, 768], P('section', None, 'tensor')
- grad_text_out_w: float32 [2, 768, 768], P('section', 'tensor', 'dp')
- grad_text_ffn_in: float32 [2, 768, 3072], P('section', 'dp', 'tensor')
- grad_text_ffn_bias: float32 [2, 3072], P('section', 'tensor')
- grad_text_ffn_out: float32 [2, 3072, 768], P('section', 'tensor', 'dp')
- grad_text_gains: float32 [2, 2, 768], P('section')
- grad_text_biases: float32 [2, 4, 768], P('section')
- grad_layout_qkv: float32 [2, 3, 192, 192], P('section', None, 'dp', 'tensor')
- grad_layout_qv_bias: float32 [2, 2, 192], P('section', None, 'tensor')
- grad_layout_out_w: float32 [2, 192, 192], P('section', 'tensor', 'dp')
- grad_layout_ffn_in: float32 [2, 192, 768], P('section', 'dp', 'tensor')
- grad_layout_ffn_bias: float32 [2, 768], P('section', 'tensor')
- grad_layout_ffn_out: float32 [2, 768, 192], P('section', 'tensor', 'dp')
- grad_layout_gains: float32 [2, 2, 192], P('section')
- grad_layout_biases: float32 [2, 4, 192], P('section')
The draws below stay inside these ranges and needn't reach their ends.
Inputs may be any that keep to these rules, and one draw needn't show every extreme that they name: `segments`: within a page the ids never fall and each document holds 1 to 256 tokens.
All inputs are finite; a program needn't handle non-finite values. No bound on the sum of `token_mask` or of `box_mask` on one device may be relied on, other than what follows from the above.
Results may differ from the reference program's by a relative error of at most 0.038.
Values may be sent and summed in bfloat16 or wider, within the bound.
No kernel may reach another device: no remote copies, remote signals or barrier semaphores. Data moves between devices by JAX's collectives and lax.ppermute only.
A program may use at most 192 MiB of HBM per device.

```python
import math
import jax
import jax.numpy as jnp
import numpy as np
from jax import lax

HEAD = 64
LHEAD = 16
FF = 3072
FFL = 768
PAGE = 512
MICRO = 2
D = 768
DL = 192
LAYERS = 2
PAGES = 4
TOKENS = 2048
N_DP = 4


def touch_ends(values, key, least, top_value):
    spot = [jax.random.randint(jax.random.fold_in(key, axis), (), 0, length) for axis, length in enumerate(values.shape)]
    longest = values.shape.index(max(values.shape))
    beside = spot[:longest] + [(spot[longest] + 1) % values.shape[longest]] + spot[longest + 1:]
    return values.at[tuple(spot)].set(least).at[tuple(beside)].set(top_value)


def block_scale(stream_key, extent, shards, low, high):
    factor_of = 1.0
    for position, blocks in shards:
        heights = jax.random.uniform(jax.random.fold_in(jax.random.fold_in(stream_key, 6), position), (blocks,), jnp.float32, low / len(shards), high / len(shards))
        factor_of = factor_of * jnp.repeat(jnp.exp(heights), extent[position] // blocks).reshape((-1,) + (1,) * (len(extent) - 1 - position))
    return factor_of


def length_profile(amount, total, limit, lean):
    weights = [(1 << 20) // math.isqrt(rank ** lean) + 1 for rank in range(2, amount + 1)]
    spare, holding = total - limit - (amount - 1), [1] * (amount - 1)
    while spare > 0:
        candidates = [i for i in range(amount - 1) if holding[i] < limit]
        whole, budget = sum([weights[i] for i in candidates]), spare
        for i in candidates:
            addition = min(limit - holding[i], max(1, budget * weights[i] // whole), spare)
            holding[i] = holding[i] + addition
            spare = spare - addition
    return np.array([limit] + holding)


def uneven_parts(own_key, number_of, total, bound, skew):
    if number_of == 2:
        one = jax.random.randint(own_key, (), max(1, total - bound), min(bound, total - 1) + 1)
        return jnp.stack([one, total - one])
    lengths = jnp.asarray(length_profile(number_of, total, bound, skew), jnp.int32)
    couples = (number_of - 1) // 2
    donor, receiver = lengths[1:1 + 2 * couples:2], lengths[2:2 + 2 * couples:2]
    margin = jnp.minimum(donor - 1, bound - receiver)
    moved = jax.random.randint(jax.random.fold_in(own_key, 1), (couples,), 0, 1 << 20) % (margin + 1)
    lengths = lengths.at[1:1 + 2 * couples:2].set(donor - moved).at[2:2 + 2 * couples:2].set(receiver + moved)
    return lengths[jax.random.permutation(jax.random.fold_in(own_key, 2), number_of)]


def bell_draw(stream_key, dims, scale, reach, pieces=(), kind=jnp.bfloat16):
    values = scale * jax.random.normal(stream_key, dims, jnp.float32)
    if pieces:
        values = values * block_scale(stream_key, dims, pieces, -0.22, 0.18)
    return jnp.clip(values, -reach, reach).astype(kind)


def setup_inputs(seed: int = 0) -> dict:
    key_list = jax.random.split(jax.random.key(seed), 24)
    return {
        "text_in": bell_draw(key_list[0], (MICRO, TOKENS, D), 1.0, 6.0, ((1, 16),)),
        "layout_in": bell_draw(key_list[1], (MICRO, TOKENS, DL), 1.0, 6.0, ((1, 16),)),
        "text_cot": bell_draw(key_list[2], (MICRO, TOKENS, D), 1.0, 6.0, ((1, 16),)),
        "layout_cot": bell_draw(key_list[3], (MICRO, TOKENS, DL), 1.0, 6.0, ((1, 16),)),
        "token_mask": touch_ends((jax.random.randint(key_list[4], (MICRO, TOKENS), 0, 100) < 15).astype(jnp.int32), jax.random.fold_in(key_list[4], 1), 0, 1),
        "box_mask": touch_ends((jax.random.randint(key_list[5], (MICRO, TOKENS), 0, 10) < 3).astype(jnp.int32), jax.random.fold_in(key_list[5], 1), 0, 1),
        "segments": jax.vmap(lambda own: jnp.searchsorted(jnp.cumsum(uneven_parts(own, 4, PAGE, PAGE // 2, 0)), jnp.arange(PAGE), side="right"))(jax.random.split(key_list[6], MICRO * PAGES)).reshape((MICRO, PAGES, PAGE)).astype(jnp.int32),
        "text_qkv": bell_draw(key_list[7], (LAYERS, 3, D, D), D ** -0.5, 0.21875, ((0, 2), (3, 4))),
        "text_qv_bias": bell_draw(key_list[8], (LAYERS, 2, D), 0.3, 1.5, ((0, 2), (2, 4)), jnp.float32),
        "text_out_w": bell_draw(key_list[9], (LAYERS, D, D), (max(D // 64, 1)) ** -0.5, 1.75, ((0, 2), (1, 4))),
        "text_ffn_in": bell_draw(key_list[10], (LAYERS, D, FF), D ** -0.5, 0.21875, ((0, 2), (2, 4))),
        "text_ffn_bias": bell_draw(key_list[11], (LAYERS, FF), 0.3, 1.5, ((0, 2), (1, 4)), jnp.float32),
        "text_ffn_out": bell_draw(key_list[12], (LAYERS, FF, D), (FF // 4) ** -0.5, 0.21875, ((0, 2), (1, 4))),
        "text_gains": jnp.clip(1.0 + 0.1 * jax.random.normal(key_list[13], (LAYERS, 2, D), jnp.float32), 0.5, 1.5),
        "text_biases": bell_draw(key_list[14], (LAYERS, 4, D), 0.3, 1.5, ((0, 2),), jnp.float32),
        "layout_qkv": bell_draw(key_list[15], (LAYERS, 3, DL, DL), DL ** -0.5, 0.4375, ((0, 2), (3, 4))),
        "layout_qv_bias": bell_draw(key_list[16], (LAYERS, 2, DL), 0.3, 1.5, ((0, 2), (2, 4)), jnp.float32),
        "layout_out_w": bell_draw(key_list[17], (LAYERS, DL, DL), (max(DL // 64, 1)) ** -0.5, 3.5, ((0, 2), (1, 4))),
        "layout_ffn_in": bell_draw(key_list[18], (LAYERS, DL, FFL), DL ** -0.5, 0.4375, ((0, 2), (2, 4))),
        "layout_ffn_bias": bell_draw(key_list[19], (LAYERS, FFL), 0.3, 1.5, ((0, 2), (1, 4)), jnp.float32),
        "layout_ffn_out": bell_draw(key_list[20], (LAYERS, FFL, DL), (FFL // 4) ** -0.5, 0.4375, ((0, 2), (1, 4))),
        "layout_gains": jnp.clip(1.0 + 0.1 * jax.random.normal(key_list[21], (LAYERS, 2, DL), jnp.float32), 0.5, 1.5),
        "layout_biases": bell_draw(key_list[22], (LAYERS, 4, DL), 0.3, 1.5, ((0, 2),), jnp.float32),
    }


EPS = 1e-05
MASKED = -1000000000.0
HIGH = lax.Precision.HIGHEST

@jax.custom_vjp
def low(v):
    return lax.optimization_barrier(v.astype(jnp.bfloat16)).astype(jnp.float32)

@jax.custom_vjp
def low_back(v):
    return v

def low_keep(v):
    return (low(v), None)

def low_pass(kept, grad):
    return (grad,)

def back_keep(v):
    return (v, None)

def back_low(kept, grad):
    return (low(grad),)
low.defvjp(low_keep, low_pass)
low_back.defvjp(back_keep, back_low)

def heads_of(matrix, width):
    return matrix.reshape(matrix.shape[0], matrix.shape[1] // width, width)

def layer_norm(inputs, gain, shift):
    centred = inputs - lax.optimization_barrier(jnp.mean(inputs, axis=-1, keepdims=True))
    inverse = lax.rsqrt(lax.optimization_barrier(jnp.mean(centred * centred, axis=-1, keepdims=True)) + EPS)
    return centred * inverse * gain + shift

def project(inputs, weights):
    biases = jnp.stack([weights[1][0], jnp.zeros_like(weights[1][0]), weights[1][1]])
    mixed = jnp.einsum('nd,cde->cne', inputs, weights[0], precision=HIGH) + biases[:, None, :]
    return low(low_back(mixed))

def scores(query, keys, width):
    return jnp.einsum('qhd,khd->hqk', heads_of(query, width), heads_of(keys, width), precision=HIGH) * width ** (-0.5)

def mix_values(probs, values, width):
    mixed = jnp.einsum('hqk,khd->qhd', probs, heads_of(values, width), precision=HIGH)
    return low(low_back(mixed.reshape(mixed.shape[0], -1)))

def finish(inputs, attended, weights):
    branch = low_back(jnp.dot(attended, weights[2], precision=HIGH)) + weights[7][0]
    first = layer_norm(inputs + branch, weights[6][0], weights[7][1])
    pre_act = low_back(jnp.dot(low(first), weights[3], precision=HIGH)) + weights[4]
    hidden_act = low(jax.nn.gelu(pre_act, approximate=False))
    ffn_out = low_back(jnp.dot(hidden_act, weights[5], precision=HIGH)) + weights[7][2]
    return low(layer_norm(first + ffn_out, weights[6][1], weights[7][3]))

def one_layer(text, layout, text_w, layout_w, fixed, same_doc):
    mix_text = project(text, text_w)
    mix_layout = project(layout, layout_w)
    score_text = low_back(scores(mix_text[0], mix_text[1], HEAD))
    score_layout = low_back(scores(mix_layout[0], mix_layout[1], LHEAD))
    detached = scores(fixed[0], fixed[1], HEAD)
    probs_text = low(jax.nn.softmax(jnp.where(same_doc, score_text + score_layout, MASKED), axis=-1))
    probs_layout = low(jax.nn.softmax(jnp.where(same_doc, score_layout + detached, MASKED), axis=-1))
    text_out = finish(text, mix_values(probs_text, mix_text[2], HEAD), text_w)
    layout_out = finish(layout, mix_values(probs_layout, mix_layout[2], LHEAD), layout_w)
    return (text_out, layout_out, (mix_text[0], mix_text[1]))

def network(weights, text, layout, probes, fixed, same_doc):
    text_w, layout_w = weights
    hidden_text, hidden_layout, pairs = ([], [], [])
    for layer_index in range(LAYERS):
        text_now = tuple((w[layer_index] for w in text_w))
        layout_now = tuple((w[layer_index] for w in layout_w))
        text = low_back(text + probes[0][layer_index])
        layout = low_back(layout + probes[1][layer_index])
        text, layout, paired = one_layer(text, layout, text_now, layout_now, fixed[layer_index], same_doc)
        hidden_text.append(text)
        hidden_layout.append(layout)
        pairs.append(paired)
    return ((jnp.stack(hidden_text), jnp.stack(hidden_layout)), pairs)

def reference(text_in, layout_in, text_cot, layout_cot, token_mask, box_mask, segments, text_qkv, text_qv_bias, text_out_w, text_ffn_in, text_ffn_bias, text_ffn_out, text_gains, text_biases, layout_qkv, layout_qv_bias, layout_out_w, layout_ffn_in, layout_ffn_bias, layout_ffn_out, layout_gains, layout_biases):
    text_w = tuple((w.astype(jnp.float32) for w in (text_qkv, text_qv_bias, text_out_w, text_ffn_in, text_ffn_bias, text_ffn_out, text_gains, text_biases)))
    layout_w = tuple((w.astype(jnp.float32) for w in (layout_qkv, layout_qv_bias, layout_out_w, layout_ffn_in, layout_ffn_bias, layout_ffn_out, layout_gains, layout_biases)))
    pages_all = MICRO * N_DP

    def paged(array):
        return array.reshape((pages_all, PAGE) + array.shape[2:])
    text_weight = 0.25 + paged(token_mask).astype(jnp.float32)
    layout_weight = 0.25 + paged(box_mask).astype(jnp.float32)
    inputs = (paged(text_in).astype(jnp.float32), paged(layout_in).astype(jnp.float32), paged(text_cot).astype(jnp.float32) * text_weight[..., None], paged(layout_cot).astype(jnp.float32) * layout_weight[..., None], segments.reshape(pages_all, PAGE))

    def one_page(total, page):
        text, layout, cot_text, cot_layout, segment = page
        same_doc = segment[:, None] == segment[None, :]
        probes = (jnp.zeros((LAYERS,) + text.shape, jnp.float32), jnp.zeros((LAYERS,) + layout.shape, jnp.float32))
        fixed = [(jnp.zeros(text.shape, jnp.float32), jnp.zeros(text.shape, jnp.float32))] * LAYERS
        for sweep in range(LAYERS):
            fixed = network((text_w, layout_w), text, layout, probes, fixed, same_doc)[1]

        def run(weights, probe):
            return network(weights, text, layout, probe, fixed, same_doc)[0]
        hidden, pull = jax.vjp(run, (text_w, layout_w), probes)
        cot_all = (jnp.zeros_like(hidden[0]).at[LAYERS - 1].set(cot_text), jnp.zeros_like(hidden[1]).at[LAYERS - 1].set(cot_layout))
        grads, probe_grads = pull(cot_all)
        total = jax.tree.map(jnp.add, total, grads)
        return (total, (hidden[0], hidden[1], probe_grads[0], probe_grads[1]))
    start = jax.tree.map(jnp.zeros_like, (text_w, layout_w))
    total, stacked = lax.scan(one_page, start, inputs)

    def unpage(array):
        moved = jnp.transpose(array, (1, 0, 2, 3))
        return moved.reshape(LAYERS, MICRO, N_DP * PAGE, array.shape[-1]).astype(jnp.bfloat16)
    text_g, layout_g = total
    return (unpage(stacked[0]), unpage(stacked[1]), unpage(stacked[2]), unpage(stacked[3]), text_g[0], text_g[1], text_g[2], text_g[3], text_g[4], text_g[5], text_g[6], text_g[7], layout_g[0], layout_g[1], layout_g[2], layout_g[3], layout_g[4], layout_g[5], layout_g[6], layout_g[7])
```

```python
import functools

import jax
import jax.numpy as jnp
from jax import lax
from jax.experimental import pallas as pl
from jax.experimental.pallas import tpu as pltpu
from jax.sharding import PartitionSpec as P

HEAD = 64
LHEAD = 16
TILE = 128

EPS = 1e-05
MASKED = -1000000000.0
BF = jnp.bfloat16
F32 = jnp.float32

NT = (((1,), (1,)), ((), ()))
TN = (((0,), (0,)), ((), ()))
NN = (((1,), (0,)), ((), ()))


def mm(a, b, dims=NN):
    return lax.dot_general(a, b, dims, preferred_element_type=F32)


def call(body, outs, name, n_scratch=()):
    return pl.pallas_call(
        body,
        out_shape=[jax.ShapeDtypeStruct(shape, dtype) for shape, dtype in outs],
        scratch_shapes=list(n_scratch),
        name=name,
        compiler_params=pltpu.CompilerParams(vmem_limit_bytes=56 * 1024 * 1024),
    )


def pack_body(layer, flag, qt0, qt1, ql0, ql1, ot0, ot1, ol0, ol1, prm, wc, woc, bc):
    heads = qt0.shape[2] // HEAD
    d = qt0.shape[1]
    dl = ql0.shape[1]
    wc[...] = jnp.zeros_like(wc)
    woc[...] = jnp.zeros_like(woc)
    bc[...] = jnp.zeros_like(bc)

    def fill(qt, ql, ot, ol):
        for c in range(3):
            for h in range(heads):
                col = (c * heads + h) * TILE
                wt = qt[c, :, h * HEAD : (h + 1) * HEAD]
                wl = ql[c, :, h * LHEAD : (h + 1) * LHEAD]
                if c == 0:
                    wt = (wt.astype(F32) * HEAD**-0.5).astype(BF)
                    wl = (wl.astype(F32) * LHEAD**-0.5).astype(BF)
                wc[0:d, col : col + HEAD] = wt
                wc[d : d + dl, col + HEAD : col + HEAD + LHEAD] = wl
        for h in range(heads):
            row = h * TILE
            woc[row : row + HEAD, 0:d] = ot[h * HEAD : (h + 1) * HEAD, :]
            woc[row + HEAD : row + HEAD + LHEAD, d : d + dl] = ol[h * LHEAD : (h + 1) * LHEAD, :]

    @pl.when(flag[0] == layer)
    def _():
        fill(qt0, ql0, ot0, ol0)

    @pl.when(flag[0] != layer)
    def _():
        fill(qt1, ql1, ot1, ol1)

    for row, c, st, sl in ((7, 0, HEAD**-0.5, LHEAD**-0.5), (8, 2, 1.0, 1.0)):
        for h in range(heads):
            col = (c * heads + h) * TILE
            bc[0:1, col : col + HEAD] = prm[row : row + 1, h * HEAD : (h + 1) * HEAD] * st
            bc[0:1, col + HEAD : col + HEAD + LHEAD] = (
                prm[row : row + 1, d + h * LHEAD : d + (h + 1) * LHEAD] * sl
            )


def attn_fwd_body(xo, xp, wc, bc, woc, segc, segr, keep, send, qkv, oc, lse):
    half = xo.shape[0]
    rows = 2 * half
    heads = wc.shape[1] // (3 * TILE)
    for ref, r0 in ((xo, 0), (xp, half)):
        qkv[r0 : r0 + half, :] = (mm(ref[...], wc[...]) + bc[0:1, :]).astype(BF)
    lse[...] = jnp.zeros_like(lse)
    for h in range(heads):
        key = qkv[:, (heads + h) * TILE : (heads + h + 1) * TILE]
        val_t = qkv[:, (2 * heads + h) * TILE : (2 * heads + h + 1) * TILE].T
        for q0 in range(0, rows, 256):
            query = qkv[q0 : q0 + 256, h * TILE : (h + 1) * TILE]
            s = mm(key, query, NT)
            s = jnp.where(segc[...] == segr[:, q0 : q0 + 256], s, MASKED)
            top = jnp.max(s, axis=0, keepdims=True)
            p = jnp.exp(s - top)
            total = jnp.sum(p, axis=0, keepdims=True)
            o = mm(val_t, p.astype(BF)) / total
            oc[q0 : q0 + 256, h * TILE : (h + 1) * TILE] = o.T.astype(BF)
            lse[h : h + 1, q0 : q0 + 256] = top + jnp.log(total)
    keep[...] = mm(oc[0:half, :], woc[...])
    send[...] = mm(oc[half:rows, :], woc[...]).astype(BF)


def gelu_pair(pre):
    phi = 0.5 * (1.0 + lax.erf(pre * (0.5**0.5)))
    slope = phi + pre * (jnp.exp(-0.5 * pre * pre) * 0.3989422804014327)
    return pre * phi, slope


def ffn_fwd_body(xo, xp, w1t, w1l, w2t, w2l, prm, keep, send, act, slope):
    d = w1t.shape[0]
    f = w1t.shape[1]
    half = xo.shape[0]
    for ref, r0 in ((xo, 0), (xp, half)):
        for w1, w2, a0, a1, f0, f1 in (
            (w1t, w2t, 0, d, 0, f),
            (w1l, w2l, d, xo.shape[1], f, act.shape[1]),
        ):
            pre = mm(ref[:, a0:a1], w1[...]) + prm[6:7, f0:f1]
            g, gp = gelu_pair(pre)
            g = g.astype(BF)
            act[r0 : r0 + half, f0:f1] = g
            slope[r0 : r0 + half, f0:f1] = gp.astype(BF)
            part = mm(g, w2[...])
            if r0 == 0:
                keep[:, a0:a1] = part
            else:
                send[:, a0:a1] = part.astype(BF)


def crossed(s, r):
    n = s.shape[0] // 2
    top = s[0:n, :].astype(F32) + r[n : 2 * n, :].astype(F32)
    low = s[n : 2 * n, :].astype(F32) + r[0:n, :].astype(F32)
    return jnp.concatenate([top, low], axis=0)


def norm_slices(h, prm, gain_row, shift_row, d, normed, inv, out):
    ivs = []
    for a0, a1 in ((0, d), (d, h.shape[1])):
        x = h[:, a0:a1]
        centred = x - jnp.mean(x, axis=-1, keepdims=True)
        iv = lax.rsqrt(jnp.mean(centred * centred, axis=-1, keepdims=True) + EPS)
        n = centred * iv
        normed[:, a0:a1] = n
        out[:, a0:a1] = (
            n * prm[gain_row : gain_row + 1, a0:a1] + prm[shift_row : shift_row + 1, a0:a1]
        ).astype(out.dtype)
        ivs.append(iv)
    lane = lax.broadcasted_iota(jnp.int32, inv.shape, 1)
    inv[...] = jnp.where(lane < HEAD, ivs[0], ivs[1])


def norm1_body(d, s, r, xo, prm, normed, inv, out):
    h = crossed(s, r) + xo[...].astype(F32) + prm[2:3, :]
    norm_slices(h, prm, 0, 3, d, normed, inv, out)


def norm2_body(d, s, r, n1, prm, normed, inv, out):
    first = n1[...] * prm[0:1, :] + prm[3:4, :]
    h = first + crossed(s, r) + prm[4:5, :]
    norm_slices(h, prm, 1, 5, d, normed, inv, out)


def norm_back_slices(dy, normed, inv, prm, gain_row, d, dh, dhb, small):
    small[...] = jnp.zeros_like(small)
    mine = dy.shape[0] // 2
    for a0, a1, lane in ((0, d, 0), (d, dy.shape[1], HEAD)):
        up = dy[:, a0:a1]
        n = normed[:, a0:a1]
        scaled = up * prm[gain_row : gain_row + 1, a0:a1]
        inner = (
            scaled
            - jnp.mean(scaled, axis=-1, keepdims=True)
            - n * jnp.mean(scaled * n, axis=-1, keepdims=True)
        )
        g = inner * inv[:, lane : lane + 1]
        dh[:, a0:a1] = g
        dhb[:, a0:a1] = g.astype(BF)
        small[0:1, a0:a1] = jnp.sum(up[0:mine] * n[0:mine], axis=0, keepdims=True)
        small[1:2, a0:a1] = jnp.sum(up[0:mine], axis=0, keepdims=True)
        small[2:3, a0:a1] = jnp.sum(g[0:mine], axis=0, keepdims=True)


def back_top_body(d, cot0, cot1, normed, inv, prm, dh, dhb, small):
    width = normed.shape[1]
    parts = []
    for cot in (cot0, cot1):
        c = cot[...].astype(F32)
        lane = lax.broadcasted_iota(jnp.int32, (c.shape[0], width), 1)
        w = jnp.where(lane < d, c[:, width : width + 1], c[:, width + 1 : width + 2])
        parts.append(c[:, 0:width] * w)
    dy = jnp.concatenate(parts, axis=0)
    norm_back_slices(dy, normed, inv, prm, 1, d, dh, dhb, small)


def back_next_body(d, dh_up, s, r, normed, inv, prm, dxin, dh, dhb, small):
    dx = (dh_up[...] + crossed(s, r)).astype(BF)
    dxin[...] = dx
    norm_back_slices(dx.astype(F32), normed, inv, prm, 1, d, dh, dhb, small)


def back_first_body(d, dh2, s, r, normed, inv, prm, dh, dhb, small):
    dx1 = dh2[...] + crossed(s, r)
    norm_back_slices(dx1, normed, inv, prm, 0, d, dh, dhb, small)


def ffn_back_body(go, gp, slope, w1t, w1l, w2t, w2l, dpre, keep, send):
    d = w1t.shape[0]
    f = w1t.shape[1]
    half = go.shape[0]
    for ref, r0 in ((go, 0), (gp, half)):
        for w1, w2, a0, a1, f0, f1 in (
            (w1t, w2t, 0, d, 0, f),
            (w1l, w2l, d, go.shape[1], f, slope.shape[1]),
        ):
            dact = mm(ref[:, a0:a1], w2[...], NT)
            dp = (dact * slope[r0 : r0 + half, f0:f1].astype(F32)).astype(BF)
            dpre[r0 : r0 + half, f0:f1] = dp
            part = mm(dp, w1[...], NT)
            if r0 == 0:
                keep[:, a0:a1] = part
            else:
                send[:, a0:a1] = part.astype(BF)


def ffn_grad_body(d, f, act, dpre, xo, xp, go, gp, g1, g2, lay, fb):
    half = xo.shape[0]
    width = xo.shape[1]
    fw = act.shape[1]
    dl = width - d
    g1[...] = (
        mm(xo[:, 0:d], dpre[0:half, 0:f], TN) + mm(xp[:, 0:d], dpre[half:, 0:f], TN)
    ).astype(BF)
    g2[...] = (
        mm(go[:, 0:d], act[0:half, 0:f], TN) + mm(gp[:, 0:d], act[half:, 0:f], TN)
    ).astype(BF)
    lay[:, 0 : fw - f] = (
        mm(xo[:, d:], dpre[0:half, f:], TN) + mm(xp[:, d:], dpre[half:, f:], TN)
    ).astype(BF)
    lay[:, fw - f : 2 * (fw - f)] = (
        mm(go[:, d:], act[0:half, f:], TN) + mm(gp[:, d:], act[half:, f:], TN)
    ).astype(BF)
    fb[...] = jnp.broadcast_to(
        jnp.sum(dpre[...].astype(F32), axis=0, keepdims=True), fb.shape
    )


def attn_back_body(go, gp, qkv, lse, segc, segr, wc, woc, keep, send, dqkv, doc):
    half = go.shape[0]
    rows = 2 * half
    heads = wc.shape[1] // (3 * TILE)
    for ref, r0 in ((go, 0), (gp, half)):
        doc[r0 : r0 + half, :] = mm(ref[...], woc[...], NT).astype(BF)
    lane = lax.broadcasted_iota(jnp.int32, (rows, TILE), 1)
    is_text = lane < HEAD
    for h in range(heads):
        key = qkv[:, (heads + h) * TILE : (heads + h + 1) * TILE]
        val = qkv[:, (2 * heads + h) * TILE : (2 * heads + h + 1) * TILE]
        query = qkv[:, h * TILE : (h + 1) * TILE]
        up = doc[:, h * TILE : (h + 1) * TILE]
        zero = jnp.zeros_like(key)
        key_text = jnp.where(is_text, key, zero)
        key_lay = jnp.where(is_text, zero, key)
        query_text = jnp.where(is_text, query, zero)
        query_lay = jnp.where(is_text, zero, query)
        up_text = jnp.where(is_text, up, zero)
        key_text_t = key_text.T
        key_lay_t = key_lay.T
        dkey = jnp.zeros((rows, TILE), F32)
        dval = jnp.zeros((rows, TILE), F32)
        for q0 in range(0, rows, 256):
            q1 = q0 + 256
            s = mm(key, query[q0:q1], NT)
            p = jnp.where(
                segc[...] == segr[:, q0:q1], jnp.exp(s - lse[h : h + 1, q0:q1]), 0.0
            )
            dp_all = mm(val, up[q0:q1], NT)
            dp_text = mm(val, up_text[q0:q1], NT)
            ds_all = p * (dp_all - jnp.sum(dp_all * p, axis=0, keepdims=True))
            ds_text = p * (dp_text - jnp.sum(dp_text * p, axis=0, keepdims=True))
            ds_all = ds_all.astype(BF)
            ds_text = ds_text.astype(BF)
            dval = dval + mm(p.astype(BF), up[q0:q1])
            dkey = dkey + mm(ds_text, query_text[q0:q1]) + mm(ds_all, query_lay[q0:q1])
            dquery_t = mm(key_text_t, ds_text) + mm(key_lay_t, ds_all)
            dqkv[q0:q1, h * TILE : (h + 1) * TILE] = dquery_t.T.astype(BF)
        dqkv[:, (heads + h) * TILE : (heads + h + 1) * TILE] = dkey.astype(BF)
        dqkv[:, (2 * heads + h) * TILE : (2 * heads + h + 1) * TILE] = dval.astype(BF)
    keep[...] = mm(dqkv[0:half, :], wc[...], NT)
    send[...] = mm(dqkv[half:rows, :], wc[...], NT).astype(BF)


def attn_grad_body(d, xo, xp, dqkv, oc, go, gp, ga, lay, qb, dt, dlay, ot, ol):
    half = xo.shape[0]
    heads = oc.shape[1] // TILE
    for c in range(3):
        for h in range(heads):
            col = (c * heads + h) * TILE
            gt = dqkv[:, col : col + HEAD]
            gl = dqkv[:, col + HEAD : col + HEAD + LHEAD]
            if c == 0:
                gt = (gt.astype(F32) * HEAD**-0.5).astype(BF)
                gl = (gl.astype(F32) * LHEAD**-0.5).astype(BF)
            dt[:, (c * heads + h) * HEAD : (c * heads + h + 1) * HEAD] = gt
            dlay[:, (c * heads + h) * LHEAD : (c * heads + h + 1) * LHEAD] = gl
    for h in range(heads):
        ot[:, h * HEAD : (h + 1) * HEAD] = oc[:, h * TILE : h * TILE + HEAD]
        ol[:, h * LHEAD : (h + 1) * LHEAD] = oc[:, h * TILE + HEAD : h * TILE + HEAD + LHEAD]
    wt = 3 * heads * HEAD
    wl = 3 * heads * LHEAD
    ga[:, 0:wt] = (
        mm(xo[:, 0:d], dt[0:half, :], TN) + mm(xp[:, 0:d], dt[half:, :], TN)
    ).astype(BF)
    ga[:, wt:] = (
        mm(go[:, 0:d], ot[0:half, :], TN) + mm(gp[:, 0:d], ot[half:, :], TN)
    ).astype(BF)
    lay[:, 0:wl] = (
        mm(xo[:, d:], dlay[0:half, :], TN) + mm(xp[:, d:], dlay[half:, :], TN)
    ).astype(BF)
    lay[:, wl:] = (
        mm(go[:, d:], ol[0:half, :], TN) + mm(gp[:, d:], ol[half:, :], TN)
    ).astype(BF)
    qb[...] = jnp.zeros_like(qb)
    qb[0:1, 0:wt] = jnp.sum(dt[...].astype(F32), axis=0, keepdims=True)
    qb[0:1, d : d + wl] = jnp.sum(dlay[...].astype(F32), axis=0, keepdims=True)


def swap(value, axis, bit):
    size = lax.axis_size(axis)
    return lax.ppermute(value, axis, [(i, i ^ bit) for i in range(size)])


def core_swap(value):
    return swap(value, "tensor", 1)


def chip_swap(value):
    return swap(value, "tensor", 2)


def pair_sum(keep, send):
    s = (keep + core_swap(send).astype(F32)).astype(BF)
    return s, chip_swap(s)


def scatter_pages(value):
    size = lax.axis_size("dp")
    me = lax.axis_index("dp")
    cur = value.reshape((size, value.shape[0] // size) + value.shape[1:])
    bit = 1
    while bit < size:
        pair = cur.reshape((cur.shape[0] // 2, 2) + cur.shape[1:])
        mine = (me // bit) % 2
        out = lax.dynamic_index_in_dim(pair, 1 - mine, 1, keepdims=False)
        held = lax.dynamic_index_in_dim(pair, mine, 1, keepdims=False)
        got = swap(out, "dp", bit)
        cur = held.astype(F32) + got.astype(F32)
        bit *= 2
        if bit < size:
            cur = cur.astype(BF)
    return cur[0].astype(F32)


def per_device(
    text_in,
    layout_in,
    text_cot,
    layout_cot,
    token_mask,
    box_mask,
    segments,
    text_qkv,
    text_qv_bias,
    text_out_w,
    text_ffn_in,
    text_ffn_bias,
    text_ffn_out,
    text_gains,
    text_biases,
    layout_qkv,
    layout_qv_bias,
    layout_out_w,
    layout_ffn_in,
    layout_ffn_bias,
    layout_ffn_out,
    layout_gains,
    layout_biases,
):
    sections = lax.axis_size("section")
    section = lax.axis_index("section")
    tensor = lax.axis_index("tensor")
    micro = text_in.shape[0]
    assert micro == sections == 2 and lax.axis_size("tensor") == 4 and segments.shape[1] == 1
    mine, d = text_in.shape[1:]
    dl = layout_in.shape[2]
    width = d + dl
    half = 2 * mine
    rows = 4 * mine
    heads = text_qkv.shape[-1] // HEAD
    f = text_ffn_in.shape[-1]
    fl = layout_ffn_in.shape[-1]
    fw = f + fl
    flag = section.astype(jnp.int32).reshape(1)

    def other_section(value):
        return lax.ppermute(value, "section", [(0, 1), (1, 0)])

    def pick(array):
        return lax.dynamic_index_in_dim(array, section, 0, keepdims=False)

    x_mine = jnp.concatenate([pick(text_in), pick(layout_in)], axis=1)
    x_own = jnp.concatenate([x_mine, chip_swap(x_mine)], axis=0)
    x_peer = core_swap(x_own)
    cot_mine = jnp.concatenate(
        [
            pick(text_cot),
            pick(layout_cot),
            (0.25 + pick(token_mask).astype(F32)).astype(BF)[:, None],
            (0.25 + pick(box_mask).astype(F32)).astype(BF)[:, None],
            jnp.zeros((mine, TILE - (width + 2) % TILE), BF),
        ],
        axis=1,
    )
    cot_mate = chip_swap(cot_mine)
    seg = pick(segments)[0].reshape(4, mine)
    seg = jnp.concatenate(
        [lax.dynamic_index_in_dim(seg, tensor ^ k, 0, keepdims=True) for k in (0, 2, 1, 3)], axis=0
    )
    segr = seg.reshape(1, rows)
    segc = seg.reshape(rows, 1)

    def wide(text, layout):
        return jnp.concatenate(
            [
                jnp.pad(text, ((0, 0), (0, d - text.shape[1]))),
                jnp.pad(layout, ((0, 0), (0, dl - layout.shape[1]))),
            ],
            axis=1,
        )

    prm_own = jnp.concatenate(
        [
            wide(text_gains[0], layout_gains[0]),
            wide(text_biases[0], layout_biases[0]),
            wide(text_ffn_bias, layout_ffn_bias),
            wide(text_qv_bias[0], layout_qv_bias[0]),
            jnp.zeros((7, width), F32),
        ],
        axis=0,
    )
    own = (
        text_qkv[0],
        layout_qkv[0],
        text_out_w[0],
        layout_out_w[0],
        text_ffn_in[0],
        layout_ffn_in[0],
        text_ffn_out[0],
        layout_ffn_out[0],
    )
    prm_oth = other_section(prm_own)
    oth = tuple(other_section(w) for w in own)

    def layer_weights(j):
        is_own = section == j
        prm = jnp.where(is_own, prm_own, prm_oth)
        wc, woc, bc = call(
            functools.partial(pack_body, j),
            [((width, 3 * heads * TILE), BF), ((heads * TILE, width), BF), ((8, 3 * heads * TILE), F32)],
            "pack",
        )(flag, own[0], oth[0], own[1], oth[1], own[2], oth[2], own[3], oth[3], prm)
        ffn = tuple(jnp.where(is_own, own[k], oth[k]) for k in range(4, 8))
        return prm, wc, woc, bc, ffn

    acts = [((half, width), F32), ((half, width), BF)]
    norm_outs = [((half, width), F32), ((half, TILE), F32), ((half, width), BF)]
    kept = []
    hidden = []
    for j in range(sections):
        prm, wc, woc, bc, ffn = layer_weights(j)
        keep, send, qkv, oc, lse = call(
            attn_fwd_body,
            acts + [((rows, 3 * heads * TILE), BF), ((rows, heads * TILE), BF), ((8, rows), F32)],
            "attn_fwd",
        )(x_own, x_peer, wc, bc, woc, segc, segr)
        s, r = pair_sum(keep, send)
        n1, inv1, x1_own = call(functools.partial(norm1_body, d), norm_outs, "norm1")(s, r, x_own, prm)
        x1_peer = core_swap(x1_own)
        keep, send, act, slope = call(
            ffn_fwd_body, acts + [((rows, fw), BF), ((rows, fw), BF)], "ffn_fwd"
        )(x1_own, x1_peer, *ffn, prm)
        s, r = pair_sum(keep, send)
        n2, inv2, y_own = call(functools.partial(norm2_body, d), norm_outs, "norm2")(s, r, n1, prm)
        hidden.append(y_own[0:mine])
        kept.append(
            (prm, wc, woc, ffn, x_own, x_peer, qkv, oc, lse, n1, inv1, x1_own, x1_peer, act, slope, n2, inv2)
        )
        if j + 1 < sections:
            x_own = y_own
            x_peer = core_swap(y_own)

    back_outs = [((half, width), F32), ((half, width), BF), ((8, width), F32)]
    grads = [None] * sections
    input_grads = [None] * sections
    for j in reversed(range(sections)):
        (prm, wc, woc, ffn, x_own, x_peer, qkv, oc, lse, n1, inv1, x1_own, x1_peer, act, slope, n2, inv2) = kept[j]
        if j == sections - 1:
            dh2, dh2b, small2 = call(functools.partial(back_top_body, d), back_outs, "back_top")(
                cot_mine, cot_mate, n2, inv2, prm
            )
        else:
            dxin, dh2, dh2b, small2 = call(
                functools.partial(back_next_body, d), [((half, width), BF)] + back_outs, "back_next"
            )(dh, s, r, n2, inv2, prm)
            input_grads[j + 1] = dxin[0:mine]
        dh2_peer = core_swap(dh2b)
        dpre, keep, send = call(ffn_back_body, [((rows, fw), BF)] + acts, "ffn_back")(
            dh2b, dh2_peer, slope, *ffn
        )
        s, r = pair_sum(keep, send)
        g1, g2, lay_f, fb = call(
            functools.partial(ffn_grad_body, d, f),
            [((d, f), BF), ((d, f), BF), ((dl, 2 * fl), BF), ((8, fw), F32)],
            "ffn_grad",
        )(act, dpre, x1_own, x1_peer, dh2b, dh2_peer)
        dh, dhb, small1 = call(functools.partial(back_first_body, d), back_outs, "back_first")(
            dh2, s, r, n1, inv1, prm
        )
        dh_peer = core_swap(dhb)
        keep, send, dqkv = call(
            attn_back_body,
            acts + [((rows, 3 * heads * TILE), BF)],
            "attn_back",
            (pltpu.VMEM((rows, heads * TILE), BF),),
        )(dhb, dh_peer, qkv, lse, segc, segr, wc, woc)
        s, r = pair_sum(keep, send)
        wt = 3 * heads * HEAD
        wl = 3 * heads * LHEAD
        ga, lay_a, qb = call(
            functools.partial(attn_grad_body, d),
            [((d, wt + heads * HEAD), BF), ((dl, wl + heads * LHEAD), BF), ((8, width), F32)],
            "attn_grad",
            (
                pltpu.VMEM((rows, wt), BF),
                pltpu.VMEM((rows, wl), BF),
                pltpu.VMEM((rows, heads * HEAD), BF),
                pltpu.VMEM((rows, heads * LHEAD), BF),
            ),
        )(x_own, x_peer, dqkv, oc, dhb, dh_peer)
        shared = jnp.concatenate(
            [small1[0:1], small2[0:1], small1[2:3], small1[1:2], small2[2:3], small2[1:2]], axis=0
        )
        local = jnp.concatenate([fb[0:1], qb[0:1]], axis=0)
        grads[j] = (ga, g1, g2, lay_a, lay_f, shared, local)
    n = mine
    final = dh + jnp.concatenate(
        [s[0:n].astype(F32) + r[n:].astype(F32), s[n:].astype(F32) + r[0:n].astype(F32)], axis=0
    )
    input_grads[0] = final[0:n].astype(BF)

    def to_owner(j):
        pairs = [(i, j) for i in range(sections) if i != j]
        return tuple(lax.ppermute(g, "section", pairs) for g in grads[j])

    got1 = to_owner(1)
    got0 = to_owner(0)
    last = section == 1
    total = []
    for a0, a1, b0, b1 in zip(grads[0], grads[1], got0, got1):
        value = jnp.where(
            last, a1.astype(F32) + b1.astype(F32), a0.astype(F32) + b0.astype(F32)
        )
        total.append(value)
    ga, g1, g2, lay_a, lay_f = (scatter_pages(v.astype(BF)) for v in total[0:5])
    shared = lax.psum(total[5], ("dp", "tensor"))
    local = lax.psum(total[6], "dp")

    def collect(parts):
        mine_now = jnp.where(last, parts[1], parts[0])
        away = jnp.where(last, parts[0], parts[1])
        got = other_section(away)
        return jnp.stack([jnp.where(last, got, mine_now), jnp.where(last, mine_now, got)])

    hid = collect(hidden)
    ing = collect(input_grads)
    chunk = ga.shape[0]
    chunk_l = lay_a.shape[0]
    g_qkv = jnp.swapaxes(ga[:, 0:wt].reshape(chunk, 3, heads * HEAD), 0, 1)
    g_lqkv = jnp.swapaxes(lay_a[:, 0:wl].reshape(chunk_l, 3, heads * LHEAD), 0, 1)
    qv = local[1, 0:wt].reshape(3, heads * HEAD)
    lqv = local[1, d : d + wl].reshape(3, heads * LHEAD)
    return (
        hid[None, :, :, 0:d],
        hid[None, :, :, d:],
        ing[None, :, :, 0:d],
        ing[None, :, :, d:],
        g_qkv[None],
        jnp.stack([qv[0], qv[2]])[None],
        ga[:, wt:].T[None],
        g1[None],
        local[0:1, 0:f],
        g2.T[None],
        shared[None, 0:2, 0:d],
        shared[None, 2:6, 0:d],
        g_lqkv[None],
        jnp.stack([lqv[0], lqv[2]])[None],
        lay_a[:, wl:].T[None],
        lay_f[:, 0:fl][None],
        local[0:1, f:fw],
        lay_f[:, fl:].T[None],
        shared[None, 0:2, d:],
        shared[None, 2:6, d:],
    )


def solution(mesh):
    in_specs = (
        P(None, ("dp", "tensor"), None),
        P(None, ("dp", "tensor"), None),
        P(None, ("dp", "tensor"), None),
        P(None, ("dp", "tensor"), None),
        P(None, ("dp", "tensor")),
        P(None, ("dp", "tensor")),
        P(None, "dp", None),
        P("section", None, None, "tensor"),
        P("section", None, "tensor"),
        P("section", "tensor", None),
        P("section", None, "tensor"),
        P("section", "tensor"),
        P("section", "tensor", None),
        P("section", None, None),
        P("section", None, None),
        P("section", None, None, "tensor"),
        P("section", None, "tensor"),
        P("section", "tensor", None),
        P("section", None, "tensor"),
        P("section", "tensor"),
        P("section", "tensor", None),
        P("section", None, None),
        P("section", None, None),
    )
    out_specs = (
        P("section", None, ("dp", "tensor"), None),
        P("section", None, ("dp", "tensor"), None),
        P("section", None, ("dp", "tensor"), None),
        P("section", None, ("dp", "tensor"), None),
        P("section", None, "dp", "tensor"),
        P("section", None, "tensor"),
        P("section", "tensor", "dp"),
        P("section", "dp", "tensor"),
        P("section", "tensor"),
        P("section", "tensor", "dp"),
        P("section", None, None),
        P("section", None, None),
        P("section", None, "dp", "tensor"),
        P("section", None, "tensor"),
        P("section", "tensor", "dp"),
        P("section", "dp", "tensor"),
        P("section", "tensor"),
        P("section", "tensor", "dp"),
        P("section", None, None),
        P("section", None, None),
    )
    return jax.shard_map(
        per_device, mesh=mesh, in_specs=in_specs, out_specs=out_specs, check_vma=False
    )
```

```python
import functools

import jax
import jax.numpy as jnp
from jax import lax
from jax.experimental import pallas as pl
from jax.experimental.pallas import tpu as pltpu
from jax.sharding import PartitionSpec as P

HEAD = 64
LHEAD = 16
TILE = 128
CHUNKS = 2

EPS = 1e-05
MASKED = -1000000000.0
BF = jnp.bfloat16
F32 = jnp.float32

NT = (((1,), (1,)), ((), ()))
TN = (((0,), (0,)), ((), ()))
NN = (((1,), (0,)), ((), ()))


def mm(a, b, dims=NN):
    return lax.dot_general(a, b, dims, preferred_element_type=F32)


def call(body, outs, name, scratch=(), us=2, hbm=False):
    def run(ids, *args):
        place = jax.ShapeDtypeStruct if hbm else pltpu.VMEM
        return pl.pallas_call(
            body,
            out_shape=[place(shape, dtype) for shape, dtype in outs],
            in_specs=[pl.BlockSpec(memory_space=pltpu.SMEM)]
            + [pl.BlockSpec(memory_space=pltpu.VMEM)] * len(args),
            scratch_shapes=list(scratch),
            name=name,
            cost_estimate=pl.CostEstimate(flops=int(us * 10**9), transcendentals=0, bytes_accessed=0),
            compiler_params=pltpu.CompilerParams(vmem_limit_bytes=24 * 1024 * 1024),
        )(ids, *[pltpu.with_memory_space_constraint(a, pltpu.VMEM) for a in args])

    return run


def cat(refs, a0=None, a1=None):
    return jnp.concatenate([ref[:, a0:a1] for ref in refs], axis=0)


def weights_body(pieces, ids, qt, ql, ot, ol, w1l, w2l, quarter, rest, qp):
    et, d = qt.shape[1:]
    el, dl = ql.shape[1:]
    qp[3 * et :, :] = jnp.zeros_like(qp[3 * et :, :])
    for c in range(3):
        qp[c * et : (c + 1) * et, :] = qt[c]
        qp[3 * et : 3 * et + el, c * dl : (c + 1) * dl] = ql[c]
    if pieces == 1:
        quarter[...] = qp[...]
    else:
        rows = quarter.shape[0]
        quarter[...] = qp[pl.ds(pl.multiple_of(ids[2] * rows, 16), rows), :]
    rest[...] = jnp.zeros_like(rest)
    rest[0:et, :] = ot[...]
    heads = el // LHEAD
    for h in range(heads):
        rest[et : et + LHEAD, h * dl : (h + 1) * dl] = ol[h * LHEAD : (h + 1) * LHEAD, :]
    deep = dl * dl // d
    for g in range(d // dl):
        rest[et + LHEAD : et + LHEAD + deep, g * dl : (g + 1) * dl] = w1l[g * deep : (g + 1) * deep, :]
        rest[et + LHEAD + deep :, g * dl : (g + 1) * dl] = w2l[g * deep : (g + 1) * deep, :]


def inputs_body(chunks, ids, tin, lin, *outs):
    s = ids[0]
    rows = tin.shape[1] // chunks
    d = tin.shape[2]
    lay = lin[s].T
    for k in range(chunks):
        outs[k][:, 0:d] = tin[s, k * rows : (k + 1) * rows, :]
        outs[k][:, d:] = lay[k * rows : (k + 1) * rows, :]


def side_body(chunks, ids, tcot, lcot, tmask, bmask, seg, *refs):
    s = ids[0]
    cots = refs[0:chunks]
    segr, segc = refs[chunks:]
    mine, d = tcot.shape[1:]
    width = d + lcot.shape[1]
    rows = mine // chunks
    lay = lcot[s].T
    wt = (0.25 + tmask[pl.ds(s, 1), :].astype(F32)).astype(BF).astype(F32)
    wb = (0.25 + bmask[pl.ds(s, 1), :].astype(F32)).astype(BF).astype(F32)
    wt = jnp.broadcast_to(wt, (TILE, mine)).T
    wb = jnp.broadcast_to(wb, (TILE, mine)).T
    for k in range(chunks):
        a, b = k * rows, (k + 1) * rows
        cots[k][:, 0:d] = tcot[s, a:b, :]
        cots[k][:, d:width] = lay[a:b, :]
        cots[k][:, width : width + 32] = wt[a:b, 0:32].astype(BF)
        cots[k][:, width + 32 : width + 64] = wb[a:b, 0:32].astype(BF)
    at = 0
    for k in range(chunks):
        for step in (0, 2, 1, 3):
            block = seg[s, pl.ds(ids[1] ^ step, 1), k * rows : (k + 1) * rows]
            segr[0:1, at : at + rows] = block
            at += rows
    segc[...] = jnp.broadcast_to(segr[...].astype(F32), (TILE, at)).T


def params_body(ids, tg, tb, tf, tq, lg, lb, lf, lq, prm):
    d = tg.shape[1]
    prm[...] = jnp.zeros_like(prm)
    for a, gains, biases, hidden, qv in ((0, tg, tb, tf, tq), (d, lg, lb, lf, lq)):
        prm[0:2, a : a + gains.shape[1]] = gains[...]
        prm[2:6, a : a + gains.shape[1]] = biases[...]
        prm[6:7, a : a + hidden.shape[1]] = hidden[...]
        prm[7:9, a : a + qv.shape[1]] = qv[...]


def pack_body(layer, pieces, heads, ids, qt, ql, ot, ol, w1l, w2l, *refs):
    got = refs[0:pieces]
    rest, prm_own, prm_oth, wct, woc, bc, o1l, o2l, prm, qp = refs[pieces:]
    et, d = qt.shape[1:]
    el, dl = ql.shape[1:]
    deep = dl * dl // d
    wct[...] = jnp.zeros_like(wct)
    woc[...] = jnp.zeros_like(woc)
    bc[...] = jnp.zeros_like(bc)

    def put(c, h, wt, wl):
        row = (c * heads + h) * TILE
        if c == 0:
            wt = (wt.astype(F32) * HEAD**-0.5).astype(BF)
            wl = (wl.astype(F32) * LHEAD**-0.5).astype(BF)
        wct[row : row + HEAD, 0:d] = wt
        wct[row + HEAD : row + HEAD + LHEAD, d:] = wl

    @pl.when(ids[0] == layer)
    def _():
        for c in range(3):
            for h in range(heads):
                put(c, h, qt[c, h * HEAD : (h + 1) * HEAD, :], ql[c, h * LHEAD : (h + 1) * LHEAD, :])
        for h in range(heads):
            woc[h * TILE : h * TILE + HEAD, 0:d] = ot[h * HEAD : (h + 1) * HEAD, :]
            woc[h * TILE + HEAD : h * TILE + HEAD + LHEAD, d:] = ol[h * LHEAD : (h + 1) * LHEAD, :]
        o1l[...] = w1l[...]
        o2l[...] = w2l[...]
        prm[...] = prm_own[...]

    @pl.when(ids[0] != layer)
    def _():
        if pieces == 1:
            qp[...] = got[0][...]
        else:
            rows = got[0].shape[0]
            for k in range(pieces):
                at = lax.rem(ids[2] + (pieces - k), pieces) * rows
                qp[pl.ds(pl.multiple_of(at, 16), rows), :] = got[k][...]
        for c in range(3):
            for h in range(heads):
                put(
                    c,
                    h,
                    qp[c * et + h * HEAD : c * et + (h + 1) * HEAD, :],
                    qp[3 * et + h * LHEAD : 3 * et + (h + 1) * LHEAD, c * dl : (c + 1) * dl],
                )
        for h in range(heads):
            woc[h * TILE : h * TILE + HEAD, 0:d] = rest[h * HEAD : (h + 1) * HEAD, :]
            woc[h * TILE + HEAD : h * TILE + HEAD + LHEAD, d:] = rest[
                et : et + LHEAD, h * dl : (h + 1) * dl
            ]
        for g in range(d // dl):
            o1l[g * deep : (g + 1) * deep, :] = rest[
                et + LHEAD : et + LHEAD + deep, g * dl : (g + 1) * dl
            ]
            o2l[g * deep : (g + 1) * deep, :] = rest[et + LHEAD + deep :, g * dl : (g + 1) * dl]
        prm[...] = prm_oth[...]

    for row, c, st, sl in ((7, 0, HEAD**-0.5, LHEAD**-0.5), (8, 2, 1.0, 1.0)):
        for h in range(heads):
            col = (c * heads + h) * TILE
            bc[0:1, col : col + HEAD] = prm[row : row + 1, h * HEAD : (h + 1) * HEAD] * st
            bc[0:1, col + HEAD : col + HEAD + LHEAD] = (
                prm[row : row + 1, d + h * LHEAD : d + (h + 1) * LHEAD] * sl
            )


def choose_body(layer, ids, a0, a1, b0, b1, a, b):
    @pl.when(ids[0] == layer)
    def _():
        a[...] = a0[...]
        b[...] = b0[...]

    @pl.when(ids[0] != layer)
    def _():
        a[...] = a1[...]
        b[...] = b1[...]


def attend(query, qkv, heads, h, segc, segr, q0, oc, lse):
    key = qkv[:, (heads + h) * TILE : (heads + h + 1) * TILE]
    val_t = qkv[:, (2 * heads + h) * TILE : (2 * heads + h + 1) * TILE].T
    for a in range(0, query.shape[0], 256):
        s = mm(key, query[a : a + 256], NT)
        same = jnp.concatenate([segc[...]] * 2, axis=1) == segr[:, q0 + a : q0 + a + 256].astype(F32)
        s = jnp.where(same, s, MASKED)
        top = jnp.max(s, axis=0, keepdims=True)
        p = jnp.exp(s - top)
        total = jnp.sum(p, axis=0, keepdims=True)
        o = mm(val_t, p.astype(BF)) / total
        oc[a : a + 256, h * TILE : (h + 1) * TILE] = o.T.astype(BF)
        lse[h : h + 1, a : a + 256] = top + jnp.log(total)


def attn_part(k, qkv, woc, segc, segr, keep, send, oc, lse):
    rows = oc.shape[0]
    heads = oc.shape[1] // TILE
    lse[...] = jnp.zeros_like(lse)
    for h in range(heads):
        query = qkv[k * rows : (k + 1) * rows, h * TILE : (h + 1) * TILE]
        attend(query, qkv, heads, h, segc, segr, k * rows, oc, lse)
    keep[...] = mm(oc[0 : rows // 2, :], woc[...])
    send[...] = mm(oc[rows // 2 :, :], woc[...]).astype(BF)


def attn_first_body(chunks, ids, *refs):
    xs = refs[0 : 2 * chunks]
    wct, bc, woc, segc, segr, keep, send, oc, lse, qkv = refs[2 * chunks :]
    at = 0
    for ref in xs:
        qkv[at : at + ref.shape[0], :] = (mm(ref[...], wct[...], NT) + bc[0:1, :]).astype(BF)
        at += ref.shape[0]
    attn_part(0, qkv, woc, segc, segr, keep, send, oc, lse)


def attn_next_body(k, ids, qkv, woc, segc, segr, keep, send, oc, lse):
    attn_part(k, qkv, woc, segc, segr, keep, send, oc, lse)


def gelu_pair(pre):
    phi = 0.5 * (1.0 + lax.erf(pre * (0.5**0.5)))
    slope = phi + pre * (jnp.exp(-0.5 * pre * pre) * 0.3989422804014327)
    return pre * phi, slope


def ffn_fwd_body(ids, xo, xp, w1t, w1l, w2t, w2l, prm, keep, send, act, slope):
    d, f = w1t.shape
    half = xo.shape[0]
    for w1, w2, a0, a1, f0, f1 in (
        (w1t, w2t, 0, d, 0, f),
        (w1l, w2l, d, xo.shape[1], f, act.shape[1]),
    ):
        pre = mm(cat((xo, xp), a0, a1), w1[...]) + prm[6:7, f0:f1]
        g, gp = gelu_pair(pre)
        g = g.astype(BF)
        act[:, f0:f1] = g
        slope[:, f0:f1] = gp.astype(BF)
        part = mm(g, w2[...])
        keep[:, a0:a1] = part[0:half]
        send[:, a0:a1] = part[half:].astype(BF)


def crossed(s, r):
    n = s.shape[0] // 2
    top = s[0:n, :].astype(F32) + r[n : 2 * n, :].astype(F32)
    low = s[n : 2 * n, :].astype(F32) + r[0:n, :].astype(F32)
    return jnp.concatenate([top, low], axis=0)


def norm_slices(h, prm, gain_row, shift_row, d, normed, inv, out):
    ivs = []
    for a0, a1 in ((0, d), (d, h.shape[1])):
        x = h[:, a0:a1]
        centred = x - jnp.mean(x, axis=-1, keepdims=True)
        iv = lax.rsqrt(jnp.mean(centred * centred, axis=-1, keepdims=True) + EPS)
        n = centred * iv
        normed[:, a0:a1] = n
        out[:, a0:a1] = (
            n * prm[gain_row : gain_row + 1, a0:a1] + prm[shift_row : shift_row + 1, a0:a1]
        ).astype(out.dtype)
        ivs.append(iv)
    lane = lax.broadcasted_iota(jnp.int32, inv.shape, 1)
    inv[...] = jnp.where(lane < HEAD, ivs[0], ivs[1])


def norm1_body(d, ids, s, r, xo, prm, normed, inv, out):
    h = crossed(s, r) + xo[...].astype(F32) + prm[2:3, :]
    norm_slices(h, prm, 0, 3, d, normed, inv, out)


def norm2_body(d, ids, s, r, n1, prm, normed, inv, out):
    first = n1[...] * prm[0:1, :] + prm[3:4, :]
    h = first + crossed(s, r) + prm[4:5, :]
    norm_slices(h, prm, 1, 5, d, normed, inv, out)


def pair_body(ids, keep, got, s):
    s[...] = (keep[...] + got[...].astype(F32)).astype(BF)


def norm_back_slices(dy, normed, inv, prm, gain_row, d, dh, dhb, small):
    small[...] = jnp.zeros_like(small)
    mine = dy.shape[0] // 2
    for a0, a1, lane in ((0, d, 0), (d, dy.shape[1], HEAD)):
        up = dy[:, a0:a1]
        n = normed[:, a0:a1]
        scaled = up * prm[gain_row : gain_row + 1, a0:a1]
        inner = (
            scaled
            - jnp.mean(scaled, axis=-1, keepdims=True)
            - n * jnp.mean(scaled * n, axis=-1, keepdims=True)
        )
        g = inner * inv[:, lane : lane + 1]
        dh[:, a0:a1] = g
        dhb[:, a0:a1] = g.astype(BF)
        small[0:1, a0:a1] = jnp.sum(up[0:mine] * n[0:mine], axis=0, keepdims=True)
        small[1:2, a0:a1] = jnp.sum(up[0:mine], axis=0, keepdims=True)
        small[2:3, a0:a1] = jnp.sum(g[0:mine], axis=0, keepdims=True)


def back_top_body(d, ids, cot0, cot1, normed, inv, prm, dh, dhb, small):
    width = normed.shape[1]
    parts = []
    for cot in (cot0, cot1):
        c = cot[...].astype(F32)
        lane = lax.broadcasted_iota(jnp.int32, (c.shape[0], width), 1)
        w = jnp.where(lane < d, c[:, width : width + 1], c[:, width + 32 : width + 33])
        parts.append(c[:, 0:width] * w)
    dy = jnp.concatenate(parts, axis=0)
    norm_back_slices(dy, normed, inv, prm, 1, d, dh, dhb, small)


def back_next_body(d, ids, dh_up, s, r, normed, inv, prm, dxin, dh, dhb, small):
    dx = (dh_up[...] + crossed(s, r)).astype(BF)
    dxin[...] = dx
    norm_back_slices(dx.astype(F32), normed, inv, prm, 1, d, dh, dhb, small)


def back_first_body(d, ids, dh2, s, r, normed, inv, prm, dh, dhb, small):
    norm_back_slices(dh2[...] + crossed(s, r), normed, inv, prm, 0, d, dh, dhb, small)


def back_last_body(ids, dh, s, r, dxin):
    dxin[...] = (dh[...] + crossed(s, r)).astype(BF)


def ffn_back_body(ids, go, gp, slope, w1t, w1l, w2t, w2l, keep, send, dpre):
    d, f = w1t.shape
    half = go.shape[0]
    for w1, w2, a0, a1, f0, f1 in (
        (w1t, w2t, 0, d, 0, f),
        (w1l, w2l, d, go.shape[1], f, slope.shape[1]),
    ):
        dact = mm(cat((go, gp), a0, a1), w2[...], NT)
        dp = (dact * slope[:, f0:f1].astype(F32)).astype(BF)
        dpre[:, f0:f1] = dp
        part = mm(dp, w1[...], NT)
        keep[:, a0:a1] = part[0:half]
        send[:, a0:a1] = part[half:].astype(BF)


def split_halves(text, lay, pages, ids, keep, send):
    tr = text.shape[0] // (2 * pages)
    ll = lay.shape[0] // (2 * pages)
    lanes = lay.shape[1]
    lr = 8 if ll % 8 == 0 else ll
    rows = tr + lr

    def put(half, ref):
        if ll // lr * lanes < ref.shape[1]:
            ref[...] = jnp.zeros_like(ref)
        for z in range(pages):
            a = (2 * z + half) * tr
            ref[z * rows : z * rows + tr, :] = text[a : a + tr]
            for g in range(ll // lr):
                b = (2 * z + half) * ll + g * lr
                ref[z * rows + tr : (z + 1) * rows, g * lanes : (g + 1) * lanes] = lay[b : b + lr]

    @pl.when(ids[0] == 0)
    def _():
        put(0, keep)
        put(1, send)

    @pl.when(ids[0] != 0)
    def _():
        put(1, keep)
        put(0, send)


def outer_body(d, f, n, pages, ids, *refs):
    left, right = refs[0 : 2 * n], refs[2 * n : 3 * n]
    keep, send, total = refs[3 * n :]
    a = cat(left)
    b = cat(right)
    text = mm(a[:, 0:d], b[:, 0:f], TN).astype(BF)
    lay = mm(a[:, d:], b[:, f:], TN).astype(BF)
    split_halves(text, lay, pages, ids, keep, send)
    total[...] = jnp.broadcast_to(jnp.sum(b.astype(F32), axis=0, keepdims=True), total.shape)


def attn_back_part(k, last, go, gp, qkv, lse, segc, segr, woc, dkv_in, dq, dkv):
    rows = dq.shape[0]
    heads = dq.shape[1] // TILE
    doc = mm(cat((go, gp)), woc[...], NT).astype(BF)
    total = qkv.shape[0]
    for h in range(heads):
        key = qkv[:, (heads + h) * TILE : (heads + h + 1) * TILE]
        val = qkv[:, (2 * heads + h) * TILE : (2 * heads + h + 1) * TILE]
        is_text = lax.broadcasted_iota(jnp.int32, (total, TILE), 1) < HEAD
        is_text_q = lax.broadcasted_iota(jnp.int32, (256, TILE), 1) < HEAD
        zero = jnp.zeros_like(key)
        key_text_t = jnp.where(is_text, key, zero).T
        key_lay_t = jnp.where(is_text, zero, key).T
        kc = slice(h * TILE, (h + 1) * TILE)
        vc = slice((heads + h) * TILE, (heads + h + 1) * TILE)
        if dkv_in is None:
            dkey = jnp.zeros((total, TILE), F32)
            dval = jnp.zeros((total, TILE), F32)
        else:
            dkey = dkv_in[:, kc]
            dval = dkv_in[:, vc]
        for a in range(0, rows, 256):
            q0 = k * rows + a
            query = qkv[q0 : q0 + 256, kc]
            up = doc[a : a + 256, kc]
            zero_q = jnp.zeros_like(query)
            up_text = jnp.where(is_text_q, up, zero_q)
            s = mm(key, query, NT)
            same = jnp.concatenate([segc[...]] * 2, axis=1) == segr[:, q0 : q0 + 256].astype(F32)
            p = jnp.where(same, jnp.exp(s - lse[h : h + 1, a : a + 256]), 0.0)
            dp_all = mm(val, up, NT)
            dp_text = mm(val, up_text, NT)
            ds_all = p * (dp_all - jnp.sum(dp_all * p, axis=0, keepdims=True))
            ds_text = p * (dp_text - jnp.sum(dp_text * p, axis=0, keepdims=True))
            ds_all = ds_all.astype(BF)
            ds_text = ds_text.astype(BF)
            dval = dval + mm(p.astype(BF), up)
            dkey = (
                dkey
                + mm(ds_text, jnp.where(is_text_q, query, zero_q))
                + mm(ds_all, jnp.where(is_text_q, zero_q, query))
            )
            dquery_t = mm(key_text_t, ds_text) + mm(key_lay_t, ds_all)
            dq[a : a + 256, kc] = dquery_t.T.astype(BF)
        dkv[:, kc] = dkey.astype(dkv.dtype)
        dkv[:, vc] = dval.astype(dkv.dtype)


def attn_back_mid_body(k, ids, go, gp, qkv, lse, segc, segr, woc, *refs):
    dkv_in = refs[0] if k else None
    attn_back_part(k, False, go, gp, qkv, lse, segc, segr, woc, dkv_in, *refs[-2:])


def attn_back_last_body(k, ids, go, gp, qkv, lse, segc, segr, woc, wct, *refs):
    dkv_in = refs[0] if k else None
    dq0 = refs[1] if k else None
    keep, send, dq, dkv = refs[-4:]
    attn_back_part(k, True, go, gp, qkv, lse, segc, segr, woc, dkv_in, dq, dkv)
    attn_dx(0, dq0 if k else dq, dkv, wct, keep, send)


def attn_dx(k, dq, dkv, wct, keep, send):
    rows, split = dq.shape
    part = mm(dq[...], wct[0:split, :]) + mm(dkv[k * rows : (k + 1) * rows, :], wct[split:, :])
    keep[...] = part[0 : rows // 2]
    send[...] = part[rows // 2 :].astype(BF)


def attn_dx_body(k, ids, dq, dkv, wct, keep, send):
    attn_dx(k, dq, dkv, wct, keep, send)


def attn_grad_body(d, n, pages, ids, *refs):
    xs, ups, dqs, ocs = refs[0 : 2 * n], refs[2 * n : 4 * n], refs[4 * n : 5 * n], refs[5 * n : 6 * n]
    dkv, keep, send, qb, dt, dl, ot, ol = refs[6 * n :]
    heads = ocs[0].shape[1] // TILE
    rows = dqs[0].shape[0]
    for c in range(3):
        for h in range(heads):
            for k in range(n):
                a = k * rows
                if c == 0:
                    tile = dqs[k][:, h * TILE : (h + 1) * TILE].astype(F32)
                    gt = (tile[:, 0:HEAD] * HEAD**-0.5).astype(BF)
                    gl = (tile[:, HEAD : HEAD + LHEAD] * LHEAD**-0.5).astype(BF)
                else:
                    col = ((c - 1) * heads + h) * TILE
                    gt = dkv[a : a + rows, col : col + HEAD]
                    gl = dkv[a : a + rows, col + HEAD : col + HEAD + LHEAD]
                i = c * heads + h
                dt[a : a + rows, i * HEAD : (i + 1) * HEAD] = gt
                dl[a : a + rows, i * LHEAD : (i + 1) * LHEAD] = gl
    for h in range(heads):
        for k in range(n):
            a = k * rows
            ot[a : a + rows, h * HEAD : (h + 1) * HEAD] = ocs[k][:, h * TILE : h * TILE + HEAD]
            ol[a : a + rows, h * LHEAD : (h + 1) * LHEAD] = ocs[k][
                :, h * TILE + HEAD : h * TILE + HEAD + LHEAD
            ]
    x = cat(xs)
    up = cat(ups)
    text = jnp.concatenate(
        [mm(x[:, 0:d], dt[...], TN).astype(BF), mm(up[:, 0:d], ot[...], TN).astype(BF)], axis=1
    )
    lay = jnp.concatenate(
        [mm(x[:, d:], dl[...], TN).astype(BF), mm(up[:, d:], ol[...], TN).astype(BF)], axis=1
    )
    split_halves(text, lay, pages, ids, keep, send)
    qb[...] = jnp.zeros_like(qb)
    qb[0:1, 0 : dt.shape[1]] = jnp.sum(dt[...].astype(F32), axis=0, keepdims=True)
    qb[0:1, d : d + dl.shape[1]] = jnp.sum(dl[...].astype(F32), axis=0, keepdims=True)


def smalls_body(n, ids, *refs):
    first, second = refs[0:n], refs[n : 2 * n]
    fb, qb, out = refs[2 * n :]
    one = sum(ref[...] for ref in first)
    two = sum(ref[...] for ref in second)
    rows = (one[0:1], two[0:1], one[2:3], one[1:2], two[2:3], two[1:2], fb[0:1, :], qb[0:1, :])
    for i, row in enumerate(rows):
        out[i : i + 1, :] = row


def away_body(n, ids, *refs):
    out = refs[2 * n]
    rows = out.shape[0] // n

    @pl.when(ids[0] == 0)
    def _():
        for k in range(n):
            out[k * rows : (k + 1) * rows, :] = refs[n + k][0:rows, :]

    @pl.when(ids[0] != 0)
    def _():
        for k in range(n):
            out[k * rows : (k + 1) * rows, :] = refs[k][0:rows, :]


def both_body(n, d, ids, *refs):
    got, text, lay = refs[2 * n :]
    s = ids[0]
    rows = got.shape[0] // n
    text[1 - s] = got[:, 0:d]
    lay[1 - s] = got[:, d:].astype(F32).T.astype(BF)

    def put(parts):
        mine = jnp.concatenate([ref[0:rows, :] for ref in parts], axis=0)
        text[s] = mine[:, 0:d]
        lay[s] = mine[:, d:].astype(F32).T.astype(BF)

    @pl.when(s == 0)
    def _():
        put(refs[0:n])

    @pl.when(s != 0)
    def _():
        put(refs[n : 2 * n])


def swap_body(ids, a, b, away):
    @pl.when(ids[0] == 0)
    def _():
        away[...] = b[...]

    @pl.when(ids[0] != 0)
    def _():
        away[...] = a[...]


def own_rows(ids, a, b, got, tr, ll, lanes):
    own = jnp.where(ids[0] == 0, a[...].astype(F32), b[...].astype(F32))
    oth = got[...].astype(F32)
    first = jnp.where(ids[0] == 0, own, oth)
    second = jnp.where(ids[0] == 0, oth, own)
    text = jnp.concatenate([first[0:tr], second[0:tr]], axis=0)
    lay = jnp.concatenate(
        [
            half[tr:, g * lanes : (g + 1) * lanes]
            for half in (first, second)
            for g in range(ll // (first.shape[0] - tr))
        ],
        axis=0,
    )
    return text, lay


def matrix_body(tr, ll, ids, a, b, got, text, lay):
    t, l = own_rows(ids, a, b, got, tr, ll, lay.shape[1])
    text[...] = t
    lay[...] = l


def proj_body(tr, ll, ids, a, b, got, qkv, out, lqkv, lout):
    et = qkv.shape[2]
    el = lqkv.shape[2]
    t, l = own_rows(ids, a, b, got, tr, ll, 4 * el)
    for c in range(3):
        qkv[c] = t[:, c * et : (c + 1) * et]
        lqkv[c] = l[:, c * el : (c + 1) * el]
    out[...] = t[:, 3 * et :].T
    lout[...] = l[:, 3 * el :].T


def swap(value, axis, bit):
    size = lax.axis_size(axis)
    return lax.ppermute(value, axis, [(i, i ^ bit) for i in range(size)])


def core_swap(value):
    return swap(value, "tensor", 1)


def chip_swap(value):
    return swap(value, "tensor", 2)


def other_section(value):
    return swap(value, "section", 1)


def around(value, axis):
    size = lax.axis_size(axis)
    return lax.ppermute(value, axis, [(i, (i + 1) % size) for i in range(size)])


def per_device(
    text_in,
    layout_in,
    text_cot,
    layout_cot,
    token_mask,
    box_mask,
    segments,
    text_qkv,
    text_qv_bias,
    text_out_w,
    text_ffn_in,
    text_ffn_bias,
    text_ffn_out,
    text_gains,
    text_biases,
    layout_qkv,
    layout_qv_bias,
    layout_out_w,
    layout_ffn_in,
    layout_ffn_bias,
    layout_ffn_out,
    layout_gains,
    layout_biases,
):
    sections = lax.axis_size("section")
    section = lax.axis_index("section")
    pages = lax.axis_size("dp")
    micro, mine, d = text_in.shape
    assert micro == sections == 2 and lax.axis_size("tensor") == 4 and segments.shape[1] == 1
    n = CHUNKS
    dl = layout_in.shape[2]
    width = d + dl
    rows = 4 * mine
    cb = mine // n
    rk = rows // n
    hk = rk // 2
    heads = text_qkv.shape[-1] // HEAD
    f = text_ffn_in.shape[-1]
    fl = layout_ffn_in.shape[-1]
    fw = f + fl
    et, el = heads * HEAD, heads * LHEAD
    wq = heads * TILE
    part = functools.partial
    ids = jnp.stack([section, lax.axis_index("tensor"), lax.axis_index("dp")]).astype(jnp.int32)

    qt = jnp.swapaxes(text_qkv[0], 1, 2)
    ql = jnp.swapaxes(layout_qkv[0], 1, 2)
    small_w = (qt, ql, text_out_w[0], layout_out_w[0], layout_ffn_in[0], layout_ffn_out[0])
    pieces = pages if pages <= 4 else 1
    deep = 16 * pieces
    qrows = -(-(3 * et + el) // deep) * deep
    quarter, rest = call(
        part(weights_body, pieces),
        [((qrows // pieces, d), BF), ((et + LHEAD + 2 * dl * dl // d, d), BF)],
        "weights",
        (pltpu.VMEM((qrows, d), BF),),
    )(ids, *small_w)
    got = [other_section(quarter)]
    xs = call(part(inputs_body, n), [((cb, width), BF)] * n, "inputs")(
        ids, text_in, jnp.swapaxes(layout_in, 1, 2)
    )
    mates = [chip_swap(x) for x in xs]
    for _ in range(pieces - 1):
        got.append(around(got[-1], "dp"))
    prm_own = call(params_body, [((16, width), F32)], "params")(
        ids,
        text_gains[0],
        text_biases[0],
        text_ffn_bias,
        text_qv_bias[0],
        layout_gains[0],
        layout_biases[0],
        layout_ffn_bias,
        layout_qv_bias[0],
    )[0]
    x_own = [jnp.concatenate([x, m], axis=0) for x, m in zip(xs, mates)]
    x_peer = [core_swap(x) for x in x_own]
    prm_oth = other_section(prm_own)
    rest_oth = other_section(rest)
    w1_oth = other_section(text_ffn_in[0])
    w2_oth = other_section(text_ffn_out[0])
    *cots, segr, segc = call(
        part(side_body, n),
        [((cb, width + 64), BF)] * n + [((1, rows), jnp.int32), ((rows, TILE), F32)],
        "side",
    )(
        ids,
        text_cot,
        jnp.swapaxes(layout_cot, 1, 2),
        token_mask,
        box_mask,
        segments.reshape(micro, 4, mine),
    )
    cot_mates = [chip_swap(c) for c in cots]

    def pair_sum(keep, send):
        s = call(pair_body, [((hk, width), BF)], "pair")(ids, keep, core_swap(send))[0]
        return s, chip_swap(s)

    acts = [((hk, width), F32), ((hk, width), BF)]
    norm_outs = [((hk, width), F32), ((hk, TILE), F32), ((hk, width), BF)]
    chunk_outs = acts + [((rk, wq), BF), ((8, rk), F32)]
    weights = []
    for j in range(sections):
        wct, woc, bc, w1l, w2l, prm = call(
            part(pack_body, j, pieces, heads),
            [
                ((3 * wq, width), BF),
                ((wq, width), BF),
                ((8, 3 * wq), F32),
                ((dl, fl), BF),
                ((fl, dl), BF),
                ((16, width), F32),
            ],
            "pack",
            (pltpu.VMEM((qrows, d), BF),),
        )(ids, *small_w, *got, rest_oth, prm_own, prm_oth)
        w1t, w2t = call(part(choose_body, j), [((d, f), BF), ((f, d), BF)], "choose")(
            ids, text_ffn_in[0], w1_oth, text_ffn_out[0], w2_oth
        )
        weights.append((wct, woc, bc, prm, (w1t, w1l, w2t, w2l)))

    kept = []
    hidden = []
    for j in range(sections):
        wct, woc, bc, prm, ffn = weights[j]
        first = call(part(attn_first_body, n), chunk_outs + [((rows, 3 * wq), BF)], "attn_first", us=4)(
            ids, *[x for pair in zip(x_own, x_peer) for x in pair], wct, bc, woc, segc, segr
        )
        qkv = first[4]
        parts = [first[0:4]]
        for k in range(1, n):
            parts.append(
                call(part(attn_next_body, k), chunk_outs, "attn_next", us=3)(ids, qkv, woc, segc, segr)
            )
        oc = [p[2] for p in parts]
        lse = [p[3] for p in parts]
        sums = [pair_sum(p[0], p[1]) for p in parts]
        n1, inv1, x1_own, x1_peer, act, slope, n2, inv2, y_own, y_peer = ([] for _ in range(10))
        sums2 = []
        for k in range(n):
            a, b, c = call(part(norm1_body, d), norm_outs, "norm1")(ids, *sums[k], x_own[k], prm)
            n1.append(a)
            inv1.append(b)
            x1_own.append(c)
            x1_peer.append(core_swap(c))
            keep, send, a, b = call(ffn_fwd_body, acts + [((rk, fw), BF)] * 2, "ffn_fwd")(
                ids, x1_own[k], x1_peer[k], *ffn, prm
            )
            act.append(a)
            slope.append(b)
            sums2.append(pair_sum(keep, send))
        for k in range(n):
            a, b, c = call(part(norm2_body, d), norm_outs, "norm2")(ids, *sums2[k], n1[k], prm)
            n2.append(a)
            inv2.append(b)
            y_own.append(c)
            if j + 1 < sections:
                y_peer.append(core_swap(c))
        hidden.append(y_own)
        kept.append((x_own, x_peer, qkv, oc, lse, n1, inv1, x1_own, x1_peer, act, slope, n2, inv2))
        x_own, x_peer = y_own, y_peer

    tr = d // (2 * pages)
    ll = dl // (2 * pages)
    grows = tr + (8 if ll % 8 == 0 else ll)
    half_outs = [((pages * grows, d), BF)] * 2 + [((8, width), F32)]

    def reduced(keep, send):
        value = call(pair_body, [((pages * grows, d), BF)], "gpair")(ids, keep, other_section(send))[0]
        return lax.psum_scatter(value, "dp", scatter_dimension=0, tiled=True)

    back_outs = [((hk, width), F32), ((hk, width), BF), ((8, width), F32)]
    grads = [None] * sections
    input_grads = [None] * sections
    small_sums = [None] * sections
    for j in reversed(range(sections)):
        x_own, x_peer, qkv, oc, lse, n1, inv1, x1_own, x1_peer, act, slope, n2, inv2 = kept[j]
        wct, woc, bc, prm, ffn = weights[j]
        dh2, dh2b, small2, dh2_peer, dpre, sums1 = ([] for _ in range(6))
        dxin = []
        for k in range(n):
            if j == sections - 1:
                a, b, c = call(part(back_top_body, d), back_outs, "back_top")(
                    ids, cots[k], cot_mates[k], n2[k], inv2[k], prm
                )
            else:
                x, a, b, c = call(part(back_next_body, d), [((hk, width), BF)] + back_outs, "back_next")(
                    ids, dh[k], *sums[k], n2[k], inv2[k], prm
                )
                dxin.append(x)
            dh2.append(a)
            dh2b.append(b)
            small2.append(c)
            dh2_peer.append(core_swap(b))
            keep, send, a = call(ffn_back_body, acts + [((rk, fw), BF)], "ffn_back")(
                ids, b, dh2_peer[k], slope[k], *ffn
            )
            dpre.append(a)
            sums1.append(pair_sum(keep, send))
        if dxin:
            input_grads[j + 1] = dxin
        outer = call(part(outer_body, d, f, n, pages), half_outs, "outer", us=3)
        both = [x for pair in zip(dh2b, dh2_peer) for x in pair]
        keep, send, _ = outer(ids, *both, *act)
        g2 = reduced(keep, send)
        both = [x for pair in zip(x1_own, x1_peer) for x in pair]
        keep, send, fb = outer(ids, *both, *dpre)
        g1 = reduced(keep, send)
        dh, dhb, small1, dh_peer, dq = ([] for _ in range(5))
        dkv = None
        for k in range(n):
            a, b, c = call(part(back_first_body, d), back_outs, "back_first")(
                ids, dh2[k], *sums1[k], n1[k], inv1[k], prm
            )
            dh.append(a)
            dhb.append(b)
            small1.append(c)
            dh_peer.append(core_swap(b))
            more = [dkv] if k else []
            if k + 1 < n:
                q, dkv = call(
                    part(attn_back_mid_body, k), [((rk, wq), BF), ((rows, 2 * wq), F32)], "attn_back", us=4
                )(ids, b, dh_peer[k], qkv, lse[k], segc, segr, woc, *more)
            else:
                more = more + dq[0:1]
                keep, send, q, dkv = call(
                    part(attn_back_last_body, k),
                    acts + [((rk, wq), BF), ((rows, 2 * wq), BF)],
                    "attn_back",
                    us=4,
                )(ids, b, dh_peer[k], qkv, lse[k], segc, segr, woc, wct, *more)
            dq.append(q)
        sums = [pair_sum(keep, send)]
        for k in range(1, n):
            keep, send = call(part(attn_dx_body, k), acts, "attn_dx", us=1)(ids, dq[k], dkv, wct)
            sums.append(pair_sum(keep, send))
        xs_all = [x for pair in zip(x_own, x_peer) for x in pair]
        ups_all = [x for pair in zip(dhb, dh_peer) for x in pair]
        keep, send, qb = call(
            part(attn_grad_body, d, n, pages),
            half_outs,
            "attn_grad",
            (
                pltpu.VMEM((rows, 3 * et), BF),
                pltpu.VMEM((rows, 3 * el), BF),
                pltpu.VMEM((rows, et), BF),
                pltpu.VMEM((rows, el), BF),
            ),
            us=3,
        )(ids, *xs_all, *ups_all, *dq, *oc, dkv)
        ga = reduced(keep, send)
        grads[j] = (g2, g1, ga)
        small_sums[j] = call(part(smalls_body, n), [((8, width), F32)], "smalls")(
            ids, *small1, *small2, fb, qb
        )[0]
    input_grads[0] = [
        call(back_last_body, [((hk, width), BF)], "back_last")(ids, dh[k], *sums[k])[0] for k in range(n)
    ]

    def collect(layers):
        parts = layers[0] + layers[1]
        away = call(part(away_body, n), [((mine, width), BF)], "away")(ids, *parts)[0]
        text, lay = call(
            part(both_body, n, d), [((micro, mine, d), BF), ((micro, dl, mine), BF)], "both", hbm=True
        )(ids, *parts, other_section(away))
        return text[None], jnp.swapaxes(lay, 1, 2)[None]

    hid_t, hid_l = collect(hidden)
    ing_t, ing_l = collect(input_grads)

    def away_half(index):
        a, b = grads[0][index], grads[1][index]
        away = call(swap_body, [((grows, d), BF)], "swap")(ids, a, b)[0]
        return a, b, other_section(away)

    mats = []
    for index in (0, 1):
        mats.append(
            call(
                part(matrix_body, tr, ll),
                [((2 * tr, f), F32), ((2 * ll, fl), F32)],
                "matrix",
                hbm=True,
            )(ids, *away_half(index))
        )
    (g2, lg2), (g1, lg1) = mats
    g_qkv, g_out, g_lqkv, g_lout = call(
        part(proj_body, tr, ll),
        [((3, 2 * tr, et), F32), ((et, 2 * tr), F32), ((3, 2 * ll, el), F32), ((el, 2 * ll), F32)],
        "proj",
        hbm=True,
    )(ids, *away_half(2))

    away = call(swap_body, [((8, width), F32)], "swap")(ids, *small_sums)[0]
    mine_now = jnp.where(section == 0, small_sums[0], small_sums[1])
    total = mine_now + other_section(away)
    bit = 1
    while bit < pages:
        total = total + swap(total, "dp", bit)
        bit *= 2
    shared = total[0:6]
    shared = shared + core_swap(shared)
    shared = shared + chip_swap(shared)
    qv = total[7, 0 : 3 * et].reshape(3, et)
    lqv = total[7, d : d + 3 * el].reshape(3, el)
    return (
        hid_t,
        hid_l,
        ing_t,
        ing_l,
        g_qkv[None],
        jnp.stack([qv[0], qv[2]])[None],
        g_out[None],
        g1[None],
        total[6:7, 0:f],
        g2.T[None],
        shared[None, 0:2, 0:d],
        shared[None, 2:6, 0:d],
        g_lqkv[None],
        jnp.stack([lqv[0], lqv[2]])[None],
        g_lout[None],
        lg1[None],
        total[6:7, f:fw],
        lg2.T[None],
        shared[None, 0:2, d:],
        shared[None, 2:6, d:],
    )


def solution(mesh):
    in_specs = (
        P(None, ("dp", "tensor"), None),
        P(None, ("dp", "tensor"), None),
        P(None, ("dp", "tensor"), None),
        P(None, ("dp", "tensor"), None),
        P(None, ("dp", "tensor")),
        P(None, ("dp", "tensor")),
        P(None, "dp", None),
        P("section", None, None, "tensor"),
        P("section", None, "tensor"),
        P("section", "tensor", None),
        P("section", None, "tensor"),
        P("section", "tensor"),
        P("section", "tensor", None),
        P("section", None, None),
        P("section", None, None),
        P("section", None, None, "tensor"),
        P("section", None, "tensor"),
        P("section", "tensor", None),
        P("section", None, "tensor"),
        P("section", "tensor"),
        P("section", "tensor", None),
        P("section", None, None),
        P("section", None, None),
    )
    out_specs = (
        P("section", None, ("dp", "tensor"), None),
        P("section", None, ("dp", "tensor"), None),
        P("section", None, ("dp", "tensor"), None),
        P("section", None, ("dp", "tensor"), None),
        P("section", None, "dp", "tensor"),
        P("section", None, "tensor"),
        P("section", "tensor", "dp"),
        P("section", "dp", "tensor"),
        P("section", "tensor"),
        P("section", "tensor", "dp"),
        P("section", None, None),
        P("section", None, None),
        P("section", None, "dp", "tensor"),
        P("section", None, "tensor"),
        P("section", "tensor", "dp"),
        P("section", "dp", "tensor"),
        P("section", "tensor"),
        P("section", "tensor", "dp"),
        P("section", None, None),
        P("section", None, None),
    )
    return jax.shard_map(
        per_device, mesh=mesh, in_specs=in_specs, out_specs=out_specs, check_vma=False
    )
```

```python
import functools

import jax
import jax.numpy as jnp
from jax import lax
from jax.experimental import pallas as pl
from jax.experimental.pallas import tpu as pltpu
from jax.sharding import PartitionSpec as P

HEAD = 64
LHEAD = 16
TILE = 128
CHUNKS = 2

EPS = 1e-05
MASKED = -1000000000.0
BF = jnp.bfloat16
F32 = jnp.float32

NT = (((1,), (1,)), ((), ()))
TN = (((0,), (0,)), ((), ()))
NN = (((1,), (0,)), ((), ()))


def mm(a, b, dims=NN):
    return lax.dot_general(a, b, dims, preferred_element_type=F32)


def call(body, outs, name, scratch=(), us=2, hbm=(), vmem=10):
    def run(turn, *args, loose=(), after=()):
        kept = 1 + len(args)
        extra = [turn.token] if turn.token is not None else []
        extra += list(after)

        def inner(*refs):
            given = refs[kept + len(extra) :]
            given[len(outs)][...] = jnp.zeros_like(given[len(outs)])
            body(*refs[0:kept], *given[0 : len(outs)], *given[len(outs) + 1 :])

        placed = [
            pltpu.with_memory_space_constraint(a, pltpu.HBM if i in loose else pltpu.VMEM)
            for i, a in enumerate(list(args) + extra)
        ]
        *results, turn.token = pl.pallas_call(
            inner,
            out_shape=[
                (jax.ShapeDtypeStruct if hbm is True or i in hbm else pltpu.VMEM)(shape, dtype)
                for i, (shape, dtype) in enumerate(outs)
            ]
            + [pltpu.VMEM((8, TILE), F32)],
            in_specs=[pl.BlockSpec(memory_space=pltpu.SMEM)]
            + [pl.BlockSpec(memory_space=pltpu.VMEM)] * len(placed),
            scratch_shapes=list(scratch),
            name=name,
            cost_estimate=pl.CostEstimate(flops=int(us * 10**8), transcendentals=0, bytes_accessed=0),
            compiler_params=pltpu.CompilerParams(vmem_limit_bytes=vmem * 1024 * 1024),
        )(turn.ids, *placed)
        return results

    return run


class Turn:
    def __init__(self, ids):
        self.ids = ids
        self.token = None


def up_to_tile(lanes):
    return -(-lanes // TILE) * TILE


def cat(refs, a0=None, a1=None):
    return jnp.concatenate([ref[:, a0:a1] for ref in refs], axis=0)


def attn_send_body(pieces, ids, qt, ql, ot, ol, full, piece):
    et, d = qt.shape[1:]
    el, dl = ql.shape[1:]
    full[3 * et :, :] = jnp.zeros_like(full[3 * et :, :])
    for c in range(3):
        full[c * et : (c + 1) * et, :] = qt[c]
        full[3 * et : 3 * et + el, c * dl : (c + 1) * dl] = ql[c]
    at = 3 * et + el
    full[at : at + et, :] = ot[...]
    for h in range(el // LHEAD):
        full[at + et : at + et + LHEAD, h * dl : (h + 1) * dl] = ol[h * LHEAD : (h + 1) * LHEAD, :]
    half = full.shape[0] // 2
    size = piece.shape[0]
    spot = ids[2] if pieces > 1 else 0
    piece[...] = full[pl.ds(pl.multiple_of(half + spot * size, 8), size), :]


def first_half_body(ids, full, direct):
    direct[...] = full[0 : direct.shape[0], :]


def ffn_lead_body(d, ids, full, direct):
    half = d // 2
    direct[0:half, :] = full[0:half, :]
    direct[half:d, :] = full[d : d + half, :]
    direct[d:, :] = full[2 * d :, :]


def ffn_send_body(pieces, ids, w1, w2, w1l, w2l, full, piece):
    d, f = w1.shape
    dl = w1l.shape[0]
    deep = dl * dl // d
    full[0:d, :] = w1[...]
    full[d : 2 * d, :] = w2[...]
    for g in range(d // dl):
        full[2 * d : 2 * d + deep, g * dl : (g + 1) * dl] = w1l[g * deep : (g + 1) * deep, :]
        full[2 * d + deep :, g * dl : (g + 1) * dl] = w2l[g * deep : (g + 1) * deep, :]
    half = d // 2
    size = piece.shape[0] // 2
    at = pl.multiple_of(half + (ids[2] if pieces > 1 else 0) * size, 8)
    piece[0:size, :] = w1[pl.ds(at, size), :]
    piece[size:, :] = w2[pl.ds(at, size), :]


def inputs_body(chunks, ids, tin, lin, *outs):
    s = ids[0]
    rows = tin.shape[1] // chunks
    d = tin.shape[2]
    lay = lin[s].T
    for k in range(chunks):
        outs[k][:, 0:d] = tin[s, k * rows : (k + 1) * rows, :]
        outs[k][:, d:] = lay[k * rows : (k + 1) * rows, :]


def side_body(chunks, ids, tcot, lcot, tmask, bmask, seg, *refs):
    s = ids[0]
    cots = refs[0:chunks]
    segr, segc = refs[chunks:]
    mine, d = tcot.shape[1:]
    width = d + lcot.shape[1]
    rows = mine // chunks
    lay = lcot[s].T
    wt = (0.25 + tmask[pl.ds(s, 1), :].astype(F32)).astype(BF).astype(F32)
    wb = (0.25 + bmask[pl.ds(s, 1), :].astype(F32)).astype(BF).astype(F32)
    wt = jnp.broadcast_to(wt, (TILE, mine)).T
    wb = jnp.broadcast_to(wb, (TILE, mine)).T
    for k in range(chunks):
        a, b = k * rows, (k + 1) * rows
        cots[k][:, 0:d] = tcot[s, a:b, :]
        cots[k][:, d:width] = lay[a:b, :]
        cots[k][:, width : width + 32] = wt[a:b, 0:32].astype(BF)
        cots[k][:, width + 32 : width + 64] = wb[a:b, 0:32].astype(BF)
    at = 0
    for first in (0, 1):
        for k in range(chunks):
            for step in (first, first ^ 2):
                block = seg[s, pl.ds(ids[1] ^ step, 1), k * rows : (k + 1) * rows]
                segr[0:1, at : at + rows] = block
                at += rows
    segc[...] = jnp.broadcast_to(segr[...].astype(F32), (TILE, at)).T


def params_body(ids, tg, tb, tf, tq, lg, lb, lf, lq, prm):
    d = tg.shape[1]
    prm[...] = jnp.zeros_like(prm)
    for a, gains, biases, hidden, qv in ((0, tg, tb, tf, tq), (d, lg, lb, lf, lq)):
        prm[0:2, a : a + gains.shape[1]] = gains[...]
        prm[2:6, a : a + gains.shape[1]] = biases[...]
        prm[6:7, a : a + hidden.shape[1]] = hidden[...]
        prm[7:9, a : a + qv.shape[1]] = qv[...]


def assemble(full, base, rows, direct, got, ids, at, size):
    half = rows // 2
    full[base : base + half, :] = direct
    n = len(got)
    for k in range(n):
        place = base + half + lax.rem(ids[2] + (n - k), n) * size
        full[pl.ds(pl.multiple_of(place, 8), size), :] = got[k][at : at + size, :]


def pick_attn_body(layer, pieces, ids, own, direct, prm_own, prm_oth, *refs):
    got = refs[0:pieces]
    out, prm = refs[pieces:]

    @pl.when(ids[0] == layer)
    def _():
        out[...] = own[...]
        prm[...] = prm_own[...]

    @pl.when(ids[0] != layer)
    def _():
        assemble(out, 0, out.shape[0], direct[...], got, ids, 0, got[0].shape[0])
        prm[...] = prm_oth[...]


def pick_ffn_body(layer, pieces, d, ids, own, direct, *refs):
    got = refs[0:pieces]
    out = refs[pieces]

    @pl.when(ids[0] == layer)
    def _():
        out[...] = own[...]

    @pl.when(ids[0] != layer)
    def _():
        size = got[0].shape[0] // 2
        half = d // 2
        assemble(out, 0, d, direct[0:half, :], got, ids, 0, size)
        assemble(out, d, d, direct[half:d, :], got, ids, size, size)
        out[2 * d :, :] = direct[d:, :]


def unfold_body(d, ids, own, mate, w1l, w2l):
    dl = w1l.shape[0]
    fl = w1l.shape[1] // 2
    deep = dl * dl // d
    for side, ref in ((0, own), (1, mate)):
        for g in range(d // dl):
            a = 2 * d
            w1l[g * deep : (g + 1) * deep, side * fl : (side + 1) * fl] = ref[
                a : a + deep, g * dl : (g + 1) * dl
            ]
            w2l[side * fl + g * deep : side * fl + (g + 1) * deep, :] = ref[
                a + deep : a + 2 * deep, g * dl : (g + 1) * dl
            ]


def pack_body(et, el, f, fl, ids, q0, q1, prm0, prm1, wct, woc, bc, fb):
    d = q0.shape[1]
    dl = wct.shape[1] - d
    hs = et // HEAD
    heads = 2 * hs
    wct[...] = jnp.zeros_like(wct)
    woc[...] = jnp.zeros_like(woc)
    bc[...] = jnp.zeros_like(bc)
    at = 3 * et + el
    for side, q, prm in ((0, q0, prm0), (1, q1, prm1)):
        for h in range(hs):
            i = side * hs + h
            for c in range(3):
                row = (c * heads + i) * TILE
                wt = q[c * et + h * HEAD : c * et + (h + 1) * HEAD, :]
                wl = q[3 * et + h * LHEAD : 3 * et + (h + 1) * LHEAD, c * dl : (c + 1) * dl]
                if c == 0:
                    wt = (wt.astype(F32) * HEAD**-0.5).astype(BF)
                    wl = (wl.astype(F32) * LHEAD**-0.5).astype(BF)
                wct[row : row + HEAD, 0:d] = wt
                wct[row + HEAD : row + HEAD + LHEAD, d:] = wl
            row = i * TILE
            woc[row : row + HEAD, 0:d] = q[at + h * HEAD : at + (h + 1) * HEAD, :]
            woc[row + HEAD : row + HEAD + LHEAD, d:] = q[
                at + et : at + et + LHEAD, h * dl : (h + 1) * dl
            ]
            for p, c, st, sl in ((7, 0, HEAD**-0.5, LHEAD**-0.5), (8, 2, 1.0, 1.0)):
                col = (c * heads + i) * TILE
                bc[0:1, col : col + HEAD] = prm[p : p + 1, h * HEAD : (h + 1) * HEAD] * st
                bc[0:1, col + HEAD : col + HEAD + LHEAD] = (
                    prm[p : p + 1, d + h * LHEAD : d + (h + 1) * LHEAD] * sl
                )
        fb[0:1, side * f : (side + 1) * f] = prm[6:7, 0:f]
        fb[0:1, 2 * f + side * fl : 2 * f + (side + 1) * fl] = prm[6:7, d : d + fl]


def gelu_pair(pre):
    phi = 0.5 * (1.0 + lax.erf(pre * (0.5**0.5)))
    slope = phi + pre * (jnp.exp(-0.5 * pre * pre) * 0.3989422804014327)
    return pre * phi, slope


def crossed(s, r):
    n = s.shape[0] // 2
    top = s[0:n, :].astype(F32) + r[n : 2 * n, :].astype(F32)
    low = s[n : 2 * n, :].astype(F32) + r[0:n, :].astype(F32)
    return jnp.concatenate([top, low], axis=0)


def norm(h, prm, gain_row, shift_row, d, normed, inv):
    ivs, outs = [], []
    for a0, a1 in ((0, d), (d, h.shape[1])):
        x = h[:, a0:a1]
        centred = x - jnp.mean(x, axis=-1, keepdims=True)
        iv = lax.rsqrt(jnp.mean(centred * centred, axis=-1, keepdims=True) + EPS)
        n = centred * iv
        normed[:, a0:a1] = n
        outs.append(n * prm[gain_row : gain_row + 1, a0:a1] + prm[shift_row : shift_row + 1, a0:a1])
        ivs.append(iv)
    lane = lax.broadcasted_iota(jnp.int32, inv.shape, 1)
    inv[...] = jnp.where(lane < HEAD, ivs[0], ivs[1])
    return outs


def project(x, wct, bc, q, kv):
    split = q.shape[1]
    q[...] = (mm(x, wct[0:split, :], NT) + bc[0:1, 0:split]).astype(BF)
    kv[...] = (mm(x, wct[split:, :], NT) + bc[0:1, split:]).astype(BF)


def project_body(n, ids, wct, bc, *refs):
    x = cat(refs[0:n])
    split = refs[n].shape[1]
    rows = refs[0].shape[0]
    q = (mm(x, wct[0:split, :], NT) + bc[0:1, 0:split]).astype(BF)
    kv = (mm(x, wct[split:, :], NT) + bc[0:1, split:]).astype(BF)
    for k in range(n):
        refs[n + k][...] = q[k * rows : (k + 1) * rows]
        refs[2 * n + k][...] = kv[k * rows : (k + 1) * rows]


def heads_columns(own, peer, i, heads, value):
    base = heads * TILE if value else 0
    a = base + i * TILE
    b = base + (i + heads // 2) % heads * TILE
    return jnp.concatenate([ref[:, a : a + TILE] for ref in own] + [ref[:, b : b + TILE] for ref in peer], axis=0)


def same_doc(segc, segr, q0, n):
    seg = segc[...]
    if n > TILE:
        seg = jnp.concatenate([seg] * (n // TILE), axis=1)
    return seg == segr[:, q0 : q0 + n].astype(F32)


def attn_body(n, ids, segc, segr, woc, *refs):
    xs, qs, own, peer = (refs[i * n : (i + 1) * n] for i in range(4))
    outs = refs[4 * n : 5 * n]
    oc, lse, sent = refs[5 * n :]
    rows = oc.shape[0]
    heads = oc.shape[1] // TILE
    same = same_doc(segc, segr, 0, rows)
    lse[...] = jnp.zeros_like(lse)
    for h in range(heads):
        key = heads_columns(own, peer, h, heads, False)
        val_t = heads_columns(own, peer, h, heads, True).T
        query = cat(qs, h * TILE, (h + 1) * TILE)
        s = jnp.where(same, mm(key, query, NT), MASKED)
        top = jnp.max(s, axis=0, keepdims=True)
        p = jnp.exp(s - top)
        total = jnp.sum(p, axis=0, keepdims=True)
        o = mm(val_t, p.astype(BF)) / total
        oc[:, h * TILE : (h + 1) * TILE] = o.T.astype(BF)
        lse[h : h + 1, :] = top + jnp.log(total)
    part = mm(oc[...], woc[...]).astype(BF)
    step = rows // n
    width = xs[0].shape[1]
    for k in range(n):
        sent[k * step : (k + 1) * step, 0:width] = xs[k][...]
    half = heads // 2 * TILE
    sent[:, width : width + half] = oc[:, half:]
    if width + half < sent.shape[1]:
        sent[:, width + half :] = jnp.zeros_like(sent[:, width + half :])
    for k in range(n):
        outs[k][...] = part[k * step : (k + 1) * step]


def hidden_parts(own, mate, w1l, w2l):
    f = own.shape[1]
    fl = w1l.shape[1]
    width = w1l.shape[0]
    d = (own.shape[0] * f - width * fl) // (2 * f)
    w1, w2 = slice(0, d), slice(d, d + f)
    return (
        (0, d, 0, f, own.at[w1], own.at[w2]),
        (0, d, f, 2 * f, mate.at[w1], mate.at[w2]),
        (d, d + width, 2 * f, 2 * f + fl, w1l, w2l),
    )


def for_mate(a, b, d, f, fl, sent):
    width = a.shape[1]
    sent[:, 0:width] = a[...]
    sent[:, width : width + f] = b[:, f : 2 * f]
    sent[:, width + f :] = b[:, 2 * f + fl :]


def ffn_body(ids, s, r, x, prm, fb, own, mate, w1l, w2l, out, n1, inv, xb, act, slope, sent):
    d = n1.shape[1] - w1l.shape[0]
    h = crossed(s, r) + x[...].astype(F32) + prm[2:3, :]
    text, lay = norm(h, prm, 0, 3, d, n1, inv)
    xb[:, 0:d] = text.astype(BF)
    xb[:, d:] = lay.astype(BF)
    parts = []
    for a0, a1, f0, f1, w1, w2 in hidden_parts(own, mate, w1l, w2l):
        pre = mm(xb[:, a0:a1], w1[...]) + fb[0:1, f0:f1]
        g, gp = gelu_pair(pre)
        g = g.astype(BF)
        act[:, f0:f1] = g
        slope[:, f0:f1] = gp.astype(BF)
        parts.append(mm(g, w2[...]))
    out[:, 0:d] = (parts[0] + parts[1]).astype(BF)
    out[:, d:] = parts[2].astype(BF)
    for_mate(xb, act, d, own.shape[1], w1l.shape[1] // 2, sent)


def second_norm(d, s, r, n1, prm, n2, inv, y):
    h = n1[...] * prm[0:1, :] + prm[3:4, :] + crossed(s, r) + prm[4:5, :]
    text, lay = norm(h, prm, 1, 5, d, n2, inv)
    y[:, 0:d] = text.astype(BF)
    y[:, d:] = lay.astype(BF)


def norm_project_body(d, ids, s, r, n1, prm, wct, bc, n2, inv, y, q, kv):
    second_norm(d, s, r, n1, prm, n2, inv, y)
    project(y[...], wct, bc, q, kv)


def norm_back(dy, normed, inv, prm, gain_row, d, dh, dhb, small):
    small[...] = jnp.zeros_like(small)
    mine = dy.shape[0] // 2
    for a0, a1, lane in ((0, d, 0), (d, dy.shape[1], HEAD)):
        up = dy[:, a0:a1]
        n = normed[:, a0:a1]
        scaled = up * prm[gain_row : gain_row + 1, a0:a1]
        inner = (
            scaled
            - jnp.mean(scaled, axis=-1, keepdims=True)
            - n * jnp.mean(scaled * n, axis=-1, keepdims=True)
        )
        g = inner * inv[:, lane : lane + 1]
        dh[:, a0:a1] = g
        dhb[:, a0:a1] = g.astype(BF)
        small[0:1, a0:a1] = jnp.sum(up[0:mine] * n[0:mine], axis=0, keepdims=True)
        small[1:2, a0:a1] = jnp.sum(up[0:mine], axis=0, keepdims=True)
        small[2:3, a0:a1] = jnp.sum(g[0:mine], axis=0, keepdims=True)


def ffn_back(dhb, slope, own, mate, w1l, w2l, dpre, out, sent):
    d = out.shape[1] - w1l.shape[0]
    parts = []
    for a0, a1, f0, f1, w1, w2 in hidden_parts(own, mate, w1l, w2l):
        dact = mm(dhb[:, a0:a1], w2[...], NT)
        dp = (dact * slope[:, f0:f1].astype(F32)).astype(BF)
        dpre[:, f0:f1] = dp
        parts.append(mm(dp, w1[...], NT))
    out[:, 0:d] = (parts[0] + parts[1]).astype(BF)
    out[:, d:] = parts[2].astype(BF)
    for_mate(dhb, dpre, d, own.shape[1], w1l.shape[1] // 2, sent)


def turn_body(ids, s, r, n1, prm, cot0, cot1, slope, own, mate, w1l, w2l, y, dh, dhb, small, dpre, out, sent, n2, inv):
    d = n1.shape[1] - w1l.shape[0]
    second_norm(d, s, r, n1, prm, n2, inv, y)
    width = n2.shape[1]
    parts = []
    for cot in (cot0, cot1):
        c = cot[...].astype(F32)
        lane = lax.broadcasted_iota(jnp.int32, (c.shape[0], width), 1)
        w = jnp.where(lane < d, c[:, width : width + 1], c[:, width + 32 : width + 33])
        parts.append(c[:, 0:width] * w)
    dy = jnp.concatenate(parts, axis=0)
    norm_back(dy, n2, inv, prm, 1, d, dh, dhb, small)
    ffn_back(dhb, slope, own, mate, w1l, w2l, dpre, out, sent)


def back_next_body(ids, dh_up, s, r, n2, inv, prm, slope, own, mate, w1l, w2l, dxin, dh, dhb, small, dpre, out, sent):
    d = n2.shape[1] - w1l.shape[0]
    dx = (dh_up[...] + crossed(s, r)).astype(BF)
    dxin[...] = dx
    norm_back(dx.astype(F32), n2, inv, prm, 1, d, dh, dhb, small)
    ffn_back(dhb, slope, own, mate, w1l, w2l, dpre, out, sent)


def attn_back_body(k, n, d, ids, dh2, s1, r1, n1, inv, prm, segc, segr, woc, lse, *refs):
    q = refs[0]
    own, peer = refs[1 : 1 + n], refs[1 + n : 1 + 2 * n]
    refs = refs[1 + 2 * n :]
    before = refs[0] if k else None
    last = k == n - 1
    dh, dhb, small, dq = refs[1 if k else 0 :][0:4]
    outs = refs[5 if k else 4 :]
    norm_back(dh2[...] + crossed(s1, r1), n1, inv, prm, 0, d, dh, dhb, small)
    rows = dq.shape[0]
    heads = dq.shape[1] // TILE
    total = 2 * n * rows
    a0 = k * rows
    doc = mm(dhb[...], woc[...], NT).astype(BF)
    same = same_doc(segc, segr, a0, rows)
    text_t = lax.broadcasted_iota(jnp.int32, (total, TILE), 1) < HEAD
    text_q = lax.broadcasted_iota(jnp.int32, (rows, TILE), 1) < HEAD
    for h in range(heads):
        hc = slice(h * TILE, (h + 1) * TILE)
        vc = slice((heads + h) * TILE, (heads + h + 1) * TILE)
        key = heads_columns(own, peer, h, heads, False)
        val = heads_columns(own, peer, h, heads, True)
        zero = jnp.zeros_like(key)
        query = q[:, hc]
        up = doc[:, hc]
        zero_q = jnp.zeros_like(query)
        s = mm(key, query, NT)
        p = jnp.where(same, jnp.exp(s - lse[h : h + 1, a0 : a0 + rows]), 0.0)
        dp_all = mm(val, up, NT)
        dp_text = mm(val, jnp.where(text_q, up, zero_q), NT)
        ds_all = (p * (dp_all - jnp.sum(dp_all * p, axis=0, keepdims=True))).astype(BF)
        ds_text = (p * (dp_text - jnp.sum(dp_text * p, axis=0, keepdims=True))).astype(BF)
        dval = mm(p.astype(BF), up)
        dkey = mm(ds_text, jnp.where(text_q, query, zero_q)) + mm(ds_all, jnp.where(text_q, zero_q, query))
        dq_t = mm(jnp.where(text_t, key, zero).T, ds_text) + mm(jnp.where(text_t, zero, key).T, ds_all)
        dq[:, hc] = dq_t.T.astype(BF)
        for col, value in ((hc, dkey), (vc, dval)):
            if before is not None:
                value = value + before[:, col]
            if last:
                outs[0][:, col] = value[0 : total // 2]
                for i in range(n):
                    at = total // 2 + i * rows
                    outs[1 + i][:, col] = value[at : at + rows].astype(BF)
            else:
                outs[0][:, col] = value


def dx_body(k, ids, dq, mine, got, wct, out, dkv, sent):
    rows, split = dq.shape
    half = split // 2
    a, b = k * rows, (k + 1) * rows
    far = got[...]
    far = jnp.concatenate(
        [far[:, half:split], far[:, 0:half], far[:, split + half :], far[:, split : split + half]], axis=1
    )
    dkv[...] = (mine[a:b, :] + far.astype(F32)).astype(BF)
    out[...] = (mm(dq[...], wct[0:split, :]) + mm(dkv[...], wct[split:, :])).astype(BF)
    for i, part in enumerate((dq[:, half:], dkv[:, half:split], dkv[:, split + half :])):
        sent[:, i * half : (i + 1) * half] = part


def back_last_body(ids, dh, s, r, dxin):
    dxin[...] = (dh[...] + crossed(s, r)).astype(BF)


def put_halves(text, lay, pages, ids, keep, send, i, n):
    tr = text.shape[0] // (2 * pages)
    ll = lay.shape[0] // (2 * pages)
    lanes = lay.shape[1]
    lr = 8 if ll % 8 == 0 else ll
    rows = tr + lr
    blank = keep.shape[1] - ll // lr * lanes

    def put(order):
        for ref, half in zip((keep, send), order):
            for z in range(pages):
                at = (z * n + i) * rows
                a = (2 * z + half) * tr
                ref[at : at + tr, :] = text[a : a + tr]
                for g in range(ll // lr):
                    b = (2 * z + half) * ll + g * lr
                    ref[at + tr : at + rows, g * lanes : (g + 1) * lanes] = lay[b : b + lr]
                if blank:
                    ref[at + tr : at + rows, ref.shape[1] - blank :] = jnp.zeros((lr, blank), ref.dtype)

    @pl.when(ids[0] == 0)
    def _():
        put((0, 1))

    @pl.when(ids[0] != 0)
    def _():
        put((1, 0))


def both_cores(own, mate, parts, at):
    left = jnp.concatenate([jnp.concatenate([ref[:, a:b] for a, b in parts], axis=1) for ref in own], axis=0)
    size = left.shape[1]
    return jnp.concatenate([left] + [ref[:, at : at + size] for ref in mate], axis=0)


def ffn_grad_body(d, f, fl, n, pages, ids, *refs):
    up, act, x, dpre, sent, sent_up = (refs[i * n : (i + 1) * n] for i in range(6))
    keep, send, total = refs[6 * n :]
    width = x[0].shape[1]
    hidden = ((0, f), (2 * f, 2 * f + fl))
    for i, (a, b, a_mate) in enumerate(((up, act, sent_up), (x, dpre, sent))):
        left = both_cores(a, a_mate, ((0, width),), 0)
        right = both_cores(b, (sent, sent_up)[i], hidden, width)
        text = mm(left[:, 0:d], right[:, 0:f], TN).astype(BF)
        lay = mm(left[:, d:], right[:, f:], TN).astype(BF)
        put_halves(text, lay, pages, ids, keep, send, i, 2)
    total[...] = jnp.broadcast_to(jnp.sum(right.astype(F32), axis=0, keepdims=True), total.shape)


def attn_grad_body(d, n, pages, ids, *refs):
    xs, ups, dqs, dkvs, ups_mate, sent_up = (refs[i * n : (i + 1) * n] for i in range(6))
    oc, sent, keep, send, qb = refs[6 * n :]
    width = xs[0].shape[1]
    half = dqs[0].shape[1] // 2
    hs = half // TILE
    x = both_cores(xs, (sent,), ((0, width),), 0)
    up = both_cores(ups, ups_mate, ((0, width),), 0)
    o = both_cores((oc,), (sent,), ((0, half),), width)
    grads = (
        both_cores(dqs, sent_up, ((0, half),), 0),
        both_cores(dkvs, sent_up, ((0, half),), half),
        both_cores(dkvs, sent_up, ((2 * half, 3 * half),), 2 * half),
    )

    def lanes(value, a, size):
        return [value[:, h * TILE + a : h * TILE + a + size] for h in range(hs)]

    tq = jnp.concatenate([v for g in grads for v in lanes(g, 0, HEAD)], axis=1)
    lq = jnp.concatenate([v for g in grads for v in lanes(g, HEAD, LHEAD)], axis=1)
    to = jnp.concatenate(lanes(o, 0, HEAD), axis=1)
    lo = jnp.concatenate(lanes(o, HEAD, LHEAD), axis=1)
    et, el = hs * HEAD, hs * LHEAD

    def scaled(value, size, width):
        lane = lax.broadcasted_iota(jnp.int32, value.shape, 1)
        return jnp.where(lane < size, value * width**-0.5, value)

    text = jnp.concatenate(
        [scaled(mm(x[:, 0:d], tq, TN), et, HEAD).astype(BF), mm(up[:, 0:d], to, TN).astype(BF)], axis=1
    )
    lay = jnp.concatenate(
        [scaled(mm(x[:, d:], lq, TN), el, LHEAD).astype(BF), mm(up[:, d:], lo, TN).astype(BF)], axis=1
    )
    put_halves(text, lay, pages, ids, keep, send, 0, 1)
    qb[...] = jnp.zeros_like(qb)
    sums = jnp.sum(tq.astype(F32), axis=0, keepdims=True)
    qb[0:1, 0 : 3 * et] = scaled(sums, et, HEAD)
    sums = jnp.sum(lq.astype(F32), axis=0, keepdims=True)
    qb[0:1, d : d + 3 * el] = scaled(sums, el, LHEAD)


def smalls_body(n, ids, *refs):
    first, second = refs[0:n], refs[n : 2 * n]
    fb, qb, out = refs[2 * n :]
    one = sum(ref[...] for ref in first)
    two = sum(ref[...] for ref in second)
    rows = (one[0:1], two[0:1], one[2:3], one[1:2], two[2:3], two[1:2], fb[0:1, :], qb[0:1, :])
    for i, row in enumerate(rows):
        out[i : i + 1, :] = row


def away_body(n, ids, *refs):
    out = refs[2 * n]
    rows = out.shape[0] // n

    @pl.when(ids[0] == 0)
    def _():
        for k in range(n):
            out[k * rows : (k + 1) * rows, :] = refs[n + k][0:rows, :]

    @pl.when(ids[0] != 0)
    def _():
        for k in range(n):
            out[k * rows : (k + 1) * rows, :] = refs[k][0:rows, :]


def both_body(n, d, ids, *refs):
    got, text, lay = refs[2 * n :]
    s = ids[0]
    rows = got.shape[0] // n
    text[1 - s] = got[:, 0:d]
    lay[1 - s] = got[:, d:].astype(F32).T.astype(BF)

    def put(parts):
        mine = jnp.concatenate([ref[0:rows, :] for ref in parts], axis=0)
        text[s] = mine[:, 0:d]
        lay[s] = mine[:, d:].astype(F32).T.astype(BF)

    @pl.when(s == 0)
    def _():
        put(refs[0:n])

    @pl.when(s != 0)
    def _():
        put(refs[n : 2 * n])


def add_body(ids, keep, got, out):
    out[...] = (keep[...].astype(F32) + got[...].astype(F32)).astype(BF)


def spread_body(pages, ids, keep, got, *outs):
    rows = outs[0].shape[0]
    for k in range(pages):
        at = pl.multiple_of(lax.rem(ids[2] + k, pages) * rows, 8)
        outs[k][...] = (
            keep[pl.ds(at, rows), :].astype(F32) + got[pl.ds(at, rows), :].astype(F32)
        ).astype(BF)


def gather_body(ids, *refs):
    out = refs[-1]
    total = refs[0][...].astype(F32)
    for ref in refs[1:-1]:
        total = total + ref[...].astype(F32)
    out[...] = total.astype(BF)


def swap_body(ids, a, b, away):
    @pl.when(ids[0] == 0)
    def _():
        away[...] = b[...]

    @pl.when(ids[0] != 0)
    def _():
        away[...] = a[...]


def own_rows(ids, a, b, got, tr, ll, lanes):
    own = jnp.where(ids[0] == 0, a.astype(F32), b.astype(F32))
    oth = got.astype(F32)
    first = jnp.where(ids[0] == 0, own, oth)
    second = jnp.where(ids[0] == 0, oth, own)
    text = jnp.concatenate([first[0:tr], second[0:tr]], axis=0)
    lay = jnp.concatenate(
        [
            half[tr:, g * lanes : (g + 1) * lanes]
            for half in (first, second)
            for g in range(ll // (first.shape[0] - tr))
        ],
        axis=0,
    )
    return text, lay


def matrices_body(tr, ll, ids, a, b, got, *outs):
    rows = a.shape[0] // (len(outs) // 2)
    for i in range(len(outs) // 2):
        at = slice(i * rows, (i + 1) * rows)
        text, lay = outs[2 * i : 2 * i + 2]
        text[...], lay[...] = own_rows(ids, a[at, :], b[at, :], got[at, :], tr, ll, lay.shape[1])


def proj_body(tr, ll, ids, a, b, got, qkv, out, lqkv, lout):
    et = qkv.shape[2]
    el = lqkv.shape[2]
    t, l = own_rows(ids, a[...], b[...], got[...], tr, ll, 4 * el)
    for c in range(3):
        qkv[c] = t[:, c * et : (c + 1) * et]
        lqkv[c] = l[:, c * el : (c + 1) * el]
    out[...] = t[:, 3 * et :].T
    lout[...] = l[:, 3 * el :].T


def swap(value, axis, bit):
    size = lax.axis_size(axis)
    return lax.ppermute(value, axis, [(i, i ^ bit) for i in range(size)])


def core_swap(value):
    return swap(value, "tensor", 1)


def chip_swap(value):
    return swap(value, "tensor", 2)


def other_section(value):
    return swap(value, "section", 1)


def around(value, axis):
    size = lax.axis_size(axis)
    return lax.ppermute(value, axis, [(i, (i + 1) % size) for i in range(size)])


def per_device(
    text_in,
    layout_in,
    text_cot,
    layout_cot,
    token_mask,
    box_mask,
    segments,
    text_qkv,
    text_qv_bias,
    text_out_w,
    text_ffn_in,
    text_ffn_bias,
    text_ffn_out,
    text_gains,
    text_biases,
    layout_qkv,
    layout_qv_bias,
    layout_out_w,
    layout_ffn_in,
    layout_ffn_bias,
    layout_ffn_out,
    layout_gains,
    layout_biases,
):
    sections = lax.axis_size("section")
    section = lax.axis_index("section")
    pages = lax.axis_size("dp")
    micro, mine, d = text_in.shape
    assert micro == sections == 2 and lax.axis_size("tensor") == 4 and segments.shape[1] == 1
    n = CHUNKS
    dl = layout_in.shape[2]
    width = d + dl
    rows = 4 * mine
    mine_rows = mine
    own = 2 * mine
    cb = mine // n
    hk = 2 * cb
    hs = text_qkv.shape[-1] // HEAD
    heads = 2 * hs
    f = text_ffn_in.shape[-1]
    fl = layout_ffn_in.shape[-1]
    fw = 2 * (f + fl)
    et, el = hs * HEAD, hs * LHEAD
    wq = heads * TILE
    part = functools.partial
    ids = Turn(
        jnp.stack([section, lax.axis_index("tensor"), lax.axis_index("dp")]).astype(jnp.int32)
    )

    pieces = pages if pages <= 4 else 1
    arows = 3 * et + el + et + LHEAD
    attn_own, piece = call(
        part(attn_send_body, pieces),
        [((arows, d), BF), ((arows // 2 // pieces, d), BF)],
        "attn_send",
    )(
        ids,
        jnp.swapaxes(text_qkv[0], 1, 2),
        jnp.swapaxes(layout_qkv[0], 1, 2),
        text_out_w[0],
        layout_out_w[0],
        loose=range(4),
    )

    def spread(value):
        out = [other_section(value)]
        for k in range(1, pieces):
            out.append(lax.ppermute(out[0], "dp", [(i, (i + k) % pages) for i in range(pages)]))
        return out

    attn_got = spread(piece)
    xs = call(part(inputs_body, n), [((cb, width), BF)] * n, "inputs")(
        ids, text_in, jnp.swapaxes(layout_in, 1, 2), loose=(0, 1)
    )
    mates = [chip_swap(x) for x in xs]
    prm_own = call(params_body, [((16, width), F32)], "params")(
        ids,
        text_gains[0],
        text_biases[0],
        text_ffn_bias,
        text_qv_bias[0],
        layout_gains[0],
        layout_biases[0],
        layout_ffn_bias,
        layout_qv_bias[0],
        loose=range(8),
    )[0]
    prm_oth = other_section(prm_own)
    x_own = [jnp.concatenate([x, m], axis=0) for x, m in zip(xs, mates)]
    *cots, segr, segc = call(
        part(side_body, n),
        [((cb, width + 64), BF)] * n + [((1, rows), jnp.int32), ((rows, TILE), F32)],
        "side",
    )(
        ids,
        text_cot,
        jnp.swapaxes(layout_cot, 1, 2),
        token_mask,
        box_mask,
        segments.reshape(micro, 4, mine),
        loose=range(5),
    )

    cot_mates = [chip_swap(c) for c in cots]
    lead = call(first_half_body, [((arows // 2, d), BF)], "attn_lead", us=0.6)(
        ids, attn_own, after=attn_got[0:1]
    )[0]
    attn_direct = other_section(lead)
    frows = 2 * d + 2 * dl * dl // d
    ffn_own, piece = call(
        part(ffn_send_body, pieces),
        [((frows, d), BF), ((d // pieces, d), BF)],
        "ffn_send",
    )(
        ids, text_ffn_in[0], text_ffn_out[0], layout_ffn_in[0], layout_ffn_out[0],
        loose=range(4), after=[attn_direct, *attn_got],
    )
    ffn_got = spread(piece)
    weights = []

    def attn_weights(j, after=()):
        q_own, prm = call(
            part(pick_attn_body, j, pieces), [((arows, d), BF), ((16, width), F32)], "pick_attn", us=0.8
        )(ids, attn_own, attn_direct, prm_own, prm_oth, *attn_got, after=after)
        wct, woc, bc, fb = call(
            part(pack_body, et, el, f, fl),
            [((3 * wq, width), BF), ((wq, width), BF), ((8, 3 * wq), F32), ((8, fw), F32)],
            "pack",
            us=1.5,
        )(ids, q_own, core_swap(q_own), prm, core_swap(prm))
        return wct, woc, bc, prm, fb

    def ffn_weights(j, after=()):
        w_own = call(part(pick_ffn_body, j, pieces, d), [((frows, d), BF)], "pick_ffn", us=1)(
            ids, ffn_own, ffn_direct, *ffn_got, after=after
        )[0]
        w_mate = core_swap(w_own)
        w1l, w2l = call(
            part(unfold_body, d), [((dl, 2 * fl), BF), ((2 * fl, dl), BF)], "unfold", us=0.6
        )(ids, w_own, w_mate)
        return w_own, w_mate, w1l, w2l

    attn_w = attn_weights(0, mates)

    qkv_outs = [((hk, wq), BF), ((hk, 2 * wq), BF)]
    norm_outs = [((hk, width), F32), ((hk, TILE), F32)]
    row_out = ((hk, width), BF)
    mate_out = ((hk, width + f + fl), BF)
    outs = call(part(project_body, n), qkv_outs[0:1] * n + qkv_outs[1:2] * n, "project", us=3)(
        ids, attn_w[0], attn_w[2], *x_own
    )
    q, kv = outs[0:n], outs[n:]
    peer = [core_swap(v) for v in kv]

    back_outs = [((hk, width), F32), ((hk, width), BF), ((8, width), F32)]
    ffn_lead = call(part(ffn_lead_body, d), [((frows - d, d), BF)], "ffn_lead", us=0.6)(
        ids, ffn_own, after=ffn_got[0:1]
    )[0]
    ffn_direct = other_section(ffn_lead)
    kept = []
    hidden = []
    for j in range(sections):
        wct, woc, bc, prm, fb = attn_w
        *s, oc, lse, xa = call(
            part(attn_body, n),
            [row_out] * n + [((own, wq), BF), ((8, own), F32), ((own, up_to_tile(width + wq // 2)), BF)],
            "attn",
            us=4,
            hbm=(n + 2,),
        )(ids, segc, segr, woc, *x_own, *q, *kv, *peer, after=[*cot_mates, *ffn_got[1:]] if j == 0 else [])
        r = [chip_swap(v) for v in s]
        ffn_w = ffn_weights(j)
        weights.append((wct, woc, bc, prm, fb, ffn_w))
        s2, n1, inv1, xb, act, slope, xf = ([] for _ in range(7))
        for k in range(n):
            outs = call(
                ffn_body,
                [row_out] + norm_outs + [row_out] + [((hk, fw), BF)] * 2 + [mate_out],
                "ffn",
                us=2,
                hbm=(6,),
            )(ids, s[k], r[k], x_own[k], prm, fb, *ffn_w)
            for got, value in zip((s2, n1, inv1, xb, act, slope, xf), outs):
                got.append(value)
        r2 = [chip_swap(v) for v in s2]
        kept.append((x_own, q, kv, peer, oc, lse, n1, inv1, xb, act, slope, xa, xf))
        y, n2, inv2 = ([] for _ in range(3))
        if j + 1 < sections:
            attn_w = attn_weights(j + 1)
            q, kv, peer = [], [], []
            for k in range(n):
                outs = call(
                    part(norm_project_body, d), norm_outs + [row_out] + qkv_outs, "norm_project", us=2
                )(
                    ids, s2[k], r2[k], n1[k], prm, attn_w[0], attn_w[2],
                )
                for got, value in zip((n2, inv2, y, q, kv), outs):
                    got.append(value)
                peer.append(core_swap(kv[k]))
            kept[j] = kept[j] + (n2, inv2)
            x_own = y
        else:
            dh2, dh2b, small2, dpre, s1, xt = ([] for _ in range(6))
            for k in range(n):
                outs = call(
                    turn_body,
                    [row_out] + back_outs + [((hk, fw), BF), row_out, mate_out],
                    "turn",
                    tuple(pltpu.VMEM(shape, dtype) for shape, dtype in norm_outs),
                    us=4,
                )(
                    ids, s2[k], r2[k], n1[k], prm, cots[k], cot_mates[k], slope[k], *ffn_w,
                )
                for got, value in zip((y, dh2, dh2b, small2, dpre, s1, xt), outs):
                    got.append(value)
        hidden.append(y)

    tr = d // (2 * pages)
    ll = dl // (2 * pages)
    grows = tr + (8 if ll % 8 == 0 else ll)

    def grad_outs(count):
        return [((count * pages * grows, d), BF)] * 2 + [((8, width), F32)]

    def over_pages(keep, got):
        value = call(add_body, [(keep.shape, BF)], "add", hbm=True)(ids, keep, got)[0]
        return lax.psum_scatter(value, "dp", scatter_dimension=0, tiled=True)

    def over_pages_now(keep, got):
        if pages > 4:
            return over_pages(keep, got)
        outs = call(part(spread_body, pages), [((grows, d), BF)] * pages, "spread", us=0.7)(
            ids, keep, got
        )
        far = [
            lax.ppermute(outs[k], "dp", [(i, (i + k) % pages) for i in range(pages)])
            for k in range(1, pages)
        ]
        return outs[0], far

    ffn_grad = call(part(ffn_grad_body, d, f, fl, n, pages), grad_outs(2), "ffn_grad", us=5, vmem=16)
    attn_grad = call(part(attn_grad_body, d, n, pages), grad_outs(1), "attn_grad", us=4)
    input_grads = [None] * sections
    small_sums = [None] * sections
    for j in reversed(range(sections)):
        x_own, q, kv, peer, oc, lse, n1, inv1, xb, act, slope, xa, xf = kept[j][0:13]
        wct, woc, bc, prm, fb, ffn_w = weights[j]
        if j + 1 < sections:
            n2, inv2 = kept[j][13:]
            dh2, dh2b, small2, dpre, dxin, s1, xt = ([] for _ in range(7))
            for k in range(n):
                outs = call(
                    back_next_body,
                    [row_out] + back_outs + [((hk, fw), BF), row_out, mate_out],
                    "back_next",
                    us=3,
                )(ids, dh[k], s[k], r[k], n2[k], inv2[k], prm, slope[k], *ffn_w)
                for got, value in zip((dxin, dh2, dh2b, small2, dpre, s1, xt), outs):
                    got.append(value)
            input_grads[j + 1] = dxin
            ffn_before = ffn_pair
        r1 = [chip_swap(v) for v in s1]
        keep, send, hsum = ffn_grad(
            ids, *dh2b, *act, *xb, *dpre, *[core_swap(v) for v in xf], *[core_swap(v) for v in xt]
        )
        ffn_pair = (keep, other_section(send))
        if j == 0:
            ffn_up = over_pages(*ffn_before)
        dh, dhb, small1, dq = ([] for _ in range(4))
        dkv = []
        for k in range(n):
            outs = call(
                part(attn_back_body, k, n, d),
                back_outs
                + [((hk, wq), BF)]
                + (
                    [((rows, 2 * wq), F32)]
                    if k + 1 < n
                    else [((own, 2 * wq), F32)] + [((hk, 2 * wq), BF)] * n
                ),
                "attn_back",
                us=5,
            )(
                ids, dh2[k], s1[k], r1[k], n1[k], inv1[k], prm, segc, segr, woc, lse,
                q[k], *kv, *peer, *dkv,
            )
            for got, value in zip((dh, dhb, small1, dq), outs):
                got.append(value)
            dkv = outs[4:]
        far = [core_swap(v) for v in dkv[1:]]
        if j == 0:
            attn_up = over_pages(*attn_pair)
        s, dkvs, xd = [], [], []
        for k in range(n):
            a, b, c = call(
                part(dx_body, k), [row_out, ((hk, 2 * wq), BF), ((hk, 3 * wq // 2), BF)], "dx", us=1.4
            )(ids, dq[k], dkv[0], far[k], wct)
            s.append(a)
            dkvs.append(b)
            xd.append(c)
        r = [chip_swap(v) for v in s]
        keep, send, hq = attn_grad(
            ids, *x_own, *dhb, *dq, *dkvs, *[core_swap(v) for v in dhb], *[core_swap(v) for v in xd], oc, core_swap(xa)
        )
        attn_pair = (keep, other_section(send))
        small_sums[j] = call(part(smalls_body, n), [((8, width), F32)], "smalls", us=0.6)(
            ids, *small1, *small2, hsum, hq
        )[0]
    lasts = []
    for k in range(n):
        lasts.append(
            call(back_last_body, [row_out], "back_last", us=0.6)(ids, dh[k], s[k], r[k])[0]
        )
    input_grads[0] = lasts

    def collect(layers):
        parts = layers[0] + layers[1]
        away = call(part(away_body, n), [((mine_rows, width), BF)], "away", us=0.6)(ids, *parts)[0]
        return parts, other_section(away)

    def both(parts, got):
        text, lay = call(
            part(both_body, n, d),
            [((micro, mine_rows, d), BF), ((micro, dl, mine_rows), BF)],
            "both",
            hbm=True,
        )(ids, *parts, got)
        return text[None], jnp.swapaxes(lay, 1, 2)[None]

    ing = collect(input_grads)
    hid = collect(hidden)
    small_away = call(swap_body, [((8, width), F32)], "swap", us=0.6)(ids, *small_sums)[0]
    small_got = other_section(small_away)
    ffn_last = over_pages(*ffn_pair)
    spreads = over_pages_now(*attn_pair)
    ing_t, ing_l = both(*ing)
    hid_t, hid_l = both(*hid)
    if pages > 4:
        attn_last = spreads
    else:
        attn_last = call(gather_body, [((grows, d), BF)], "gather", us=0.7)(ids, spreads[0], *spreads[1])[0]

    def away_half(a, b, loose):
        away = call(swap_body, [(a.shape, BF)], "swap", us=0.6)(ids, a, b, loose=loose)[0]
        return a, b, other_section(away)

    rs = (1,) if pages <= 4 else (0, 1)
    attn_parts = away_half(attn_last, attn_up, rs)
    ffn_parts = away_half(ffn_last, ffn_up, (0, 1))
    g_qkv, g_out, g_lqkv, g_lout = call(
        part(proj_body, tr, ll),
        [((3, 2 * tr, et), F32), ((et, 2 * tr), F32), ((3, 2 * ll, el), F32), ((el, 2 * ll), F32)],
        "proj",
        hbm=True,
    )(ids, *attn_parts, loose=rs)
    g2, lg2, g1, lg1 = call(
        part(matrices_body, tr, ll),
        [((2 * tr, f), F32), ((2 * ll, fl), F32)] * 2,
        "matrices",
        hbm=True,
    )(ids, *ffn_parts, loose=(0, 1))

    total = jnp.where(section == 0, small_sums[0], small_sums[1]) + small_got
    bit = 1
    while bit < pages:
        total = total + swap(total, "dp", bit)
        bit *= 2
    shared = total[0:6]
    shared = shared + core_swap(shared)
    shared = shared + chip_swap(shared)
    qv = total[7, 0 : 3 * et].reshape(3, et)
    lqv = total[7, d : d + 3 * el].reshape(3, el)
    return (
        hid_t,
        hid_l,
        ing_t,
        ing_l,
        g_qkv[None],
        jnp.stack([qv[0], qv[2]])[None],
        g_out[None],
        g1[None],
        total[6:7, 0:f],
        g2.T[None],
        shared[None, 0:2, 0:d],
        shared[None, 2:6, 0:d],
        g_lqkv[None],
        jnp.stack([lqv[0], lqv[2]])[None],
        g_lout[None],
        lg1[None],
        total[6:7, f:fw],
        lg2.T[None],
        shared[None, 0:2, d:],
        shared[None, 2:6, d:],
    )


def solution(mesh):
    in_specs = (
        P(None, ("dp", "tensor"), None),
        P(None, ("dp", "tensor"), None),
        P(None, ("dp", "tensor"), None),
        P(None, ("dp", "tensor"), None),
        P(None, ("dp", "tensor")),
        P(None, ("dp", "tensor")),
        P(None, "dp", None),
        P("section", None, None, "tensor"),
        P("section", None, "tensor"),
        P("section", "tensor", None),
        P("section", None, "tensor"),
        P("section", "tensor"),
        P("section", "tensor", None),
        P("section", None, None),
        P("section", None, None),
        P("section", None, None, "tensor"),
        P("section", None, "tensor"),
        P("section", "tensor", None),
        P("section", None, "tensor"),
        P("section", "tensor"),
        P("section", "tensor", None),
        P("section", None, None),
        P("section", None, None),
    )
    out_specs = (
        P("section", None, ("dp", "tensor"), None),
        P("section", None, ("dp", "tensor"), None),
        P("section", None, ("dp", "tensor"), None),
        P("section", None, ("dp", "tensor"), None),
        P("section", None, "dp", "tensor"),
        P("section", None, "tensor"),
        P("section", "tensor", "dp"),
        P("section", "dp", "tensor"),
        P("section", "tensor"),
        P("section", "tensor", "dp"),
        P("section", None, None),
        P("section", None, None),
        P("section", None, "dp", "tensor"),
        P("section", None, "tensor"),
        P("section", "tensor", "dp"),
        P("section", "dp", "tensor"),
        P("section", "tensor"),
        P("section", "tensor", "dp"),
        P("section", None, None),
        P("section", None, None),
    )
    return jax.shard_map(
        per_device, mesh=mesh, in_specs=in_specs, out_specs=out_specs, check_vma=False
    )
```

```python
import functools

import jax
import jax.numpy as jnp
from jax import lax
from jax.experimental import pallas as pl
from jax.experimental.pallas import tpu as pltpu
from jax.sharding import PartitionSpec as P

HEAD = 64
LHEAD = 16
TILE = 128
CHUNKS = 2

EPS = 1e-05
MASKED = -1000000000.0
BF = jnp.bfloat16
F32 = jnp.float32

NT = (((1,), (1,)), ((), ()))
TN = (((0,), (0,)), ((), ()))
NN = (((1,), (0,)), ((), ()))


def mm(a, b, dims=NN):
    return lax.dot_general(a, b, dims, preferred_element_type=F32)


def call(body, outs, name, scratch=(), us=2, hbm=(), vmem=10):
    def run(turn, *args, loose=(), after=()):
        kept = 1 + len(args)
        extra = [turn.token] if turn.token is not None else []
        extra += list(after)

        def inner(*refs):
            given = refs[kept + len(extra) :]
            given[len(outs)][...] = jnp.zeros_like(given[len(outs)])
            body(*refs[0:kept], *given[0 : len(outs)], *given[len(outs) + 1 :])

        placed = [
            pltpu.with_memory_space_constraint(a, pltpu.HBM if i in loose else pltpu.VMEM)
            for i, a in enumerate(list(args) + extra)
        ]
        *results, turn.token = pl.pallas_call(
            inner,
            out_shape=[
                (jax.ShapeDtypeStruct if hbm is True or i in hbm else pltpu.VMEM)(shape, dtype)
                for i, (shape, dtype) in enumerate(outs)
            ]
            + [pltpu.VMEM((8, TILE), F32)],
            in_specs=[pl.BlockSpec(memory_space=pltpu.SMEM)]
            + [pl.BlockSpec(memory_space=pltpu.VMEM)] * len(placed),
            scratch_shapes=list(scratch),
            name=name,
            cost_estimate=pl.CostEstimate(flops=int(us * 10**8), transcendentals=0, bytes_accessed=0),
            compiler_params=pltpu.CompilerParams(vmem_limit_bytes=vmem * 1024 * 1024),
        )(turn.ids, *placed)
        return results

    return run


class Turn:
    def __init__(self, ids):
        self.ids = ids
        self.token = None


def up_to_tile(lanes):
    return -(-lanes // TILE) * TILE


def cat(refs, a0=None, a1=None):
    return jnp.concatenate([ref[:, a0:a1] for ref in refs], axis=0)


def attn_send_body(pieces, ids, qt, ql, ot, ol, full, piece):
    et, d = qt.shape[1:]
    el, dl = ql.shape[1:]
    full[3 * et :, :] = jnp.zeros_like(full[3 * et :, :])
    for c in range(3):
        full[c * et : (c + 1) * et, :] = qt[c]
        full[3 * et : 3 * et + el, c * dl : (c + 1) * dl] = ql[c]
    at = 3 * et + el
    full[at : at + et, :] = ot[...]
    for h in range(el // LHEAD):
        full[at + et : at + et + LHEAD, h * dl : (h + 1) * dl] = ol[h * LHEAD : (h + 1) * LHEAD, :]
    half = full.shape[0] // 2
    size = piece.shape[0]
    spot = ids[2] if pieces > 1 else 0
    piece[...] = full[pl.ds(pl.multiple_of(half + spot * size, 8), size), :]


def first_half_body(ids, full, direct):
    direct[...] = full[0 : direct.shape[0], :]


def ffn_lead_body(d, ids, full, direct):
    half = d // 2
    direct[0:half, :] = full[0:half, :]
    direct[half:d, :] = full[d : d + half, :]
    direct[d:, :] = full[2 * d :, :]


def ffn_send_body(pieces, ids, w1, w2, w1l, w2l, full, piece):
    d, f = w1.shape
    dl = w1l.shape[0]
    deep = dl * dl // d
    full[0:d, :] = w1[...]
    full[d : 2 * d, :] = w2[...]
    for g in range(d // dl):
        full[2 * d : 2 * d + deep, g * dl : (g + 1) * dl] = w1l[g * deep : (g + 1) * deep, :]
        full[2 * d + deep :, g * dl : (g + 1) * dl] = w2l[g * deep : (g + 1) * deep, :]
    half = d // 2
    size = piece.shape[0] // 2
    at = pl.multiple_of(half + (ids[2] if pieces > 1 else 0) * size, 8)
    piece[0:size, :] = w1[pl.ds(at, size), :]
    piece[size:, :] = w2[pl.ds(at, size), :]


def inputs_body(ids, tin, lin, out):
    s = ids[0]
    d = tin.shape[2]
    out[:, 0:d] = tin[s]
    out[:, d:] = lin[s].T


def side_body(chunks, ids, tcot, lcot, tmask, bmask, seg, cot, segr, segc):
    s = ids[0]
    mine, d = tcot.shape[1:]
    width = d + lcot.shape[1]
    rows = mine // chunks
    wt = (0.25 + tmask[pl.ds(s, 1), :].astype(F32)).astype(BF).astype(F32)
    wb = (0.25 + bmask[pl.ds(s, 1), :].astype(F32)).astype(BF).astype(F32)
    cot[:, 0:d] = tcot[s]
    cot[:, d:width] = lcot[s].T
    cot[:, width : width + 32] = jnp.broadcast_to(wt, (TILE, mine)).T[:, 0:32].astype(BF)
    cot[:, width + 32 : width + 64] = jnp.broadcast_to(wb, (TILE, mine)).T[:, 0:32].astype(BF)
    at = 0
    for first in (0, 1):
        for k in range(chunks):
            for step in (first, first ^ 2):
                block = seg[s, pl.ds(ids[1] ^ step, 1), k * rows : (k + 1) * rows]
                segr[0:1, at : at + rows] = block
                at += rows
    segc[...] = jnp.broadcast_to(segr[...].astype(F32), (TILE, at)).T


def params_body(ids, tg, tb, tf, tq, lg, lb, lf, lq, prm):
    d = tg.shape[1]
    prm[...] = jnp.zeros_like(prm)
    for a, gains, biases, hidden, qv in ((0, tg, tb, tf, tq), (d, lg, lb, lf, lq)):
        prm[0:2, a : a + gains.shape[1]] = gains[...]
        prm[2:6, a : a + gains.shape[1]] = biases[...]
        prm[6:7, a : a + hidden.shape[1]] = hidden[...]
        prm[7:9, a : a + qv.shape[1]] = qv[...]


def assemble(full, base, rows, direct, got, ids, at, size):
    half = rows // 2
    full[base : base + half, :] = direct
    n = len(got)
    for k in range(n):
        place = base + half + lax.rem(ids[2] + (n - k), n) * size
        full[pl.ds(pl.multiple_of(place, 8), size), :] = got[k][at : at + size, :]


def pick_attn_body(layer, pieces, ids, own, direct, prm_own, prm_oth, *refs):
    got = refs[0:pieces]
    out, prm = refs[pieces:]

    @pl.when(ids[0] == layer)
    def _():
        out[...] = own[...]
        prm[...] = prm_own[...]

    @pl.when(ids[0] != layer)
    def _():
        assemble(out, 0, out.shape[0], direct[...], got, ids, 0, got[0].shape[0])
        prm[...] = prm_oth[...]


def pick_ffn_body(layer, pieces, d, ids, own, direct, *refs):
    got = refs[0:pieces]
    out = refs[pieces]

    @pl.when(ids[0] == layer)
    def _():
        out[...] = own[...]

    @pl.when(ids[0] != layer)
    def _():
        size = got[0].shape[0] // 2
        half = d // 2
        assemble(out, 0, d, direct[0:half, :], got, ids, 0, size)
        assemble(out, d, d, direct[half:d, :], got, ids, size, size)
        out[2 * d :, :] = direct[d:, :]


def unfold_body(d, ids, own, mate, w1l, w2l):
    dl = w1l.shape[0]
    fl = w1l.shape[1] // 2
    deep = dl * dl // d
    for side, ref in ((0, own), (1, mate)):
        for g in range(d // dl):
            a = 2 * d
            w1l[g * deep : (g + 1) * deep, side * fl : (side + 1) * fl] = ref[
                a : a + deep, g * dl : (g + 1) * dl
            ]
            w2l[side * fl + g * deep : side * fl + (g + 1) * deep, :] = ref[
                a + deep : a + 2 * deep, g * dl : (g + 1) * dl
            ]


def pack_body(et, el, f, fl, ids, q0, q1, prm0, prm1, wct, woc, bc, fb):
    d = q0.shape[1]
    dl = wct.shape[1] - d
    hs = et // HEAD
    heads = 2 * hs
    wct[...] = jnp.zeros_like(wct)
    woc[...] = jnp.zeros_like(woc)
    bc[...] = jnp.zeros_like(bc)
    at = 3 * et + el
    for side, q, prm in ((0, q0, prm0), (1, q1, prm1)):
        for h in range(hs):
            i = side * hs + h
            for c in range(3):
                row = (c * heads + i) * TILE
                wt = q[c * et + h * HEAD : c * et + (h + 1) * HEAD, :]
                wl = q[3 * et + h * LHEAD : 3 * et + (h + 1) * LHEAD, c * dl : (c + 1) * dl]
                if c == 0:
                    wt = (wt.astype(F32) * HEAD**-0.5).astype(BF)
                    wl = (wl.astype(F32) * LHEAD**-0.5).astype(BF)
                wct[row : row + HEAD, 0:d] = wt
                wct[row + HEAD : row + HEAD + LHEAD, d:] = wl
            row = i * TILE
            woc[row : row + HEAD, 0:d] = q[at + h * HEAD : at + (h + 1) * HEAD, :]
            woc[row + HEAD : row + HEAD + LHEAD, d:] = q[
                at + et : at + et + LHEAD, h * dl : (h + 1) * dl
            ]
            for p, c, st, sl in ((7, 0, HEAD**-0.5, LHEAD**-0.5), (8, 2, 1.0, 1.0)):
                col = (c * heads + i) * TILE
                bc[0:1, col : col + HEAD] = prm[p : p + 1, h * HEAD : (h + 1) * HEAD] * st
                bc[0:1, col + HEAD : col + HEAD + LHEAD] = (
                    prm[p : p + 1, d + h * LHEAD : d + (h + 1) * LHEAD] * sl
                )
        fb[0:1, side * f : (side + 1) * f] = prm[6:7, 0:f]
        fb[0:1, 2 * f + side * fl : 2 * f + (side + 1) * fl] = prm[6:7, d : d + fl]


def gelu_pair(pre):
    phi = 0.5 * (1.0 + lax.erf(pre * (0.5**0.5)))
    slope = phi + pre * (jnp.exp(-0.5 * pre * pre) * 0.3989422804014327)
    return pre * phi, slope


def crossed(s, r, chunks=1):
    n = s.shape[0] // (2 * chunks)
    parts = []
    for k in range(chunks):
        a, b, c = 2 * k * n, (2 * k + 1) * n, 2 * (k + 1) * n
        parts.append(s[a:b, :].astype(F32) + r[b:c, :].astype(F32))
        parts.append(s[b:c, :].astype(F32) + r[a:b, :].astype(F32))
    return jnp.concatenate(parts, axis=0)


def norm(h, prm, gain_row, shift_row, d, normed, inv):
    ivs, outs = [], []
    for a0, a1 in ((0, d), (d, h.shape[1])):
        x = h[:, a0:a1]
        centred = x - jnp.mean(x, axis=-1, keepdims=True)
        iv = lax.rsqrt(jnp.mean(centred * centred, axis=-1, keepdims=True) + EPS)
        n = centred * iv
        normed[:, a0:a1] = n
        outs.append(n * prm[gain_row : gain_row + 1, a0:a1] + prm[shift_row : shift_row + 1, a0:a1])
        ivs.append(iv)
    lane = lax.broadcasted_iota(jnp.int32, inv.shape, 1)
    inv[...] = jnp.where(lane < HEAD, ivs[0], ivs[1])
    return outs


def project(x, wct, bc, q, kv):
    split = q.shape[1]
    q[...] = (mm(x, wct[0:split, :], NT) + bc[0:1, 0:split]).astype(BF)
    kv[...] = (mm(x, wct[split:, :], NT) + bc[0:1, split:]).astype(BF)


def project_body(n, ids, wct, bc, *refs):
    x, far = refs[0][...], refs[1][...]
    refs = (None,) * n + refs[2:]
    split = refs[n].shape[1]
    half = split // 2
    rows = refs[n].shape[0]
    kv = (mm(far, wct[split:, :], NT) + bc[0:1, split:]).astype(BF)
    for k in range(n):
        part = kv[k * rows : (k + 1) * rows]
        for i, a in enumerate((half, 0, split + half, split)):
            refs[3 * n + k][:, i * half : (i + 1) * half] = part[:, a : a + half]
    q = (mm(x, wct[0:split, :], NT) + bc[0:1, 0:split]).astype(BF)
    kv = (mm(x, wct[split:, :], NT) + bc[0:1, split:]).astype(BF)
    for k in range(n):
        refs[n + k][...] = q[k * rows : (k + 1) * rows]
        refs[2 * n + k][...] = kv[k * rows : (k + 1) * rows]


def heads_columns(own, peer, i, heads, value):
    base = heads * TILE if value else 0
    a = base + i * TILE
    b = base + (i + heads // 2) % heads * TILE
    return jnp.concatenate([ref[:, a : a + TILE] for ref in own] + [ref[:, b : b + TILE] for ref in peer], axis=0)


def same_doc(segc, segr, q0, n):
    seg = segc[...]
    if n > TILE:
        seg = jnp.concatenate([seg] * (n // TILE), axis=1)
    return seg == segr[:, q0 : q0 + n].astype(F32)


def attn_body(n, ids, segc, segr, woc, *refs):
    xs, qs, own, peer = (refs[i * n : (i + 1) * n] for i in range(4))
    outs = refs[4 * n : 5 * n]
    oc, lse, sent = refs[5 * n :]
    rows = oc.shape[0]
    heads = oc.shape[1] // TILE
    same = same_doc(segc, segr, 0, rows)
    lse[...] = jnp.zeros_like(lse)
    for h in range(heads):
        key = heads_columns(own, peer, h, heads, False)
        val_t = heads_columns(own, peer, h, heads, True).T
        query = cat(qs, h * TILE, (h + 1) * TILE)
        s = jnp.where(same, mm(key, query, NT), MASKED)
        top = jnp.max(s, axis=0, keepdims=True)
        p = jnp.exp(s - top)
        total = jnp.sum(p, axis=0, keepdims=True)
        o = mm(val_t, p.astype(BF)) / total
        oc[:, h * TILE : (h + 1) * TILE] = o.T.astype(BF)
        lse[h : h + 1, :] = top + jnp.log(total)
    part = mm(oc[...], woc[...]).astype(BF)
    step = rows // n
    width = xs[0].shape[1]
    for k in range(n):
        sent[k * step : (k + 1) * step, 0:width] = xs[k][...]
    half = heads // 2 * TILE
    sent[:, width : width + half] = oc[:, half:]
    if width + half < sent.shape[1]:
        sent[:, width + half :] = jnp.zeros_like(sent[:, width + half :])
    for k in range(n):
        outs[k][...] = part[k * step : (k + 1) * step]


def hidden_parts(own, mate, w1l, w2l):
    f = own.shape[1]
    fl = w1l.shape[1]
    width = w1l.shape[0]
    d = (own.shape[0] * f - width * fl) // (2 * f)
    w1, w2 = slice(0, d), slice(d, d + f)
    return (
        (0, d, 0, f, own.at[w1], own.at[w2]),
        (0, d, f, 2 * f, mate.at[w1], mate.at[w2]),
        (d, d + width, 2 * f, 2 * f + fl, w1l, w2l),
    )


def for_mate(a, b, d, f, fl, sent):
    width = a.shape[1]
    sent[:, 0:width] = a[...]
    sent[:, width : width + f] = b[:, f : 2 * f]
    sent[:, width + f :] = b[:, 2 * f + fl :]


def ffn_body(ids, s, r, x, prm, fb, own, mate, w1l, w2l, out, n1, inv, xb, act, slope, sent):
    d = n1.shape[1] - w1l.shape[0]
    h = crossed(s, r) + x[...].astype(F32) + prm[2:3, :]
    text, lay = norm(h, prm, 0, 3, d, n1, inv)
    xb[:, 0:d] = text.astype(BF)
    xb[:, d:] = lay.astype(BF)
    parts = []
    for a0, a1, f0, f1, w1, w2 in hidden_parts(own, mate, w1l, w2l):
        pre = mm(xb[:, a0:a1], w1[...]) + fb[0:1, f0:f1]
        g, gp = gelu_pair(pre)
        g = g.astype(BF)
        act[:, f0:f1] = g
        slope[:, f0:f1] = gp.astype(BF)
        parts.append(mm(g, w2[...]))
    out[:, 0:d] = (parts[0] + parts[1]).astype(BF)
    out[:, d:] = parts[2].astype(BF)
    for_mate(xb, act, d, own.shape[1], w1l.shape[1] // 2, sent)


def second_norm(d, s, r, n1, prm, n2, inv, y, chunks=1):
    h = n1[...] * prm[0:1, :] + prm[3:4, :] + crossed(s, r, chunks) + prm[4:5, :]
    text, lay = norm(h, prm, 1, 5, d, n2, inv)
    y[:, 0:d] = text.astype(BF)
    y[:, d:] = lay.astype(BF)


def wait_body(ids):
    pass


def norm_project_body(d, ids, s, r, n1, prm, wct, bc, n2, inv, y, q, kv):
    second_norm(d, s, r, n1, prm, n2, inv, y)
    project(y[...], wct, bc, q, kv)


def norm_back(dy, normed, inv, prm, gain_row, d, n, dh, dhb, small):
    small[...] = jnp.zeros_like(small)
    block = dy.shape[0] // (2 * n)

    def total(value):
        return sum(
            jnp.sum(value[2 * k * block : (2 * k + 1) * block], axis=0, keepdims=True) for k in range(n)
        )

    for a0, a1, lane in ((0, d, 0), (d, dy.shape[1], HEAD)):
        up = dy[:, a0:a1]
        x = normed[:, a0:a1]
        scaled = up * prm[gain_row : gain_row + 1, a0:a1]
        inner = (
            scaled
            - jnp.mean(scaled, axis=-1, keepdims=True)
            - x * jnp.mean(scaled * x, axis=-1, keepdims=True)
        )
        g = inner * inv[:, lane : lane + 1]
        dh[:, a0:a1] = g
        dhb[:, a0:a1] = g.astype(BF)
        small[0:1, a0:a1] = total(up * x)
        small[1:2, a0:a1] = total(up)
        small[2:3, a0:a1] = total(g)


def ffn_back(dhb, slopes, own, mate, w1l, w2l, dpre, out, sents):
    d = out.shape[1] - w1l.shape[0]
    f, fl = own.shape[1], w1l.shape[1] // 2
    parts = []
    for a0, a1, f0, f1, w1, w2 in hidden_parts(own, mate, w1l, w2l):
        dact = mm(dhb[:, a0:a1], w2[...], NT)
        dp = (dact * cat(slopes, f0, f1).astype(F32)).astype(BF)
        dpre[:, f0:f1] = dp
        parts.append(mm(dp, w1[...], NT))
    out[:, 0:d] = (parts[0] + parts[1]).astype(BF)
    out[:, d:] = parts[2].astype(BF)
    rows = sents[0].shape[0]
    for k, sent in enumerate(sents):
        a, b = k * rows, (k + 1) * rows
        for_mate(dhb[a:b, :], dpre[a:b, :], d, f, fl, sent)


def turn_body(n, ids, prm, own, mate, w1l, w2l, cot0, cot1, *refs):
    s, r, n1, slopes = (refs[i * n : (i + 1) * n] for i in range(4))
    y, dh, dhb, small, dpre, out = refs[4 * n : 4 * n + 6]
    sents = refs[4 * n + 6 : 5 * n + 6]
    n2, inv = refs[5 * n + 6 :]
    width = n2.shape[1]
    d = width - w1l.shape[0]
    second_norm(d, cat(s), cat(r), cat(n1), prm, n2, inv, y, n)
    parts = []
    step = cot0.shape[0] // n
    for k in range(n):
        for cot in (cot0, cot1):
            c = cot[k * step : (k + 1) * step, :].astype(F32)
            lane = lax.broadcasted_iota(jnp.int32, (c.shape[0], width), 1)
            w = jnp.where(lane < d, c[:, width : width + 1], c[:, width + 32 : width + 33])
            parts.append(c[:, 0:width] * w)
    norm_back(jnp.concatenate(parts, axis=0), n2, inv, prm, 1, d, n, dh, dhb, small)
    ffn_back(dhb, slopes, own, mate, w1l, w2l, dpre, out, sents)


def back_next_body(n, ids, dh_up, s, r, prm, own, mate, w1l, w2l, *refs):
    n2, inv, slopes = (refs[i * n : (i + 1) * n] for i in range(3))
    dxin, dh, dhb, small, dpre, out = refs[3 * n : 3 * n + 6]
    sents = refs[3 * n + 6 :]
    d = dh.shape[1] - w1l.shape[0]
    dx = (dh_up[...] + crossed(s, r, n)).astype(BF)
    dxin[...] = dx
    norm_back(dx.astype(F32), cat(n2), cat(inv), prm, 1, d, n, dh, dhb, small)
    ffn_back(dhb, slopes, own, mate, w1l, w2l, dpre, out, sents)


def attn_back_body(n, d, ids, dh2, s1, r1, prm, segc, segr, woc, lse, *refs):
    n1, inv, qs, own, peer = (refs[i * n : (i + 1) * n] for i in range(5))
    dh, dhb, small, dq, mine = refs[5 * n : 5 * n + 5]
    fars = refs[5 * n + 5 : 6 * n + 5]
    sents = refs[6 * n + 5 :]
    norm_back(dh2[...] + crossed(s1, r1, n), cat(n1), cat(inv), prm, 0, d, n, dh, dhb, small)
    rows = dq.shape[0]
    step = rows // n
    for k, sent in enumerate(sents):
        sent[...] = dhb[k * step : (k + 1) * step, :]
    heads = dq.shape[1] // TILE
    total = 2 * rows
    doc = mm(dhb[...], woc[...], NT).astype(BF)
    same = same_doc(segc, segr, 0, rows)
    text_t = lax.broadcasted_iota(jnp.int32, (total, TILE), 1) < HEAD
    text_q = lax.broadcasted_iota(jnp.int32, (rows, TILE), 1) < HEAD
    for h in range(heads):
        hc = slice(h * TILE, (h + 1) * TILE)
        vc = slice((heads + h) * TILE, (heads + h + 1) * TILE)
        key = heads_columns(own, peer, h, heads, False)
        val = heads_columns(own, peer, h, heads, True)
        zero = jnp.zeros_like(key)
        query = cat(qs, h * TILE, (h + 1) * TILE)
        up = doc[:, hc]
        zero_q = jnp.zeros_like(query)
        s = mm(key, query, NT)
        p = jnp.where(same, jnp.exp(s - lse[h : h + 1, :]), 0.0)
        dp_all = mm(val, up, NT)
        dp_text = mm(val, jnp.where(text_q, up, zero_q), NT)
        ds_all = (p * (dp_all - jnp.sum(dp_all * p, axis=0, keepdims=True))).astype(BF)
        ds_text = (p * (dp_text - jnp.sum(dp_text * p, axis=0, keepdims=True))).astype(BF)
        dval = mm(p.astype(BF), up)
        dkey = mm(ds_text, jnp.where(text_q, query, zero_q)) + mm(ds_all, jnp.where(text_q, zero_q, query))
        dq_t = mm(jnp.where(text_t, key, zero).T, ds_text) + mm(jnp.where(text_t, zero, key).T, ds_all)
        dq[:, hc] = dq_t.T.astype(BF)
        for col, value in ((hc, dkey), (vc, dval)):
            mine[:, col] = value[0:rows]
            for k, far in enumerate(fars):
                far[:, col] = value[rows + k * step : rows + (k + 1) * step].astype(BF)


def dx_body(n, ids, dq, mine, wct, *refs):
    fars = refs[0:n]
    out, dkv = refs[n : n + 2]
    sents = refs[n + 2 :]
    rows, split = dq.shape
    half = split // 2
    far = cat(fars)
    far = jnp.concatenate(
        [far[:, half:split], far[:, 0:half], far[:, split + half :], far[:, split : split + half]], axis=1
    )
    dkv[...] = (mine[...] + far.astype(F32)).astype(BF)
    out[...] = (mm(dq[...], wct[0:split, :]) + mm(dkv[...], wct[split:, :])).astype(BF)
    step = rows // n
    for k, sent in enumerate(sents):
        a, b = k * step, (k + 1) * step
        for i, part in enumerate((dq[a:b, half:], dkv[a:b, half:split], dkv[a:b, split + half :])):
            sent[:, i * half : (i + 1) * half] = part


def back_last_body(n, ids, dh, s, r, dxin):
    dxin[...] = (dh[...] + crossed(s, r, n)).astype(BF)


def put_halves(text, lay, pages, ids, keep, send, i, n):
    tr = text.shape[0] // (2 * pages)
    ll = lay.shape[0] // (2 * pages)
    lanes = lay.shape[1]
    lr = 8 if ll % 8 == 0 else ll
    rows = tr + lr
    blank = keep.shape[1] - ll // lr * lanes

    def put(order):
        for ref, half in zip((keep, send), order):
            for z in range(pages):
                at = (z * n + i) * rows
                a = (2 * z + half) * tr
                ref[at : at + tr, :] = text[a : a + tr]
                for g in range(ll // lr):
                    b = (2 * z + half) * ll + g * lr
                    ref[at + tr : at + rows, g * lanes : (g + 1) * lanes] = lay[b : b + lr]
                if blank:
                    ref[at + tr : at + rows, ref.shape[1] - blank :] = jnp.zeros((lr, blank), ref.dtype)

    @pl.when(ids[0] == 0)
    def _():
        put((0, 1))

    @pl.when(ids[0] != 0)
    def _():
        put((1, 0))


def both_cores(own, mate, parts, at):
    left = jnp.concatenate([jnp.concatenate([ref[:, a:b] for a, b in parts], axis=1) for ref in own], axis=0)
    size = left.shape[1]
    return jnp.concatenate([left] + [ref[:, at : at + size] for ref in mate], axis=0)


def ffn_grad_body(d, f, fl, n, pages, ids, *refs):
    up, dpre = refs[0:1], refs[1:2]
    act, x, sent, sent_up = (refs[2 + i * n : 2 + (i + 1) * n] for i in range(4))
    keep, send, total = refs[2 + 4 * n :]
    width = x[0].shape[1]
    hidden = ((0, f), (2 * f, 2 * f + fl))
    for i, (a, b, a_mate) in enumerate(((up, act, sent_up), (x, dpre, sent))):
        left = both_cores(a, a_mate, ((0, width),), 0)
        right = both_cores(b, (sent, sent_up)[i], hidden, width)
        text = mm(left[:, 0:d], right[:, 0:f], TN).astype(BF)
        lay = mm(left[:, d:], right[:, f:], TN).astype(BF)
        put_halves(text, lay, pages, ids, keep, send, i, 2)
    total[...] = jnp.broadcast_to(jnp.sum(right.astype(F32), axis=0, keepdims=True), total.shape)


def attn_grad_body(d, n, pages, ids, *refs):
    ups, dqs, dkvs = refs[0:1], refs[1:2], refs[2:3]
    xs, ups_mate, sent_up = (refs[3 + i * n : 3 + (i + 1) * n] for i in range(3))
    oc, sent, keep, send, qb = refs[3 + 3 * n :]
    width = xs[0].shape[1]
    half = dqs[0].shape[1] // 2
    hs = half // TILE
    x = both_cores(xs, (sent,), ((0, width),), 0)
    up = both_cores(ups, ups_mate, ((0, width),), 0)
    o = both_cores((oc,), (sent,), ((0, half),), width)
    grads = (
        both_cores(dqs, sent_up, ((0, half),), 0),
        both_cores(dkvs, sent_up, ((0, half),), half),
        both_cores(dkvs, sent_up, ((2 * half, 3 * half),), 2 * half),
    )

    def lanes(value, a, size):
        return [value[:, h * TILE + a : h * TILE + a + size] for h in range(hs)]

    tq = jnp.concatenate([v for g in grads for v in lanes(g, 0, HEAD)], axis=1)
    lq = jnp.concatenate([v for g in grads for v in lanes(g, HEAD, LHEAD)], axis=1)
    to = jnp.concatenate(lanes(o, 0, HEAD), axis=1)
    lo = jnp.concatenate(lanes(o, HEAD, LHEAD), axis=1)
    et, el = hs * HEAD, hs * LHEAD

    def scaled(value, size, width):
        lane = lax.broadcasted_iota(jnp.int32, value.shape, 1)
        return jnp.where(lane < size, value * width**-0.5, value)

    text = jnp.concatenate(
        [scaled(mm(x[:, 0:d], tq, TN), et, HEAD).astype(BF), mm(up[:, 0:d], to, TN).astype(BF)], axis=1
    )
    lay = jnp.concatenate(
        [scaled(mm(x[:, d:], lq, TN), el, LHEAD).astype(BF), mm(up[:, d:], lo, TN).astype(BF)], axis=1
    )
    put_halves(text, lay, pages, ids, keep, send, 0, 1)
    qb[...] = jnp.zeros_like(qb)
    sums = jnp.sum(tq.astype(F32), axis=0, keepdims=True)
    qb[0:1, 0 : 3 * et] = scaled(sums, et, HEAD)
    sums = jnp.sum(lq.astype(F32), axis=0, keepdims=True)
    qb[0:1, d : d + 3 * el] = scaled(sums, el, LHEAD)


def smalls_body(ids, *refs):
    one, two, fb, qb, out = refs
    rows = (one[0:1], two[0:1], one[2:3], one[1:2], two[2:3], two[1:2], fb[0:1, :], qb[0:1, :])
    for i, row in enumerate(rows):
        out[i : i + 1, :] = row


def own_block(refs, rows, n):
    value = cat(refs)
    return jnp.concatenate([value[2 * k * rows : (2 * k + 1) * rows] for k in range(n)], axis=0)


def away_body(n, cut, ids, *refs):
    out = refs[-1]
    rows = out.shape[0] // n

    @pl.when(ids[0] == 0)
    def _():
        out[...] = own_block(refs[cut:-1], rows, n)

    @pl.when(ids[0] != 0)
    def _():
        out[...] = own_block(refs[0:cut], rows, n)


def both_body(n, cut, d, ids, *refs):
    got, text, lay = refs[-3:]
    parts = refs[:-3]
    s = ids[0]
    rows = got.shape[0] // n
    text[1 - s] = got[:, 0:d]
    lay[1 - s] = got[:, d:].astype(F32).T.astype(BF)

    def put(refs):
        mine = own_block(refs, rows, n)
        text[s] = mine[:, 0:d]
        lay[s] = mine[:, d:].astype(F32).T.astype(BF)

    @pl.when(s == 0)
    def _():
        put(parts[0:cut])

    @pl.when(s != 0)
    def _():
        put(parts[cut:])


def add_body(ids, keep, got, out):
    out[...] = (keep[...].astype(F32) + got[...].astype(F32)).astype(BF)


def halve_body(bit, size, ids, a, b, keep, send):
    mine = lax.rem(ids[2] // bit, 2)
    for i in range(keep.shape[0] // size):
        for ref, side in ((keep, mine), (send, 1 - mine)):
            at = pl.ds(pl.multiple_of((2 * i + side) * size, 8), size)
            ref[i * size : (i + 1) * size, :] = (a[at, :].astype(F32) + b[at, :].astype(F32)).astype(BF)


def swap_body(ids, a, b, away):
    @pl.when(ids[0] == 0)
    def _():
        away[...] = b[...]

    @pl.when(ids[0] != 0)
    def _():
        away[...] = a[...]


def own_rows(ids, a, b, got, tr, ll, lanes):
    own = jnp.where(ids[0] == 0, a.astype(F32), b.astype(F32))
    oth = got.astype(F32)
    first = jnp.where(ids[0] == 0, own, oth)
    second = jnp.where(ids[0] == 0, oth, own)
    text = jnp.concatenate([first[0:tr], second[0:tr]], axis=0)
    lay = jnp.concatenate(
        [
            half[tr:, g * lanes : (g + 1) * lanes]
            for half in (first, second)
            for g in range(ll // (first.shape[0] - tr))
        ],
        axis=0,
    )
    return text, lay


def matrices_body(tr, ll, ids, a, b, got, *outs):
    rows = a.shape[0] // (len(outs) // 2)
    for i in range(len(outs) // 2):
        at = slice(i * rows, (i + 1) * rows)
        text, lay = outs[2 * i : 2 * i + 2]
        text[...], lay[...] = own_rows(ids, a[at, :], b[at, :], got[at, :], tr, ll, lay.shape[1])


def proj_body(tr, ll, ids, a, b, got, qkv, out, lqkv, lout):
    et = qkv.shape[2]
    el = lqkv.shape[2]
    t, l = own_rows(ids, a[...], b[...], got[...], tr, ll, 4 * el)
    for c in range(3):
        qkv[c] = t[:, c * et : (c + 1) * et]
        lqkv[c] = l[:, c * el : (c + 1) * el]
    out[...] = t[:, 3 * et :].T
    lout[...] = l[:, 3 * el :].T


def swap(value, axis, bit):
    size = lax.axis_size(axis)
    return lax.ppermute(value, axis, [(i, i ^ bit) for i in range(size)])


def core_swap(value):
    return swap(value, "tensor", 1)


def chip_swap(value):
    return swap(value, "tensor", 2)


def other_section(value):
    return swap(value, "section", 1)


def around(value, axis):
    size = lax.axis_size(axis)
    return lax.ppermute(value, axis, [(i, (i + 1) % size) for i in range(size)])


def per_device(
    text_in,
    layout_in,
    text_cot,
    layout_cot,
    token_mask,
    box_mask,
    segments,
    text_qkv,
    text_qv_bias,
    text_out_w,
    text_ffn_in,
    text_ffn_bias,
    text_ffn_out,
    text_gains,
    text_biases,
    layout_qkv,
    layout_qv_bias,
    layout_out_w,
    layout_ffn_in,
    layout_ffn_bias,
    layout_ffn_out,
    layout_gains,
    layout_biases,
):
    sections = lax.axis_size("section")
    section = lax.axis_index("section")
    pages = lax.axis_size("dp")
    micro, mine, d = text_in.shape
    assert micro == sections == 2 and lax.axis_size("tensor") == 4 and segments.shape[1] == 1
    n = CHUNKS
    dl = layout_in.shape[2]
    width = d + dl
    rows = 4 * mine
    mine_rows = mine
    own = 2 * mine
    cb = mine // n
    hk = 2 * cb
    hs = text_qkv.shape[-1] // HEAD
    heads = 2 * hs
    f = text_ffn_in.shape[-1]
    fl = layout_ffn_in.shape[-1]
    fw = 2 * (f + fl)
    et, el = hs * HEAD, hs * LHEAD
    wq = heads * TILE
    part = functools.partial
    ids = Turn(
        jnp.stack([section, lax.axis_index("tensor"), lax.axis_index("dp")]).astype(jnp.int32)
    )

    pieces = pages if pages <= 4 else 1
    arows = 3 * et + el + et + LHEAD
    attn_own, piece = call(
        part(attn_send_body, pieces),
        [((arows, d), BF), ((arows // 2 // pieces, d), BF)],
        "attn_send",
    )(
        ids,
        jnp.swapaxes(text_qkv[0], 1, 2),
        jnp.swapaxes(layout_qkv[0], 1, 2),
        text_out_w[0],
        layout_out_w[0],
        loose=range(4),
    )

    def spread(value):
        out = [other_section(value)]
        for k in range(1, pieces):
            out.append(lax.ppermute(out[0], "dp", [(i, (i + k) % pages) for i in range(pages)]))
        return out

    attn_got = spread(piece)
    x_mine = call(inputs_body, [((mine, width), BF)], "inputs")(
        ids, text_in, jnp.swapaxes(layout_in, 1, 2), loose=(0, 1)
    )[0]
    x_mate = chip_swap(x_mine)
    prm_own = call(params_body, [((16, width), F32)], "params")(
        ids,
        text_gains[0],
        text_biases[0],
        text_ffn_bias,
        text_qv_bias[0],
        layout_gains[0],
        layout_biases[0],
        layout_ffn_bias,
        layout_qv_bias[0],
        loose=range(8),
    )[0]
    prm_oth = other_section(prm_own)
    x_all = jnp.concatenate(
        [v[k * cb : (k + 1) * cb] for k in range(n) for v in (x_mine, x_mate)], axis=0
    )
    x_own = [x_all[k * hk : (k + 1) * hk] for k in range(n)]
    cot, segr, segc = call(
        part(side_body, n),
        [((mine, width + 64), BF), ((1, rows), jnp.int32), ((rows, TILE), F32)],
        "side",
    )(
        ids,
        text_cot,
        jnp.swapaxes(layout_cot, 1, 2),
        token_mask,
        box_mask,
        segments.reshape(micro, 4, mine),
        loose=range(5),
    )

    x_peer = core_swap(x_all)
    cot_mate = chip_swap(cot)
    lead = call(first_half_body, [((arows // 2, d), BF)], "attn_lead", us=0.6)(
        ids, attn_own, after=attn_got[0:1]
    )[0]
    attn_direct = other_section(lead)
    frows = 2 * d + 2 * dl * dl // d
    ffn_own, piece = call(
        part(ffn_send_body, pieces),
        [((frows, d), BF), ((d // pieces, d), BF)],
        "ffn_send",
    )(
        ids, text_ffn_in[0], text_ffn_out[0], layout_ffn_in[0], layout_ffn_out[0],
        loose=range(4), after=[attn_direct, *attn_got],
    )
    ffn_got = spread(piece)
    weights = []

    def attn_weights(j, after=()):
        q_own, prm = call(
            part(pick_attn_body, j, pieces), [((arows, d), BF), ((16, width), F32)], "pick_attn", us=0.8
        )(ids, attn_own, attn_direct, prm_own, prm_oth, *attn_got, after=after)
        wct, woc, bc, fb = call(
            part(pack_body, et, el, f, fl),
            [((3 * wq, width), BF), ((wq, width), BF), ((8, 3 * wq), F32), ((8, fw), F32)],
            "pack",
            us=1.5,
        )(ids, q_own, core_swap(q_own), prm, core_swap(prm))
        return wct, woc, bc, prm, fb

    def ffn_weights(j, after=()):
        w_own = call(part(pick_ffn_body, j, pieces, d), [((frows, d), BF)], "pick_ffn", us=1)(
            ids, ffn_own, ffn_direct, *ffn_got, after=after
        )[0]
        w_mate = core_swap(w_own)
        w1l, w2l = call(
            part(unfold_body, d), [((dl, 2 * fl), BF), ((2 * fl, dl), BF)], "unfold", us=0.6
        )(ids, w_own, w_mate)
        return w_own, w_mate, w1l, w2l

    attn_w = attn_weights(0, [x_peer])

    qkv_outs = [((hk, wq), BF), ((hk, 2 * wq), BF)]
    norm_outs = [((hk, width), F32), ((hk, TILE), F32)]
    row_out = ((hk, width), BF)
    mate_out = ((hk, width + f + fl), BF)
    ffn_lead = call(part(ffn_lead_body, d), [((frows - d, d), BF)], "ffn_lead", us=0.6)(
        ids, ffn_own, after=ffn_got[0:1]
    )[0]
    ffn_direct = other_section(ffn_lead)
    outs = call(part(project_body, n), qkv_outs[0:1] * n + qkv_outs[1:2] * (2 * n), "project", us=3)(
        ids, attn_w[0], attn_w[2], x_all, x_peer
    )
    q, kv, peer = outs[0:n], outs[n : 2 * n], outs[2 * n :]

    own_row = ((own, width), BF)
    back_outs = [((own, width), F32), own_row, ((8, width), F32)]
    kept = []
    hidden = []
    for j in range(sections):
        wct, woc, bc, prm, fb = attn_w
        *s, oc, lse, xa = call(
            part(attn_body, n),
            [row_out] * n + [((own, wq), BF), ((8, own), F32), ((own, up_to_tile(width + wq // 2)), BF)],
            "attn",
            us=4,
            hbm=(n + 2,),
        )(ids, segc, segr, woc, *x_own, *q, *kv, *peer, after=[cot_mate] if j == 0 else mates_up)
        r = [chip_swap(v) for v in s]
        xa = core_swap(xa)
        attn_next = attn_weights(j + 1) if j + 1 < sections else None
        ffn_w = ffn_weights(j)
        weights.append((wct, woc, bc, prm, fb, ffn_w))
        s2, n1, inv1, xb, act, slope, xf = ([] for _ in range(7))
        for k in range(n):
            outs = call(
                ffn_body,
                [row_out] + norm_outs + [row_out] + [((hk, fw), BF)] * 2 + [mate_out],
                "ffn",
                us=2 if j + 1 < sections else 60,
                hbm=(6,),
            )(ids, s[k], r[k], x_own[k], prm, fb, *ffn_w, after=[xa] if k == n - 1 else [])
            for got, value in zip((s2, n1, inv1, xb, act, slope, xf), outs):
                got.append(value)
        r2 = [chip_swap(v) for v in s2]
        xf = [core_swap(v) for v in xf]
        mates_up = xf
        kept.append((x_own, q, kv, peer, oc, lse, n1, inv1, xb, act, slope, xa, xf))
        y, n2, inv2 = ([] for _ in range(3))
        if j + 1 < sections:
            q, kv, peer = [], [], []
            for k in range(n):
                outs = call(
                    part(norm_project_body, d), norm_outs + [row_out] + qkv_outs, "norm_project", us=2
                )(
                    ids, s2[k], r2[k], n1[k], prm, attn_next[0], attn_next[2],
                )
                for got, value in zip((n2, inv2, y, q, kv), outs):
                    got.append(value)
                peer.append(core_swap(kv[k]))
            kept[j] = kept[j] + (n2, inv2)
            x_own = y
            attn_w = attn_next
        else:
            call(wait_body, [], "wait", us=1)(ids, after=[r2[0], xf[0]])
            last, dh2, dh2b, small2, dpre, s1, *xt = call(
                part(turn_body, n),
                [own_row] + back_outs + [((own, fw), BF), own_row] + [mate_out] * n,
                "turn",
                (pltpu.VMEM((own, width), F32), pltpu.VMEM((own, TILE), F32)),
                us=5,
                vmem=14,
            )(ids, prm, *ffn_w, cot, cot_mate, *s2, *r2, *n1, *slope)
            y = [last]
        hidden.append(y)

    tr = d // (2 * pages)
    ll = dl // (2 * pages)
    grows = tr + (8 if ll % 8 == 0 else ll)

    def grad_outs(count):
        return [((count * pages * grows, d), BF)] * 2 + [((8, width), F32)]

    def over_pages(keep, got):
        value = call(add_body, [(keep.shape, BF)], "add", hbm=True)(ids, keep, got)[0]
        return lax.psum_scatter(value, "dp", scatter_dimension=0, tiled=True)

    class OverPages:
        def __init__(self, keep, got):
            self.a, self.b, self.bit = keep, got, 1
            self.size = keep.shape[0] // pages

        def step(self):
            if pages > 4:
                if self.bit == 1:
                    self.out = over_pages(self.a, self.b)
                    self.bit = pages
            elif self.bit < pages:
                rows = self.a.shape[0] // 2
                self.a, send = call(
                    part(halve_body, self.bit, self.size), [((rows, d), BF)] * 2, "halve", us=0.7
                )(ids, self.a, self.b)
                self.b = swap(send, "dp", self.bit)
                self.bit *= 2
            else:
                self.out = call(add_body, [(self.a.shape, BF)], "add", us=0.7)(ids, self.a, self.b)[0]

    def collect(layers):
        parts = list(layers[0]) + list(layers[1])
        cut = len(layers[0])
        away = call(part(away_body, n, cut), [((mine_rows, width), BF)], "away", us=0.6)(ids, *parts)[0]
        return parts, cut, other_section(away)

    def both(parts, cut, got):
        text, lay = call(
            part(both_body, n, cut, d),
            [((micro, mine_rows, d), BF), ((micro, dl, mine_rows), BF)],
            "both",
            hbm=True,
        )(ids, *parts, got)
        return text[None], jnp.swapaxes(lay, 1, 2)[None]

    ffn_grad = call(part(ffn_grad_body, d, f, fl, n, pages), grad_outs(2), "ffn_grad", us=5, vmem=16)
    attn_grad = call(part(attn_grad_body, d, n, pages), grad_outs(1), "attn_grad", us=4)
    hid = collect(hidden)
    input_grads = [None] * sections
    small_sums = [None] * sections
    for j in reversed(range(sections)):
        x_own, q, kv, peer, oc, lse, n1, inv1, xb, act, slope, xa, xf = kept[j][0:13]
        wct, woc, bc, prm, fb, ffn_w = weights[j]
        if j + 1 < sections:
            n2, inv2 = kept[j][13:]
            dxin, dh2, dh2b, small2, dpre, s1, *xt = call(
                part(back_next_body, n),
                [own_row] + back_outs + [((own, fw), BF), own_row] + [mate_out] * n,
                "back_next",
                us=5,
                vmem=14,
            )(ids, dh, s, r, prm, *ffn_w, *n2, *inv2, *slope)
            input_grads[j + 1] = [dxin]
        r1 = chip_swap(s1)
        if j == 0:
            attn_up = OverPages(*attn_pair)
            attn_up.step()
        keep, send, hsum = ffn_grad(
            ids, dh2b, dpre, *act, *xb, *xf, *[core_swap(v) for v in xt]
        )
        ffn_pair = (keep, other_section(send))
        if j == 0:
            ffn_up.step()
        dh, dhb, small1, dq, mine, *more = call(
            part(attn_back_body, n, d),
            back_outs + [((own, wq), BF), ((own, 2 * wq), F32)] + [((hk, 2 * wq), BF)] * n + [row_out] * n,
            "attn_back",
            us=7,
            vmem=14,
        )(ids, dh2, s1, r1, prm, segc, segr, woc, lse, *n1, *inv1, *q, *kv, *peer)
        far = [core_swap(v) for v in more[0:n]]
        ups = [core_swap(v) for v in more[n:]]
        s, dkv, *xd = call(
            part(dx_body, n),
            [own_row, ((own, 2 * wq), BF)] + [((hk, 3 * wq // 2), BF)] * n,
            "dx",
            us=2.5,
        )(ids, dq, mine, wct, *far)
        r = chip_swap(s)
        keep, send, hq = attn_grad(
            ids, dhb, dq, dkv, *x_own, *ups, *[core_swap(v) for v in xd], oc, xa
        )
        attn_pair = (keep, other_section(send))
        if j:
            ffn_up = OverPages(*ffn_pair)
            ffn_up.step()
        small_sums[j] = call(smalls_body, [((8, width), F32)], "smalls", us=0.6)(
            ids, small1, small2, hsum, hq
        )[0]
    input_grads[0] = call(part(back_last_body, n), [own_row], "back_last", us=0.6)(ids, dh, s, r)

    ing = collect(input_grads)
    attn_up.step()
    ffn_up.step()
    ffn_last = over_pages(*ffn_pair)
    attn_last = OverPages(*attn_pair)
    attn_last.step()
    small_away = call(swap_body, [((8, width), F32)], "swap", us=0.6)(ids, *small_sums)[0]
    small_got = other_section(small_away)
    hid_t, hid_l = both(*hid)
    attn_last.step()
    ing_t, ing_l = both(*ing)
    attn_up.step()
    def away_half(a, b, loose):
        away = call(swap_body, [(a.shape, BF)], "swap", us=0.6)(ids, a, b, loose=loose)[0]
        return a, b, other_section(away)

    rs = (1,) if pages <= 4 else (0, 1)
    rs = () if pages <= 4 else (0, 1)
    ffn_parts = away_half(ffn_last, ffn_up.out, (0,) if pages <= 4 else (0, 1))
    attn_last.step()
    attn_parts = away_half(attn_last.out, attn_up.out, rs)
    g2, lg2, g1, lg1 = call(
        part(matrices_body, tr, ll),
        [((2 * tr, f), F32), ((2 * ll, fl), F32)] * 2,
        "matrices",
        hbm=True,
    )(ids, *ffn_parts, loose=(0,) if pages <= 4 else (0, 1))
    g_qkv, g_out, g_lqkv, g_lout = call(
        part(proj_body, tr, ll),
        [((3, 2 * tr, et), F32), ((et, 2 * tr), F32), ((3, 2 * ll, el), F32), ((el, 2 * ll), F32)],
        "proj",
        hbm=True,
    )(ids, *attn_parts, loose=rs)

    total = jnp.where(section == 0, small_sums[0], small_sums[1]) + small_got
    bit = 1
    while bit < pages:
        total = total + swap(total, "dp", bit)
        bit *= 2
    shared = total[0:6]
    shared = shared + core_swap(shared)
    shared = shared + chip_swap(shared)
    qv = total[7, 0 : 3 * et].reshape(3, et)
    lqv = total[7, d : d + 3 * el].reshape(3, el)
    return (
        hid_t,
        hid_l,
        ing_t,
        ing_l,
        g_qkv[None],
        jnp.stack([qv[0], qv[2]])[None],
        g_out[None],
        g1[None],
        total[6:7, 0:f],
        g2.T[None],
        shared[None, 0:2, 0:d],
        shared[None, 2:6, 0:d],
        g_lqkv[None],
        jnp.stack([lqv[0], lqv[2]])[None],
        g_lout[None],
        lg1[None],
        total[6:7, f:fw],
        lg2.T[None],
        shared[None, 0:2, d:],
        shared[None, 2:6, d:],
    )


def solution(mesh):
    in_specs = (
        P(None, ("dp", "tensor"), None),
        P(None, ("dp", "tensor"), None),
        P(None, ("dp", "tensor"), None),
        P(None, ("dp", "tensor"), None),
        P(None, ("dp", "tensor")),
        P(None, ("dp", "tensor")),
        P(None, "dp", None),
        P("section", None, None, "tensor"),
        P("section", None, "tensor"),
        P("section", "tensor", None),
        P("section", None, "tensor"),
        P("section", "tensor"),
        P("section", "tensor", None),
        P("section", None, None),
        P("section", None, None),
        P("section", None, None, "tensor"),
        P("section", None, "tensor"),
        P("section", "tensor", None),
        P("section", None, "tensor"),
        P("section", "tensor"),
        P("section", "tensor", None),
        P("section", None, None),
        P("section", None, None),
    )
    out_specs = (
        P("section", None, ("dp", "tensor"), None),
        P("section", None, ("dp", "tensor"), None),
        P("section", None, ("dp", "tensor"), None),
        P("section", None, ("dp", "tensor"), None),
        P("section", None, "dp", "tensor"),
        P("section", None, "tensor"),
        P("section", "tensor", "dp"),
        P("section", "dp", "tensor"),
        P("section", "tensor"),
        P("section", "tensor", "dp"),
        P("section", None, None),
        P("section", None, None),
        P("section", None, "dp", "tensor"),
        P("section", None, "tensor"),
        P("section", "tensor", "dp"),
        P("section", "dp", "tensor"),
        P("section", "tensor"),
        P("section", "tensor", "dp"),
        P("section", None, None),
        P("section", None, None),
    )
    return jax.shard_map(
        per_device, mesh=mesh, in_specs=in_specs, out_specs=out_specs, check_vma=False
    )
```

```python
import functools

import jax
import jax.numpy as jnp
from jax import lax
from jax.experimental import pallas as pl
from jax.experimental.pallas import tpu as pltpu
from jax.sharding import PartitionSpec as P

HEAD = 64
LHEAD = 16
TILE = 128
CHUNKS = 2

EPS = 1e-05
MASKED = -1000000000.0
BF = jnp.bfloat16
F32 = jnp.float32

NT = (((1,), (1,)), ((), ()))
TN = (((0,), (0,)), ((), ()))
NN = (((1,), (0,)), ((), ()))


def mm(a, b, dims=NN):
    return lax.dot_general(a, b, dims, preferred_element_type=F32)


def call(body, outs, name, scratch=(), us=2, hbm=(), vmem=10):
    def run(turn, *args, loose=(), after=()):
        kept = 1 + len(args)
        extra = [turn.token] if turn.token is not None else []
        extra += list(after)

        def inner(*refs):
            given = refs[kept + len(extra) :]
            given[len(outs)][...] = jnp.zeros_like(given[len(outs)])
            body(*refs[0:kept], *given[0 : len(outs)], *given[len(outs) + 1 :])

        placed = [
            pltpu.with_memory_space_constraint(a, pltpu.HBM if i in loose else pltpu.VMEM)
            for i, a in enumerate(list(args) + extra)
        ]
        *results, turn.token = pl.pallas_call(
            inner,
            out_shape=[
                (jax.ShapeDtypeStruct if hbm is True or i in hbm else pltpu.VMEM)(shape, dtype)
                for i, (shape, dtype) in enumerate(outs)
            ]
            + [pltpu.VMEM((8, TILE), F32)],
            in_specs=[pl.BlockSpec(memory_space=pltpu.SMEM)]
            + [pl.BlockSpec(memory_space=pltpu.VMEM)] * len(placed),
            scratch_shapes=list(scratch),
            name=name,
            cost_estimate=pl.CostEstimate(flops=int(us * 10**8), transcendentals=0, bytes_accessed=0),
            compiler_params=pltpu.CompilerParams(vmem_limit_bytes=vmem * 1024 * 1024),
        )(turn.ids, *placed)
        return results

    return run


class Turn:
    def __init__(self, ids):
        self.ids = ids
        self.token = None


def up_to_tile(lanes):
    return -(-lanes // TILE) * TILE


def cat(refs, a0=None, a1=None):
    return jnp.concatenate([ref[:, a0:a1] for ref in refs], axis=0)


def attn_send_body(pieces, ids, qt, ql, ot, ol, full, piece):
    et, d = qt.shape[1:]
    el, dl = ql.shape[1:]
    full[3 * et :, :] = jnp.zeros_like(full[3 * et :, :])
    for c in range(3):
        full[c * et : (c + 1) * et, :] = qt[c]
        full[3 * et : 3 * et + el, c * dl : (c + 1) * dl] = ql[c]
    at = 3 * et + el
    full[at : at + et, :] = ot[...]
    for h in range(el // LHEAD):
        full[at + et : at + et + LHEAD, h * dl : (h + 1) * dl] = ol[h * LHEAD : (h + 1) * LHEAD, :]
    half = full.shape[0] // 2
    size = piece.shape[0]
    spot = ids[2] if pieces > 1 else 0
    piece[...] = full[pl.ds(pl.multiple_of(half + spot * size, 8), size), :]


def first_half_body(ids, full, direct):
    direct[...] = full[0 : direct.shape[0], :]


def ffn_lead_body(d, ids, full, direct):
    half = d // 2
    direct[0:half, :] = full[0:half, :]
    direct[half:d, :] = full[d : d + half, :]
    direct[d:, :] = full[2 * d :, :]


def ffn_send_body(pieces, ids, w1, w2, w1l, w2l, full, piece):
    d, f = w1.shape
    dl = w1l.shape[0]
    deep = dl * dl // d
    full[0:d, :] = w1[...]
    full[d : 2 * d, :] = w2[...]
    for g in range(d // dl):
        full[2 * d : 2 * d + deep, g * dl : (g + 1) * dl] = w1l[g * deep : (g + 1) * deep, :]
        full[2 * d + deep :, g * dl : (g + 1) * dl] = w2l[g * deep : (g + 1) * deep, :]
    half = d // 2
    size = piece.shape[0] // 2
    at = pl.multiple_of(half + (ids[2] if pieces > 1 else 0) * size, 8)
    piece[0:size, :] = w1[pl.ds(at, size), :]
    piece[size:, :] = w2[pl.ds(at, size), :]


def inputs_body(ids, tin, lin, out):
    s = ids[0]
    d = tin.shape[2]
    out[:, 0:d] = tin[s]
    out[:, d:] = lin[s].T


def side_body(chunks, ids, tcot, lcot, tmask, bmask, seg, cot, segr, segc):
    s = ids[0]
    mine, d = tcot.shape[1:]
    width = d + lcot.shape[1]
    rows = mine // chunks
    wt = (0.25 + tmask[pl.ds(s, 1), :].astype(F32)).astype(BF).astype(F32)
    wb = (0.25 + bmask[pl.ds(s, 1), :].astype(F32)).astype(BF).astype(F32)
    cot[:, 0:d] = tcot[s]
    cot[:, d:width] = lcot[s].T
    cot[:, width : width + 32] = jnp.broadcast_to(wt, (TILE, mine)).T[:, 0:32].astype(BF)
    cot[:, width + 32 : width + 64] = jnp.broadcast_to(wb, (TILE, mine)).T[:, 0:32].astype(BF)
    at = 0
    for first in (0, 1):
        for k in range(chunks):
            for step in (first, first ^ 2):
                block = seg[s, pl.ds(ids[1] ^ step, 1), k * rows : (k + 1) * rows]
                segr[0:1, at : at + rows] = block
                at += rows
    segc[...] = jnp.broadcast_to(segr[...].astype(F32), (TILE, at)).T


def params_body(ids, tg, tb, tf, tq, lg, lb, lf, lq, prm):
    d = tg.shape[1]
    prm[...] = jnp.zeros_like(prm)
    for a, gains, biases, hidden, qv in ((0, tg, tb, tf, tq), (d, lg, lb, lf, lq)):
        prm[0:2, a : a + gains.shape[1]] = gains[...]
        prm[2:6, a : a + gains.shape[1]] = biases[...]
        prm[6:7, a : a + hidden.shape[1]] = hidden[...]
        prm[7:9, a : a + qv.shape[1]] = qv[...]


def assemble(full, base, rows, direct, got, ids, at, size):
    half = rows // 2
    full[base : base + half, :] = direct
    n = len(got)
    for k in range(n):
        place = base + half + lax.rem(ids[2] + (n - k), n) * size
        full[pl.ds(pl.multiple_of(place, 8), size), :] = got[k][at : at + size, :]


def pick_attn_body(layer, pieces, ids, own, direct, prm_own, prm_oth, *refs):
    got = refs[0:pieces]
    out, prm = refs[pieces:]

    @pl.when(ids[0] == layer)
    def _():
        out[...] = own[...]
        prm[...] = prm_own[...]

    @pl.when(ids[0] != layer)
    def _():
        assemble(out, 0, out.shape[0], direct[...], got, ids, 0, got[0].shape[0])
        prm[...] = prm_oth[...]


def pick_ffn_body(layer, pieces, d, ids, own, direct, *refs):
    got = refs[0:pieces]
    out = refs[pieces]

    @pl.when(ids[0] == layer)
    def _():
        out[...] = own[...]

    @pl.when(ids[0] != layer)
    def _():
        size = got[0].shape[0] // 2
        half = d // 2
        assemble(out, 0, d, direct[0:half, :], got, ids, 0, size)
        assemble(out, d, d, direct[half:d, :], got, ids, size, size)
        out[2 * d :, :] = direct[d:, :]


def unfold_body(d, ids, own, mate, w1l, w2l):
    dl = w1l.shape[0]
    fl = w1l.shape[1] // 2
    deep = dl * dl // d
    for side, ref in ((0, own), (1, mate)):
        for g in range(d // dl):
            a = 2 * d
            w1l[g * deep : (g + 1) * deep, side * fl : (side + 1) * fl] = ref[
                a : a + deep, g * dl : (g + 1) * dl
            ]
            w2l[side * fl + g * deep : side * fl + (g + 1) * deep, :] = ref[
                a + deep : a + 2 * deep, g * dl : (g + 1) * dl
            ]


def pack_body(et, el, f, fl, ids, q0, q1, prm0, prm1, wct, woc, bc, fb):
    d = q0.shape[1]
    dl = wct.shape[1] - d
    hs = et // HEAD
    heads = 2 * hs
    wct[...] = jnp.zeros_like(wct)
    woc[...] = jnp.zeros_like(woc)
    bc[...] = jnp.zeros_like(bc)
    at = 3 * et + el
    for side, q, prm in ((0, q0, prm0), (1, q1, prm1)):
        for h in range(hs):
            i = side * hs + h
            for c in range(3):
                row = (c * heads + i) * TILE
                wt = q[c * et + h * HEAD : c * et + (h + 1) * HEAD, :]
                wl = q[3 * et + h * LHEAD : 3 * et + (h + 1) * LHEAD, c * dl : (c + 1) * dl]
                if c == 0:
                    wt = (wt.astype(F32) * HEAD**-0.5).astype(BF)
                    wl = (wl.astype(F32) * LHEAD**-0.5).astype(BF)
                wct[row : row + HEAD, 0:d] = wt
                wct[row + HEAD : row + HEAD + LHEAD, d:] = wl
            row = i * TILE
            woc[row : row + HEAD, 0:d] = q[at + h * HEAD : at + (h + 1) * HEAD, :]
            woc[row + HEAD : row + HEAD + LHEAD, d:] = q[
                at + et : at + et + LHEAD, h * dl : (h + 1) * dl
            ]
            for p, c, st, sl in ((7, 0, HEAD**-0.5, LHEAD**-0.5), (8, 2, 1.0, 1.0)):
                col = (c * heads + i) * TILE
                bc[0:1, col : col + HEAD] = prm[p : p + 1, h * HEAD : (h + 1) * HEAD] * st
                bc[0:1, col + HEAD : col + HEAD + LHEAD] = (
                    prm[p : p + 1, d + h * LHEAD : d + (h + 1) * LHEAD] * sl
                )
        fb[0:1, side * f : (side + 1) * f] = prm[6:7, 0:f]
        fb[0:1, 2 * f + side * fl : 2 * f + (side + 1) * fl] = prm[6:7, d : d + fl]


def gelu_pair(pre):
    phi = 0.5 * (1.0 + lax.erf(pre * (0.5**0.5)))
    slope = phi + pre * (jnp.exp(-0.5 * pre * pre) * 0.3989422804014327)
    return pre * phi, slope


def crossed(s, r, chunks=1):
    n = s.shape[0] // (2 * chunks)
    parts = []
    for k in range(chunks):
        a, b, c = 2 * k * n, (2 * k + 1) * n, 2 * (k + 1) * n
        parts.append(s[a:b, :].astype(F32) + r[b:c, :].astype(F32))
        parts.append(s[b:c, :].astype(F32) + r[a:b, :].astype(F32))
    return jnp.concatenate(parts, axis=0)


def norm(h, prm, gain_row, shift_row, d, normed, inv):
    ivs, outs = [], []
    for a0, a1 in ((0, d), (d, h.shape[1])):
        x = h[:, a0:a1]
        centred = x - jnp.mean(x, axis=-1, keepdims=True)
        iv = lax.rsqrt(jnp.mean(centred * centred, axis=-1, keepdims=True) + EPS)
        n = centred * iv
        normed[:, a0:a1] = n
        outs.append(n * prm[gain_row : gain_row + 1, a0:a1] + prm[shift_row : shift_row + 1, a0:a1])
        ivs.append(iv)
    lane = lax.broadcasted_iota(jnp.int32, inv.shape, 1)
    inv[...] = jnp.where(lane < HEAD, ivs[0], ivs[1])
    return outs


def project(x, wct, bc, q, kv):
    split = q.shape[1]
    q[...] = (mm(x, wct[0:split, :], NT) + bc[0:1, 0:split]).astype(BF)
    kv[...] = (mm(x, wct[split:, :], NT) + bc[0:1, split:]).astype(BF)


def project_body(n, ids, wct, bc, *refs):
    x, far = refs[0][...], refs[1][...]
    refs = (None,) * n + refs[2:]
    split = refs[n].shape[1]
    half = split // 2
    rows = refs[n].shape[0]
    kv = (mm(far, wct[split:, :], NT) + bc[0:1, split:]).astype(BF)
    for k in range(n):
        part = kv[k * rows : (k + 1) * rows]
        for i, a in enumerate((half, 0, split + half, split)):
            refs[3 * n + k][:, i * half : (i + 1) * half] = part[:, a : a + half]
    q = (mm(x, wct[0:split, :], NT) + bc[0:1, 0:split]).astype(BF)
    kv = (mm(x, wct[split:, :], NT) + bc[0:1, split:]).astype(BF)
    for k in range(n):
        refs[n + k][...] = q[k * rows : (k + 1) * rows]
        refs[2 * n + k][...] = kv[k * rows : (k + 1) * rows]


def heads_columns(own, peer, i, heads, value):
    base = heads * TILE if value else 0
    a = base + i * TILE
    b = base + (i + heads // 2) % heads * TILE
    return jnp.concatenate([ref[:, a : a + TILE] for ref in own] + [ref[:, b : b + TILE] for ref in peer], axis=0)


def same_doc(segc, segr, q0, n):
    seg = segc[...]
    if n > TILE:
        seg = jnp.concatenate([seg] * (n // TILE), axis=1)
    return seg == segr[:, q0 : q0 + n].astype(F32)


def attn_body(n, ids, segc, segr, woc, *refs):
    xs, qs, own, peer = (refs[i * n : (i + 1) * n] for i in range(4))
    outs = refs[4 * n : 5 * n]
    oc, lse, sent = refs[5 * n :]
    rows = oc.shape[0]
    heads = oc.shape[1] // TILE
    same = same_doc(segc, segr, 0, rows)
    lse[...] = jnp.zeros_like(lse)
    for h in range(heads):
        key = heads_columns(own, peer, h, heads, False)
        val_t = heads_columns(own, peer, h, heads, True).T
        query = cat(qs, h * TILE, (h + 1) * TILE)
        s = jnp.where(same, mm(key, query, NT), MASKED)
        top = jnp.max(s, axis=0, keepdims=True)
        p = jnp.exp(s - top)
        total = jnp.sum(p, axis=0, keepdims=True)
        o = mm(val_t, p.astype(BF)) / total
        oc[:, h * TILE : (h + 1) * TILE] = o.T.astype(BF)
        lse[h : h + 1, :] = top + jnp.log(total)
    part = mm(oc[...], woc[...]).astype(BF)
    step = rows // n
    width = xs[0].shape[1]
    for k in range(n):
        sent[k * step : (k + 1) * step, 0:width] = xs[k][...]
    half = heads // 2 * TILE
    sent[:, width : width + half] = oc[:, half:]
    if width + half < sent.shape[1]:
        sent[:, width + half :] = jnp.zeros_like(sent[:, width + half :])
    for k in range(n):
        outs[k][...] = part[k * step : (k + 1) * step]


def hidden_parts(own, mate, w1l, w2l):
    f = own.shape[1]
    fl = w1l.shape[1]
    width = w1l.shape[0]
    d = (own.shape[0] * f - width * fl) // (2 * f)
    w1, w2 = slice(0, d), slice(d, d + f)
    return (
        (0, d, 0, f, own.at[w1], own.at[w2]),
        (0, d, f, 2 * f, mate.at[w1], mate.at[w2]),
        (d, d + width, 2 * f, 2 * f + fl, w1l, w2l),
    )


def for_mate(a, b, d, f, fl, sent):
    width = a.shape[1]
    sent[:, 0:width] = a[...]
    sent[:, width : width + f] = b[:, f : 2 * f]
    sent[:, width + f :] = b[:, 2 * f + fl :]


def ffn_body(ids, s, r, x, prm, fb, own, mate, w1l, w2l, out, n1, inv, xb, act, slope, sent):
    d = n1.shape[1] - w1l.shape[0]
    h = crossed(s, r) + x[...].astype(F32) + prm[2:3, :]
    text, lay = norm(h, prm, 0, 3, d, n1, inv)
    xb[:, 0:d] = text.astype(BF)
    xb[:, d:] = lay.astype(BF)
    parts = []
    for a0, a1, f0, f1, w1, w2 in hidden_parts(own, mate, w1l, w2l):
        pre = mm(xb[:, a0:a1], w1[...]) + fb[0:1, f0:f1]
        g, gp = gelu_pair(pre)
        g = g.astype(BF)
        act[:, f0:f1] = g
        slope[:, f0:f1] = gp.astype(BF)
        parts.append(mm(g, w2[...]))
    out[:, 0:d] = (parts[0] + parts[1]).astype(BF)
    out[:, d:] = parts[2].astype(BF)
    for_mate(xb, act, d, own.shape[1], w1l.shape[1] // 2, sent)


def second_norm(d, s, r, n1, prm, n2, inv, y, chunks=1):
    h = n1[...] * prm[0:1, :] + prm[3:4, :] + crossed(s, r, chunks) + prm[4:5, :]
    text, lay = norm(h, prm, 1, 5, d, n2, inv)
    y[:, 0:d] = text.astype(BF)
    y[:, d:] = lay.astype(BF)


def wait_body(ids):
    pass


def norm_project_body(d, ids, s, r, n1, prm, wct, bc, n2, inv, y, q, kv):
    second_norm(d, s, r, n1, prm, n2, inv, y)
    project(y[...], wct, bc, q, kv)


def norm_back(dy, normed, inv, prm, gain_row, d, n, dh, dhb, small):
    small[...] = jnp.zeros_like(small)
    block = dy.shape[0] // (2 * n)

    def total(value):
        return sum(
            jnp.sum(value[2 * k * block : (2 * k + 1) * block], axis=0, keepdims=True) for k in range(n)
        )

    for a0, a1, lane in ((0, d, 0), (d, dy.shape[1], HEAD)):
        up = dy[:, a0:a1]
        x = normed[:, a0:a1]
        scaled = up * prm[gain_row : gain_row + 1, a0:a1]
        inner = (
            scaled
            - jnp.mean(scaled, axis=-1, keepdims=True)
            - x * jnp.mean(scaled * x, axis=-1, keepdims=True)
        )
        g = inner * inv[:, lane : lane + 1]
        dh[:, a0:a1] = g
        dhb[:, a0:a1] = g.astype(BF)
        small[0:1, a0:a1] = total(up * x)
        small[1:2, a0:a1] = total(up)
        small[2:3, a0:a1] = total(g)


def ffn_back(dhb, slopes, own, mate, w1l, w2l, dpre, out, sents):
    d = out.shape[1] - w1l.shape[0]
    f, fl = own.shape[1], w1l.shape[1] // 2
    parts = []
    for a0, a1, f0, f1, w1, w2 in hidden_parts(own, mate, w1l, w2l):
        dact = mm(dhb[:, a0:a1], w2[...], NT)
        dp = (dact * cat(slopes, f0, f1).astype(F32)).astype(BF)
        dpre[:, f0:f1] = dp
        parts.append(mm(dp, w1[...], NT))
    out[:, 0:d] = (parts[0] + parts[1]).astype(BF)
    out[:, d:] = parts[2].astype(BF)
    rows = sents[0].shape[0]
    for k, sent in enumerate(sents):
        a, b = k * rows, (k + 1) * rows
        for_mate(dhb[a:b, :], dpre[a:b, :], d, f, fl, sent)


def turn_body(n, ids, prm, own, mate, w1l, w2l, cot0, cot1, *refs):
    s, r, n1, slopes = (refs[i * n : (i + 1) * n] for i in range(4))
    y, dh, dhb, small, dpre, out = refs[4 * n : 4 * n + 6]
    sents = refs[4 * n + 6 : 5 * n + 6]
    n2, inv = refs[5 * n + 6 :]
    width = n2.shape[1]
    d = width - w1l.shape[0]
    second_norm(d, cat(s), cat(r), cat(n1), prm, n2, inv, y, n)
    parts = []
    step = cot0.shape[0] // n
    for k in range(n):
        for cot in (cot0, cot1):
            c = cot[k * step : (k + 1) * step, :].astype(F32)
            lane = lax.broadcasted_iota(jnp.int32, (c.shape[0], width), 1)
            w = jnp.where(lane < d, c[:, width : width + 1], c[:, width + 32 : width + 33])
            parts.append(c[:, 0:width] * w)
    norm_back(jnp.concatenate(parts, axis=0), n2, inv, prm, 1, d, n, dh, dhb, small)
    ffn_back(dhb, slopes, own, mate, w1l, w2l, dpre, out, sents)


def back_next_body(n, ids, dh_up, s, r, prm, own, mate, w1l, w2l, *refs):
    n2, inv, slopes = (refs[i * n : (i + 1) * n] for i in range(3))
    dxin, dh, dhb, small, dpre, out = refs[3 * n : 3 * n + 6]
    sents = refs[3 * n + 6 :]
    d = dh.shape[1] - w1l.shape[0]
    dx = (dh_up[...] + crossed(s, r, n)).astype(BF)
    dxin[...] = dx
    norm_back(dx.astype(F32), cat(n2), cat(inv), prm, 1, d, n, dh, dhb, small)
    ffn_back(dhb, slopes, own, mate, w1l, w2l, dpre, out, sents)


def attn_back_body(n, d, ids, dh2, s1, r1, prm, segc, segr, woc, lse, *refs):
    n1, inv, qs, own, peer = (refs[i * n : (i + 1) * n] for i in range(5))
    dh, dhb, small, dq, mine = refs[5 * n : 5 * n + 5]
    fars = refs[5 * n + 5 : 6 * n + 5]
    sents = refs[6 * n + 5 :]
    norm_back(dh2[...] + crossed(s1, r1, n), cat(n1), cat(inv), prm, 0, d, n, dh, dhb, small)
    rows = dq.shape[0]
    step = rows // n
    for k, sent in enumerate(sents):
        sent[...] = dhb[k * step : (k + 1) * step, :]
    heads = dq.shape[1] // TILE
    total = 2 * rows
    doc = mm(dhb[...], woc[...], NT).astype(BF)
    same = same_doc(segc, segr, 0, rows)
    text_t = lax.broadcasted_iota(jnp.int32, (total, TILE), 1) < HEAD
    text_q = lax.broadcasted_iota(jnp.int32, (rows, TILE), 1) < HEAD
    for h in range(heads):
        hc = slice(h * TILE, (h + 1) * TILE)
        vc = slice((heads + h) * TILE, (heads + h + 1) * TILE)
        key = heads_columns(own, peer, h, heads, False)
        val = heads_columns(own, peer, h, heads, True)
        zero = jnp.zeros_like(key)
        query = cat(qs, h * TILE, (h + 1) * TILE)
        up = doc[:, hc]
        zero_q = jnp.zeros_like(query)
        s = mm(key, query, NT)
        p = jnp.where(same, jnp.exp(s - lse[h : h + 1, :]), 0.0)
        dp_all = mm(val, up, NT)
        dp_text = mm(val, jnp.where(text_q, up, zero_q), NT)
        ds_all = (p * (dp_all - jnp.sum(dp_all * p, axis=0, keepdims=True))).astype(BF)
        ds_text = (p * (dp_text - jnp.sum(dp_text * p, axis=0, keepdims=True))).astype(BF)
        dval = mm(p.astype(BF), up)
        dkey = mm(ds_text, jnp.where(text_q, query, zero_q)) + mm(ds_all, jnp.where(text_q, zero_q, query))
        dq_t = mm(jnp.where(text_t, key, zero).T, ds_text) + mm(jnp.where(text_t, zero, key).T, ds_all)
        dq[:, hc] = dq_t.T.astype(BF)
        for col, value in ((hc, dkey), (vc, dval)):
            mine[:, col] = value[0:rows]
            for k, far in enumerate(fars):
                far[:, col] = value[rows + k * step : rows + (k + 1) * step].astype(BF)


def dx_body(n, ids, dq, mine, wct, *refs):
    fars = refs[0:n]
    out, dkv = refs[n : n + 2]
    sents = refs[n + 2 :]
    rows, split = dq.shape
    half = split // 2
    far = cat(fars)
    far = jnp.concatenate(
        [far[:, half:split], far[:, 0:half], far[:, split + half :], far[:, split : split + half]], axis=1
    )
    dkv[...] = (mine[...] + far.astype(F32)).astype(BF)
    out[...] = (mm(dq[...], wct[0:split, :]) + mm(dkv[...], wct[split:, :])).astype(BF)
    step = rows // n
    for k, sent in enumerate(sents):
        a, b = k * step, (k + 1) * step
        for i, part in enumerate((dq[a:b, half:], dkv[a:b, half:split], dkv[a:b, split + half :])):
            sent[:, i * half : (i + 1) * half] = part


def back_last_body(n, ids, dh, s, r, dxin):
    dxin[...] = (dh[...] + crossed(s, r, n)).astype(BF)


def put_halves(text, lay, pages, ids, keep, send, i, n):
    tr = text.shape[0] // (2 * pages)
    ll = lay.shape[0] // (2 * pages)
    lanes = lay.shape[1]
    lr = 8 if ll % 8 == 0 else ll
    rows = tr + lr
    blank = keep.shape[1] - ll // lr * lanes

    def put(order):
        for ref, half in zip((keep, send), order):
            for z in range(pages):
                at = (z * n + i) * rows
                a = (2 * z + half) * tr
                ref[at : at + tr, :] = text[a : a + tr]
                for g in range(ll // lr):
                    b = (2 * z + half) * ll + g * lr
                    ref[at + tr : at + rows, g * lanes : (g + 1) * lanes] = lay[b : b + lr]
                if blank:
                    ref[at + tr : at + rows, ref.shape[1] - blank :] = jnp.zeros((lr, blank), ref.dtype)

    @pl.when(ids[0] == 0)
    def _():
        put((0, 1))

    @pl.when(ids[0] != 0)
    def _():
        put((1, 0))


def both_cores(own, mate, parts, at):
    left = jnp.concatenate([jnp.concatenate([ref[:, a:b] for a, b in parts], axis=1) for ref in own], axis=0)
    size = left.shape[1]
    return jnp.concatenate([left] + [ref[:, at : at + size] for ref in mate], axis=0)


def ffn_grad_body(d, f, fl, n, pages, ids, *refs):
    up, dpre = refs[0:1], refs[1:2]
    act, x, sent, sent_up = (refs[2 + i * n : 2 + (i + 1) * n] for i in range(4))
    keep, send, total = refs[2 + 4 * n :]
    width = x[0].shape[1]
    hidden = ((0, f), (2 * f, 2 * f + fl))
    for i, (a, b, a_mate) in enumerate(((up, act, sent_up), (x, dpre, sent))):
        left = both_cores(a, a_mate, ((0, width),), 0)
        right = both_cores(b, (sent, sent_up)[i], hidden, width)
        text = mm(left[:, 0:d], right[:, 0:f], TN).astype(BF)
        lay = mm(left[:, d:], right[:, f:], TN).astype(BF)
        put_halves(text, lay, pages, ids, keep, send, i, 2)
    total[...] = jnp.broadcast_to(jnp.sum(right.astype(F32), axis=0, keepdims=True), total.shape)


def attn_grad_body(d, n, pages, ids, *refs):
    ups, dqs, dkvs = refs[0:1], refs[1:2], refs[2:3]
    xs, ups_mate, sent_up = (refs[3 + i * n : 3 + (i + 1) * n] for i in range(3))
    oc, sent, keep, send, qb = refs[3 + 3 * n :]
    width = xs[0].shape[1]
    half = dqs[0].shape[1] // 2
    hs = half // TILE
    x = both_cores(xs, (sent,), ((0, width),), 0)
    up = both_cores(ups, ups_mate, ((0, width),), 0)
    o = both_cores((oc,), (sent,), ((0, half),), width)
    grads = (
        both_cores(dqs, sent_up, ((0, half),), 0),
        both_cores(dkvs, sent_up, ((0, half),), half),
        both_cores(dkvs, sent_up, ((2 * half, 3 * half),), 2 * half),
    )

    def lanes(value, a, size):
        return [value[:, h * TILE + a : h * TILE + a + size] for h in range(hs)]

    tq = jnp.concatenate([v for g in grads for v in lanes(g, 0, HEAD)], axis=1)
    lq = jnp.concatenate([v for g in grads for v in lanes(g, HEAD, LHEAD)], axis=1)
    to = jnp.concatenate(lanes(o, 0, HEAD), axis=1)
    lo = jnp.concatenate(lanes(o, HEAD, LHEAD), axis=1)
    et, el = hs * HEAD, hs * LHEAD

    def scaled(value, size, width):
        lane = lax.broadcasted_iota(jnp.int32, value.shape, 1)
        return jnp.where(lane < size, value * width**-0.5, value)

    text = jnp.concatenate(
        [scaled(mm(x[:, 0:d], tq, TN), et, HEAD).astype(BF), mm(up[:, 0:d], to, TN).astype(BF)], axis=1
    )
    lay = jnp.concatenate(
        [scaled(mm(x[:, d:], lq, TN), el, LHEAD).astype(BF), mm(up[:, d:], lo, TN).astype(BF)], axis=1
    )
    put_halves(text, lay, pages, ids, keep, send, 0, 1)
    qb[...] = jnp.zeros_like(qb)
    sums = jnp.sum(tq.astype(F32), axis=0, keepdims=True)
    qb[0:1, 0 : 3 * et] = scaled(sums, et, HEAD)
    sums = jnp.sum(lq.astype(F32), axis=0, keepdims=True)
    qb[0:1, d : d + 3 * el] = scaled(sums, el, LHEAD)


def smalls_body(ids, *refs):
    one, two, fb, qb, out = refs
    rows = (one[0:1], two[0:1], one[2:3], one[1:2], two[2:3], two[1:2], fb[0:1, :], qb[0:1, :])
    for i, row in enumerate(rows):
        out[i : i + 1, :] = row


def own_block(refs, rows, n):
    value = cat(refs)
    return jnp.concatenate([value[2 * k * rows : (2 * k + 1) * rows] for k in range(n)], axis=0)


def away_body(n, cut, ids, *refs):
    out = refs[-1]
    rows = out.shape[0] // n

    @pl.when(ids[0] == 0)
    def _():
        out[...] = own_block(refs[cut:-1], rows, n)

    @pl.when(ids[0] != 0)
    def _():
        out[...] = own_block(refs[0:cut], rows, n)


def both_body(n, cut, d, ids, *refs):
    got, text, lay = refs[-3:]
    parts = refs[:-3]
    s = ids[0]
    rows = got.shape[0] // n
    text[1 - s] = got[:, 0:d]
    lay[1 - s] = got[:, d:].astype(F32).T.astype(BF)

    def put(refs):
        mine = own_block(refs, rows, n)
        text[s] = mine[:, 0:d]
        lay[s] = mine[:, d:].astype(F32).T.astype(BF)

    @pl.when(s == 0)
    def _():
        put(parts[0:cut])

    @pl.when(s != 0)
    def _():
        put(parts[cut:])


def add_body(ids, keep, got, out):
    out[...] = (keep[...].astype(F32) + got[...].astype(F32)).astype(BF)


def halve_body(bit, size, ids, a, b, keep, send):
    mine = lax.rem(ids[2] // bit, 2)
    for i in range(keep.shape[0] // size):
        for ref, side in ((keep, mine), (send, 1 - mine)):
            at = pl.ds(pl.multiple_of((2 * i + side) * size, 8), size)
            ref[i * size : (i + 1) * size, :] = (a[at, :].astype(F32) + b[at, :].astype(F32)).astype(BF)


def swap_body(ids, a, b, away):
    @pl.when(ids[0] == 0)
    def _():
        away[...] = b[...]

    @pl.when(ids[0] != 0)
    def _():
        away[...] = a[...]


def small_halves_body(ids, both, shared, mine, away):
    n = shared.shape[0] // 2

    def put(layer, ref):
        ref[0:n, :] = shared[layer * n : (layer + 1) * n, :]
        ref[n:, :] = both[layer * 8 + n : (layer + 1) * 8, :]

    @pl.when(ids[0] == 0)
    def _():
        put(0, mine)
        put(1, away)

    @pl.when(ids[0] != 0)
    def _():
        put(1, mine)
        put(0, away)


def own_rows(ids, a, b, got, tr, ll, lanes):
    own = jnp.where(ids[0] == 0, a.astype(F32), b.astype(F32))
    oth = got.astype(F32)
    first = jnp.where(ids[0] == 0, own, oth)
    second = jnp.where(ids[0] == 0, oth, own)
    text = jnp.concatenate([first[0:tr], second[0:tr]], axis=0)
    lay = jnp.concatenate(
        [
            half[tr:, g * lanes : (g + 1) * lanes]
            for half in (first, second)
            for g in range(ll // (first.shape[0] - tr))
        ],
        axis=0,
    )
    return text, lay


def matrices_body(tr, ll, ids, a, b, got, *outs):
    rows = a.shape[0] // (len(outs) // 2)
    for i in range(len(outs) // 2):
        at = slice(i * rows, (i + 1) * rows)
        text, lay = outs[2 * i : 2 * i + 2]
        text[...], lay[...] = own_rows(ids, a[at, :], b[at, :], got[at, :], tr, ll, lay.shape[1])


def proj_body(tr, ll, ids, a, b, got, qkv, out, lqkv, lout):
    et = qkv.shape[2]
    el = lqkv.shape[2]
    t, l = own_rows(ids, a[...], b[...], got[...], tr, ll, 4 * el)
    for c in range(3):
        qkv[c] = t[:, c * et : (c + 1) * et]
        lqkv[c] = l[:, c * el : (c + 1) * el]
    out[...] = t[:, 3 * et :].T
    lout[...] = l[:, 3 * el :].T


def swap(value, axis, bit):
    size = lax.axis_size(axis)
    return lax.ppermute(value, axis, [(i, i ^ bit) for i in range(size)])


def core_swap(value):
    return swap(value, "tensor", 1)


def chip_swap(value):
    return swap(value, "tensor", 2)


def other_section(value):
    return swap(value, "section", 1)


def around(value, axis):
    size = lax.axis_size(axis)
    return lax.ppermute(value, axis, [(i, (i + 1) % size) for i in range(size)])


def per_device(
    text_in,
    layout_in,
    text_cot,
    layout_cot,
    token_mask,
    box_mask,
    segments,
    text_qkv,
    text_qv_bias,
    text_out_w,
    text_ffn_in,
    text_ffn_bias,
    text_ffn_out,
    text_gains,
    text_biases,
    layout_qkv,
    layout_qv_bias,
    layout_out_w,
    layout_ffn_in,
    layout_ffn_bias,
    layout_ffn_out,
    layout_gains,
    layout_biases,
):
    sections = lax.axis_size("section")
    section = lax.axis_index("section")
    pages = lax.axis_size("dp")
    micro, mine, d = text_in.shape
    assert micro == sections == 2 and lax.axis_size("tensor") == 4 and segments.shape[1] == 1
    n = CHUNKS
    dl = layout_in.shape[2]
    width = d + dl
    rows = 4 * mine
    mine_rows = mine
    own = 2 * mine
    cb = mine // n
    hk = 2 * cb
    hs = text_qkv.shape[-1] // HEAD
    heads = 2 * hs
    f = text_ffn_in.shape[-1]
    fl = layout_ffn_in.shape[-1]
    fw = 2 * (f + fl)
    et, el = hs * HEAD, hs * LHEAD
    wq = heads * TILE
    part = functools.partial
    ids = Turn(
        jnp.stack([section, lax.axis_index("tensor"), lax.axis_index("dp")]).astype(jnp.int32)
    )

    pieces = pages if pages <= 4 else 1
    arows = 3 * et + el + et + LHEAD
    attn_own, piece = call(
        part(attn_send_body, pieces),
        [((arows, d), BF), ((arows // 2 // pieces, d), BF)],
        "attn_send",
    )(
        ids,
        jnp.swapaxes(text_qkv[0], 1, 2),
        jnp.swapaxes(layout_qkv[0], 1, 2),
        text_out_w[0],
        layout_out_w[0],
        loose=range(4),
    )

    def spread(value):
        out = [other_section(value)]
        for k in range(1, pieces):
            out.append(lax.ppermute(out[0], "dp", [(i, (i + k) % pages) for i in range(pages)]))
        return out

    attn_got = spread(piece)
    x_mine = call(inputs_body, [((mine, width), BF)], "inputs")(
        ids, text_in, jnp.swapaxes(layout_in, 1, 2), loose=(0, 1)
    )[0]
    x_mate = chip_swap(x_mine)
    prm_own = call(params_body, [((16, width), F32)], "params")(
        ids,
        text_gains[0],
        text_biases[0],
        text_ffn_bias,
        text_qv_bias[0],
        layout_gains[0],
        layout_biases[0],
        layout_ffn_bias,
        layout_qv_bias[0],
        loose=range(8),
    )[0]
    prm_oth = other_section(prm_own)
    x_all = jnp.concatenate(
        [v[k * cb : (k + 1) * cb] for k in range(n) for v in (x_mine, x_mate)], axis=0
    )
    x_own = [x_all[k * hk : (k + 1) * hk] for k in range(n)]
    cot, segr, segc = call(
        part(side_body, n),
        [((mine, width + 64), BF), ((1, rows), jnp.int32), ((rows, TILE), F32)],
        "side",
    )(
        ids,
        text_cot,
        jnp.swapaxes(layout_cot, 1, 2),
        token_mask,
        box_mask,
        segments.reshape(micro, 4, mine),
        loose=range(5),
    )

    x_peer = core_swap(x_all)
    cot_mate = chip_swap(cot)
    lead = call(first_half_body, [((arows // 2, d), BF)], "attn_lead", us=0.6)(
        ids, attn_own, after=attn_got[0:1]
    )[0]
    attn_direct = other_section(lead)
    frows = 2 * d + 2 * dl * dl // d
    ffn_own, piece = call(
        part(ffn_send_body, pieces),
        [((frows, d), BF), ((d // pieces, d), BF)],
        "ffn_send",
    )(
        ids, text_ffn_in[0], text_ffn_out[0], layout_ffn_in[0], layout_ffn_out[0],
        loose=range(4), after=[attn_direct, *attn_got],
    )
    ffn_got = spread(piece)
    weights = []

    def attn_weights(j, after=()):
        q_own, prm = call(
            part(pick_attn_body, j, pieces), [((arows, d), BF), ((16, width), F32)], "pick_attn", us=0.8
        )(ids, attn_own, attn_direct, prm_own, prm_oth, *attn_got, after=after)
        return q_own, prm

    def attn_packed(q_own, prm):
        wct, woc, bc, fb = call(
            part(pack_body, et, el, f, fl),
            [((3 * wq, width), BF), ((wq, width), BF), ((8, 3 * wq), F32), ((8, fw), F32)],
            "pack",
            us=1.5,
        )(ids, q_own, core_swap(q_own), prm, core_swap(prm))
        return wct, woc, bc, prm, fb

    def ffn_weights(j, after=()):
        w_own = call(part(pick_ffn_body, j, pieces, d), [((frows, d), BF)], "pick_ffn", us=1)(
            ids, ffn_own, ffn_direct, *ffn_got, after=after
        )[0]
        w_mate = core_swap(w_own)
        w1l, w2l = call(
            part(unfold_body, d), [((dl, 2 * fl), BF), ((2 * fl, dl), BF)], "unfold", us=0.6
        )(ids, w_own, w_mate)
        return w_own, w_mate, w1l, w2l

    picked = attn_weights(0, [x_peer])
    ffn_lead = call(part(ffn_lead_body, d), [((frows - d, d), BF)], "ffn_lead", us=0.6)(
        ids, ffn_own, after=ffn_got[0:1]
    )[0]
    ffn_direct = other_section(ffn_lead)
    attn_w = attn_packed(*picked)

    qkv_outs = [((hk, wq), BF), ((hk, 2 * wq), BF)]
    norm_outs = [((hk, width), F32), ((hk, TILE), F32)]
    row_out = ((hk, width), BF)
    mate_out = ((hk, width + f + fl), BF)
    outs = call(part(project_body, n), qkv_outs[0:1] * n + qkv_outs[1:2] * (2 * n), "project", us=3)(
        ids, attn_w[0], attn_w[2], x_all, x_peer
    )
    q, kv, peer = outs[0:n], outs[n : 2 * n], outs[2 * n :]

    own_row = ((own, width), BF)
    back_outs = [((own, width), F32), own_row, ((8, width), F32)]
    kept = []
    hidden = []
    for j in range(sections):
        wct, woc, bc, prm, fb = attn_w
        *s, oc, lse, xa = call(
            part(attn_body, n),
            [row_out] * n + [((own, wq), BF), ((8, own), F32), ((own, up_to_tile(width + wq // 2)), BF)],
            "attn",
            us=4,
            hbm=(n + 2,),
        )(ids, segc, segr, woc, *x_own, *q, *kv, *peer, after=[cot_mate] if j == 0 else mates_up)
        r = [chip_swap(v) for v in s]
        xa = core_swap(xa)
        attn_next = attn_packed(*attn_weights(j + 1, ffn_got[1:])) if j + 1 < sections else None
        ffn_w = ffn_weights(j)
        weights.append((wct, woc, bc, prm, fb, ffn_w))
        s2, n1, inv1, xb, act, slope, xf = ([] for _ in range(7))
        for k in range(n):
            outs = call(
                ffn_body,
                [row_out] + norm_outs + [row_out] + [((hk, fw), BF)] * 2 + [mate_out],
                "ffn",
                us=2 if j + 1 < sections else 60,
                hbm=(6,),
            )(ids, s[k], r[k], x_own[k], prm, fb, *ffn_w, after=[xa] if k == n - 1 else [])
            for got, value in zip((s2, n1, inv1, xb, act, slope, xf), outs):
                got.append(value)
        r2 = [chip_swap(v) for v in s2]
        xf = [core_swap(v) for v in xf]
        mates_up = xf
        kept.append((x_own, q, kv, peer, oc, lse, n1, inv1, xb, act, slope, xa, xf))
        y, n2, inv2 = ([] for _ in range(3))
        if j + 1 < sections:
            q, kv, peer = [], [], []
            for k in range(n):
                outs = call(
                    part(norm_project_body, d), norm_outs + [row_out] + qkv_outs, "norm_project", us=2
                )(
                    ids, s2[k], r2[k], n1[k], prm, attn_next[0], attn_next[2],
                )
                for got, value in zip((n2, inv2, y, q, kv), outs):
                    got.append(value)
                peer.append(core_swap(kv[k]))
            kept[j] = kept[j] + (n2, inv2)
            x_own = y
            attn_w = attn_next
        else:
            call(wait_body, [], "wait", us=1)(ids, after=[r2[0], xf[0]])
            last, dh2, dh2b, small2, dpre, s1, *xt = call(
                part(turn_body, n),
                [own_row] + back_outs + [((own, fw), BF), own_row] + [mate_out] * n,
                "turn",
                (pltpu.VMEM((own, width), F32), pltpu.VMEM((own, TILE), F32)),
                us=5,
                vmem=14,
            )(ids, prm, *ffn_w, cot, cot_mate, *s2, *r2, *n1, *slope)
            y = [last]
        hidden.append(y)

    tr = d // (2 * pages)
    ll = dl // (2 * pages)
    grows = tr + (8 if ll % 8 == 0 else ll)

    def grad_outs(count):
        return [((count * pages * grows, d), BF)] * 2 + [((8, width), F32)]

    def over_pages(keep, got):
        value = call(add_body, [(keep.shape, BF)], "add", hbm=True)(ids, keep, got)[0]
        return lax.psum_scatter(value, "dp", scatter_dimension=0, tiled=True)

    class OverPages:
        def __init__(self, keep, got):
            self.a, self.b, self.bit = keep, got, 1
            self.size = keep.shape[0] // pages

        def step(self):
            if pages > 4:
                if self.bit == 1:
                    self.out = over_pages(self.a, self.b)
                    self.bit = pages
            elif self.bit < pages:
                rows = self.a.shape[0] // 2
                self.a, send = call(
                    part(halve_body, self.bit, self.size), [((rows, d), BF)] * 2, "halve", us=0.7
                )(ids, self.a, self.b)
                self.b = swap(send, "dp", self.bit)
                self.bit *= 2
            else:
                self.out = call(add_body, [(self.a.shape, BF)], "add", us=0.7)(ids, self.a, self.b)[0]

    def collect(layers):
        parts = list(layers[0]) + list(layers[1])
        cut = len(layers[0])
        away = call(part(away_body, n, cut), [((mine_rows, width), BF)], "away", us=0.6)(ids, *parts)[0]
        return parts, cut, other_section(away)

    def both(parts, cut, got):
        text, lay = call(
            part(both_body, n, cut, d),
            [((micro, mine_rows, d), BF), ((micro, dl, mine_rows), BF)],
            "both",
            hbm=True,
        )(ids, *parts, got)
        return text[None], jnp.swapaxes(lay, 1, 2)[None]

    ffn_grad = call(part(ffn_grad_body, d, f, fl, n, pages), grad_outs(2), "ffn_grad", us=5, vmem=16)
    attn_grad = call(part(attn_grad_body, d, n, pages), grad_outs(1), "attn_grad", us=4)
    hid = collect(hidden)
    input_grads = [None] * sections
    small_sums = [None] * sections
    for j in reversed(range(sections)):
        x_own, q, kv, peer, oc, lse, n1, inv1, xb, act, slope, xa, xf = kept[j][0:13]
        wct, woc, bc, prm, fb, ffn_w = weights[j]
        if j + 1 < sections:
            n2, inv2 = kept[j][13:]
            dxin, dh2, dh2b, small2, dpre, s1, *xt = call(
                part(back_next_body, n),
                [own_row] + back_outs + [((own, fw), BF), own_row] + [mate_out] * n,
                "back_next",
                us=5,
                vmem=14,
            )(ids, dh, s, r, prm, *ffn_w, *n2, *inv2, *slope)
            input_grads[j + 1] = [dxin]
        r1 = chip_swap(s1)
        if j == 0:
            attn_up = OverPages(*attn_pair)
            attn_up.step()
        keep, send, hsum = ffn_grad(
            ids, dh2b, dpre, *act, *xb, *xf, *[core_swap(v) for v in xt]
        )
        ffn_pair = (keep, other_section(send))
        if j == 0:
            ffn_up.step()
        dh, dhb, small1, dq, mine, *more = call(
            part(attn_back_body, n, d),
            back_outs + [((own, wq), BF), ((own, 2 * wq), F32)] + [((hk, 2 * wq), BF)] * n + [row_out] * n,
            "attn_back",
            us=7,
            vmem=14,
        )(ids, dh2, s1, r1, prm, segc, segr, woc, lse, *n1, *inv1, *q, *kv, *peer)
        far = [core_swap(v) for v in more[0:n]]
        ups = [core_swap(v) for v in more[n:]]
        s, dkv, *xd = call(
            part(dx_body, n),
            [own_row, ((own, 2 * wq), BF)] + [((hk, 3 * wq // 2), BF)] * n,
            "dx",
            us=2.5,
        )(ids, dq, mine, wct, *far)
        r = chip_swap(s)
        keep, send, hq = attn_grad(
            ids, dhb, dq, dkv, *x_own, *ups, *[core_swap(v) for v in xd], oc, xa
        )
        attn_pair = (keep, other_section(send))
        if j:
            ffn_up = OverPages(*ffn_pair)
            ffn_up.step()
        if j:
            small_sums[j] = call(smalls_body, [((8, width), F32)], "smalls", us=0.6)(
                ids, small1, small2, hsum, hq
            )[0]
    input_grads[0] = call(part(back_last_body, n), [own_row], "back_last", us=0.6)(ids, dh, s, r)

    ing = collect(input_grads)
    small_sums[0] = call(smalls_body, [((8, width), F32)], "smalls", us=0.6)(
        ids, small1, small2, hsum, hq
    )[0]
    both_sums = jnp.concatenate(small_sums, axis=0)
    bit = 1
    while bit < pages:
        both_sums = both_sums + swap(both_sums, "dp", bit)
        bit *= 2
    shared_sums = jnp.concatenate([both_sums[0:6], both_sums[8:14]], axis=0)
    shared_sums = shared_sums + core_swap(shared_sums)
    shared_sums = shared_sums + chip_swap(shared_sums)
    attn_up.step()
    ffn_up.step()
    ffn_last = OverPages(*ffn_pair)
    ffn_last.step()
    ffn_last.step()
    attn_last = OverPages(*attn_pair)
    attn_last.step()
    small_mine, small_away = call(small_halves_body, [((8, width), F32)] * 2, "small_halves", us=0.6)(
        ids, both_sums, shared_sums
    )
    small_got = other_section(small_away)
    hid_t, hid_l = both(*hid)
    attn_last.step()
    ing_t, ing_l = both(*ing)
    attn_up.step()
    def away_half(a, b, loose):
        away = call(swap_body, [(a.shape, BF)], "swap", us=0.6)(ids, a, b, loose=loose)[0]
        return a, b, other_section(away)

    rs = (1,) if pages <= 4 else (0, 1)
    rs = () if pages <= 4 else (0, 1)
    ffn_last.step()
    ffn_parts = away_half(ffn_last.out, ffn_up.out, rs)
    attn_last.step()
    attn_parts = away_half(attn_last.out, attn_up.out, rs)
    g2, lg2, g1, lg1 = call(
        part(matrices_body, tr, ll),
        [((2 * tr, f), F32), ((2 * ll, fl), F32)] * 2,
        "matrices",
        hbm=True,
    )(ids, *ffn_parts, loose=rs)
    g_qkv, g_out, g_lqkv, g_lout = call(
        part(proj_body, tr, ll),
        [((3, 2 * tr, et), F32), ((et, 2 * tr), F32), ((3, 2 * ll, el), F32), ((el, 2 * ll), F32)],
        "proj",
        hbm=True,
    )(ids, *attn_parts, loose=rs)

    total = small_mine + small_got
    shared = total[0:6]
    qv = total[7, 0 : 3 * et].reshape(3, et)
    lqv = total[7, d : d + 3 * el].reshape(3, el)
    return (
        hid_t,
        hid_l,
        ing_t,
        ing_l,
        g_qkv[None],
        jnp.stack([qv[0], qv[2]])[None],
        g_out[None],
        g1[None],
        total[6:7, 0:f],
        g2.T[None],
        shared[None, 0:2, 0:d],
        shared[None, 2:6, 0:d],
        g_lqkv[None],
        jnp.stack([lqv[0], lqv[2]])[None],
        g_lout[None],
        lg1[None],
        total[6:7, f:fw],
        lg2.T[None],
        shared[None, 0:2, d:],
        shared[None, 2:6, d:],
    )


def solution(mesh):
    in_specs = (
        P(None, ("dp", "tensor"), None),
        P(None, ("dp", "tensor"), None),
        P(None, ("dp", "tensor"), None),
        P(None, ("dp", "tensor"), None),
        P(None, ("dp", "tensor")),
        P(None, ("dp", "tensor")),
        P(None, "dp", None),
        P("section", None, None, "tensor"),
        P("section", None, "tensor"),
        P("section", "tensor", None),
        P("section", None, "tensor"),
        P("section", "tensor"),
        P("section", "tensor", None),
        P("section", None, None),
        P("section", None, None),
        P("section", None, None, "tensor"),
        P("section", None, "tensor"),
        P("section", "tensor", None),
        P("section", None, "tensor"),
        P("section", "tensor"),
        P("section", "tensor", None),
        P("section", None, None),
        P("section", None, None),
    )
    out_specs = (
        P("section", None, ("dp", "tensor"), None),
        P("section", None, ("dp", "tensor"), None),
        P("section", None, ("dp", "tensor"), None),
        P("section", None, ("dp", "tensor"), None),
        P("section", None, "dp", "tensor"),
        P("section", None, "tensor"),
        P("section", "tensor", "dp"),
        P("section", "dp", "tensor"),
        P("section", "tensor"),
        P("section", "tensor", "dp"),
        P("section", None, None),
        P("section", None, None),
        P("section", None, "dp", "tensor"),
        P("section", None, "tensor"),
        P("section", "tensor", "dp"),
        P("section", "dp", "tensor"),
        P("section", "tensor"),
        P("section", "tensor", "dp"),
        P("section", None, None),
        P("section", None, None),
    )
    return jax.shard_map(
        per_device, mesh=mesh, in_specs=in_specs, out_specs=out_specs, check_vma=False
    )
```

```python
import functools

import jax
import jax.numpy as jnp
from jax import lax
from jax.experimental import pallas as pl
from jax.experimental.pallas import tpu as pltpu
from jax.sharding import PartitionSpec as P

HEAD = 64
LHEAD = 16
TILE = 128
CHUNKS = 2

EPS = 1e-05
MASKED = -1000000000.0
BF = jnp.bfloat16
F32 = jnp.float32

NT = (((1,), (1,)), ((), ()))
TN = (((0,), (0,)), ((), ()))
NN = (((1,), (0,)), ((), ()))


def mm(a, b, dims=NN):
    return lax.dot_general(a, b, dims, preferred_element_type=F32)


def call(body, outs, name, scratch=(), us=2, hbm=(), vmem=10):
    def run(turn, *args, loose=(), after=()):
        kept = 1 + len(args)
        extra = [turn.token] if turn.token is not None else []
        extra += list(after)

        def inner(*refs):
            given = refs[kept + len(extra) :]
            given[len(outs)][...] = jnp.zeros_like(given[len(outs)])
            body(*refs[0:kept], *given[0 : len(outs)], *given[len(outs) + 1 :])

        placed = [
            pltpu.with_memory_space_constraint(a, pltpu.HBM if i in loose else pltpu.VMEM)
            for i, a in enumerate(list(args) + extra)
        ]
        *results, turn.token = pl.pallas_call(
            inner,
            out_shape=[
                (jax.ShapeDtypeStruct if hbm is True or i in hbm else pltpu.VMEM)(shape, dtype)
                for i, (shape, dtype) in enumerate(outs)
            ]
            + [pltpu.VMEM((8, TILE), F32)],
            in_specs=[pl.BlockSpec(memory_space=pltpu.SMEM)]
            + [pl.BlockSpec(memory_space=pltpu.VMEM)] * len(placed),
            scratch_shapes=list(scratch),
            name=name,
            cost_estimate=pl.CostEstimate(flops=int(us * 10**8), transcendentals=0, bytes_accessed=0),
            compiler_params=pltpu.CompilerParams(vmem_limit_bytes=vmem * 1024 * 1024),
        )(turn.ids, *placed)
        return results

    return run


class Turn:
    def __init__(self, ids):
        self.ids = ids
        self.token = None


def up_to_tile(lanes):
    return -(-lanes // TILE) * TILE


def cat(refs, a0=None, a1=None):
    return jnp.concatenate([ref[:, a0:a1] for ref in refs], axis=0)


def attn_send_body(pieces, ids, qt, ql, ot, ol, full, piece):
    et, d = qt.shape[1:]
    el, dl = ql.shape[1:]
    full[3 * et :, :] = jnp.zeros_like(full[3 * et :, :])
    for c in range(3):
        full[c * et : (c + 1) * et, :] = qt[c]
        full[3 * et : 3 * et + el, c * dl : (c + 1) * dl] = ql[c]
    at = 3 * et + el
    full[at : at + et, :] = ot[...]
    for h in range(el // LHEAD):
        full[at + et : at + et + LHEAD, h * dl : (h + 1) * dl] = ol[h * LHEAD : (h + 1) * LHEAD, :]
    half = full.shape[0] // 2
    size = piece.shape[0]
    spot = ids[2] if pieces > 1 else 0
    piece[...] = full[pl.ds(pl.multiple_of(half + spot * size, 8), size), :]


def first_half_body(ids, full, direct):
    direct[...] = full[0 : direct.shape[0], :]


def ffn_lead_body(d, ids, full, direct):
    half = d // 2
    direct[0:half, :] = full[0:half, :]
    direct[half:d, :] = full[d : d + half, :]
    direct[d:, :] = full[2 * d :, :]


def ffn_send_body(pieces, ids, w1, w2, w1l, w2l, full, piece):
    d, f = w1.shape
    dl = w1l.shape[0]
    deep = dl * dl // d
    full[0:d, :] = w1[...]
    full[d : 2 * d, :] = w2[...]
    for g in range(d // dl):
        full[2 * d : 2 * d + deep, g * dl : (g + 1) * dl] = w1l[g * deep : (g + 1) * deep, :]
        full[2 * d + deep :, g * dl : (g + 1) * dl] = w2l[g * deep : (g + 1) * deep, :]
    half = d // 2
    size = piece.shape[0] // 2
    at = pl.multiple_of(half + (ids[2] if pieces > 1 else 0) * size, 8)
    piece[0:size, :] = w1[pl.ds(at, size), :]
    piece[size:, :] = w2[pl.ds(at, size), :]


def inputs_body(ids, tin, lin, out):
    s = ids[0]
    d = tin.shape[2]
    out[:, 0:d] = tin[s]
    out[:, d:] = lin[s].T


def side_body(chunks, ids, tcot, lcot, tmask, bmask, seg, cot, segr, segc):
    s = ids[0]
    mine, d = tcot.shape[1:]
    width = d + lcot.shape[1]
    rows = mine // chunks
    wt = (0.25 + tmask[pl.ds(s, 1), :].astype(F32)).astype(BF).astype(F32)
    wb = (0.25 + bmask[pl.ds(s, 1), :].astype(F32)).astype(BF).astype(F32)
    cot[:, 0:d] = tcot[s]
    cot[:, d:width] = lcot[s].T
    cot[:, width : width + 32] = jnp.broadcast_to(wt, (TILE, mine)).T[:, 0:32].astype(BF)
    cot[:, width + 32 : width + 64] = jnp.broadcast_to(wb, (TILE, mine)).T[:, 0:32].astype(BF)
    at = 0
    for first in (0, 1):
        for k in range(chunks):
            for step in (first, first ^ 2):
                block = seg[s, pl.ds(ids[1] ^ step, 1), k * rows : (k + 1) * rows]
                segr[0:1, at : at + rows] = block
                at += rows
    segc[...] = jnp.broadcast_to(segr[...].astype(F32), (TILE, at)).T


def params_body(ids, tg, tb, tf, tq, lg, lb, lf, lq, prm):
    d = tg.shape[1]
    prm[...] = jnp.zeros_like(prm)
    for a, gains, biases, hidden, qv in ((0, tg, tb, tf, tq), (d, lg, lb, lf, lq)):
        prm[0:2, a : a + gains.shape[1]] = gains[...]
        prm[2:6, a : a + gains.shape[1]] = biases[...]
        prm[6:7, a : a + hidden.shape[1]] = hidden[...]
        prm[7:9, a : a + qv.shape[1]] = qv[...]


def assemble(full, base, rows, direct, got, ids, at, size):
    half = rows // 2
    full[base : base + half, :] = direct
    n = len(got)
    for k in range(n):
        place = base + half + lax.rem(ids[2] + (n - k), n) * size
        full[pl.ds(pl.multiple_of(place, 8), size), :] = got[k][at : at + size, :]


def pick_attn_body(layer, pieces, ids, own, direct, prm_own, prm_oth, *refs):
    got = refs[0:pieces]
    out, prm = refs[pieces:]

    @pl.when(ids[0] == layer)
    def _():
        out[...] = own[...]
        prm[...] = prm_own[...]

    @pl.when(ids[0] != layer)
    def _():
        assemble(out, 0, out.shape[0], direct[...], got, ids, 0, got[0].shape[0])
        prm[...] = prm_oth[...]


def pick_ffn_body(layer, pieces, d, ids, own, direct, *refs):
    got = refs[0:pieces]
    out = refs[pieces]

    @pl.when(ids[0] == layer)
    def _():
        out[...] = own[...]

    @pl.when(ids[0] != layer)
    def _():
        size = got[0].shape[0] // 2
        half = d // 2
        assemble(out, 0, d, direct[0:half, :], got, ids, 0, size)
        assemble(out, d, d, direct[half:d, :], got, ids, size, size)
        out[2 * d :, :] = direct[d:, :]


def unfold_body(d, ids, own, mate, w1l, w2l):
    dl = w1l.shape[0]
    fl = w1l.shape[1] // 2
    deep = dl * dl // d
    for side, ref in ((0, own), (1, mate)):
        for g in range(d // dl):
            a = 2 * d
            w1l[g * deep : (g + 1) * deep, side * fl : (side + 1) * fl] = ref[
                a : a + deep, g * dl : (g + 1) * dl
            ]
            w2l[side * fl + g * deep : side * fl + (g + 1) * deep, :] = ref[
                a + deep : a + 2 * deep, g * dl : (g + 1) * dl
            ]


def pack_body(et, el, f, fl, ids, q0, q1, prm0, prm1, wct, woc, bc, fb):
    d = q0.shape[1]
    dl = wct.shape[1] - d
    hs = et // HEAD
    heads = 2 * hs
    wct[...] = jnp.zeros_like(wct)
    woc[...] = jnp.zeros_like(woc)
    bc[...] = jnp.zeros_like(bc)
    at = 3 * et + el
    for side, q, prm in ((0, q0, prm0), (1, q1, prm1)):
        for h in range(hs):
            i = side * hs + h
            for c in range(3):
                row = (c * heads + i) * TILE
                wt = q[c * et + h * HEAD : c * et + (h + 1) * HEAD, :]
                wl = q[3 * et + h * LHEAD : 3 * et + (h + 1) * LHEAD, c * dl : (c + 1) * dl]
                if c == 0:
                    wt = (wt.astype(F32) * HEAD**-0.5).astype(BF)
                    wl = (wl.astype(F32) * LHEAD**-0.5).astype(BF)
                wct[row : row + HEAD, 0:d] = wt
                wct[row + HEAD : row + HEAD + LHEAD, d:] = wl
            row = i * TILE
            woc[row : row + HEAD, 0:d] = q[at + h * HEAD : at + (h + 1) * HEAD, :]
            woc[row + HEAD : row + HEAD + LHEAD, d:] = q[
                at + et : at + et + LHEAD, h * dl : (h + 1) * dl
            ]
            for p, c, st, sl in ((7, 0, HEAD**-0.5, LHEAD**-0.5), (8, 2, 1.0, 1.0)):
                col = (c * heads + i) * TILE
                bc[0:1, col : col + HEAD] = prm[p : p + 1, h * HEAD : (h + 1) * HEAD] * st
                bc[0:1, col + HEAD : col + HEAD + LHEAD] = (
                    prm[p : p + 1, d + h * LHEAD : d + (h + 1) * LHEAD] * sl
                )
        fb[0:1, side * f : (side + 1) * f] = prm[6:7, 0:f]
        fb[0:1, 2 * f + side * fl : 2 * f + (side + 1) * fl] = prm[6:7, d : d + fl]


def gelu_pair(pre):
    phi = 0.5 * (1.0 + lax.erf(pre * (0.5**0.5)))
    slope = phi + pre * (jnp.exp(-0.5 * pre * pre) * 0.3989422804014327)
    return pre * phi, slope


def crossed(s, r, chunks=1):
    n = s.shape[0] // (2 * chunks)
    parts = []
    for k in range(chunks):
        a, b, c = 2 * k * n, (2 * k + 1) * n, 2 * (k + 1) * n
        parts.append(s[a:b, :].astype(F32) + r[b:c, :].astype(F32))
        parts.append(s[b:c, :].astype(F32) + r[a:b, :].astype(F32))
    return jnp.concatenate(parts, axis=0)


def norm(h, prm, gain_row, shift_row, d, normed, inv):
    ivs, outs = [], []
    for a0, a1 in ((0, d), (d, h.shape[1])):
        x = h[:, a0:a1]
        centred = x - jnp.mean(x, axis=-1, keepdims=True)
        iv = lax.rsqrt(jnp.mean(centred * centred, axis=-1, keepdims=True) + EPS)
        n = centred * iv
        normed[:, a0:a1] = n
        outs.append(n * prm[gain_row : gain_row + 1, a0:a1] + prm[shift_row : shift_row + 1, a0:a1])
        ivs.append(iv)
    lane = lax.broadcasted_iota(jnp.int32, inv.shape, 1)
    inv[...] = jnp.where(lane < HEAD, ivs[0], ivs[1])
    return outs


def project(x, wct, bc, q, kv):
    split = q.shape[1]
    q[...] = (mm(x, wct[0:split, :], NT) + bc[0:1, 0:split]).astype(BF)
    kv[...] = (mm(x, wct[split:, :], NT) + bc[0:1, split:]).astype(BF)


def project_body(n, ids, wct, bc, *refs):
    x, far = refs[0][...], refs[1][...]
    refs = (None,) * n + refs[2:]
    split = refs[n].shape[1]
    half = split // 2
    rows = refs[n].shape[0]
    kv = (mm(far, wct[split:, :], NT) + bc[0:1, split:]).astype(BF)
    for k in range(n):
        part = kv[k * rows : (k + 1) * rows]
        for i, a in enumerate((half, 0, split + half, split)):
            refs[3 * n + k][:, i * half : (i + 1) * half] = part[:, a : a + half]
    q = (mm(x, wct[0:split, :], NT) + bc[0:1, 0:split]).astype(BF)
    kv = (mm(x, wct[split:, :], NT) + bc[0:1, split:]).astype(BF)
    for k in range(n):
        refs[n + k][...] = q[k * rows : (k + 1) * rows]
        refs[2 * n + k][...] = kv[k * rows : (k + 1) * rows]


def heads_columns(own, peer, i, heads, value):
    base = heads * TILE if value else 0
    a = base + i * TILE
    b = base + (i + heads // 2) % heads * TILE
    return jnp.concatenate([ref[:, a : a + TILE] for ref in own] + [ref[:, b : b + TILE] for ref in peer], axis=0)


def same_doc(segc, segr, q0, n):
    seg = segc[...]
    if n > TILE:
        seg = jnp.concatenate([seg] * (n // TILE), axis=1)
    return seg == segr[:, q0 : q0 + n].astype(F32)


def attn_body(n, ids, segc, segr, woc, *refs):
    xs, qs, own, peer = (refs[i * n : (i + 1) * n] for i in range(4))
    outs = refs[4 * n : 5 * n]
    oc, lse, sent = refs[5 * n :]
    rows = oc.shape[0]
    heads = oc.shape[1] // TILE
    same = same_doc(segc, segr, 0, rows)
    lse[...] = jnp.zeros_like(lse)
    for h in range(heads):
        key = heads_columns(own, peer, h, heads, False)
        val_t = heads_columns(own, peer, h, heads, True).T
        query = cat(qs, h * TILE, (h + 1) * TILE)
        s = jnp.where(same, mm(key, query, NT), MASKED)
        top = jnp.max(s, axis=0, keepdims=True)
        p = jnp.exp(s - top)
        total = jnp.sum(p, axis=0, keepdims=True)
        o = mm(val_t, p.astype(BF)) / total
        oc[:, h * TILE : (h + 1) * TILE] = o.T.astype(BF)
        lse[h : h + 1, :] = top + jnp.log(total)
    part = mm(oc[...], woc[...]).astype(BF)
    step = rows // n
    width = xs[0].shape[1]
    for k in range(n):
        sent[k * step : (k + 1) * step, 0:width] = xs[k][...]
    half = heads // 2 * TILE
    sent[:, width : width + half] = oc[:, half:]
    if width + half < sent.shape[1]:
        sent[:, width + half :] = jnp.zeros_like(sent[:, width + half :])
    for k in range(n):
        outs[k][...] = part[k * step : (k + 1) * step]


def hidden_parts(own, mate, w1l, w2l):
    f = own.shape[1]
    fl = w1l.shape[1]
    width = w1l.shape[0]
    d = (own.shape[0] * f - width * fl) // (2 * f)
    w1, w2 = slice(0, d), slice(d, d + f)
    return (
        (0, d, 0, f, own.at[w1], own.at[w2]),
        (0, d, f, 2 * f, mate.at[w1], mate.at[w2]),
        (d, d + width, 2 * f, 2 * f + fl, w1l, w2l),
    )


def for_mate(a, b, d, f, fl, sent):
    width = a.shape[1]
    sent[:, 0:width] = a[...]
    sent[:, width : width + f] = b[:, f : 2 * f]
    sent[:, width + f :] = b[:, 2 * f + fl :]


def ffn_body(ids, s, r, x, prm, fb, own, mate, w1l, w2l, out, n1, inv, xb, act, slope, sent):
    d = n1.shape[1] - w1l.shape[0]
    h = crossed(s, r) + x[...].astype(F32) + prm[2:3, :]
    text, lay = norm(h, prm, 0, 3, d, n1, inv)
    xb[:, 0:d] = text.astype(BF)
    xb[:, d:] = lay.astype(BF)
    parts = []
    for a0, a1, f0, f1, w1, w2 in hidden_parts(own, mate, w1l, w2l):
        pre = mm(xb[:, a0:a1], w1[...]) + fb[0:1, f0:f1]
        g, gp = gelu_pair(pre)
        g = g.astype(BF)
        act[:, f0:f1] = g
        slope[:, f0:f1] = gp.astype(BF)
        parts.append(mm(g, w2[...]))
    out[:, 0:d] = (parts[0] + parts[1]).astype(BF)
    out[:, d:] = parts[2].astype(BF)
    for_mate(xb, act, d, own.shape[1], w1l.shape[1] // 2, sent)


def second_norm(d, s, r, n1, prm, n2, inv, y, chunks=1):
    h = n1[...] * prm[0:1, :] + prm[3:4, :] + crossed(s, r, chunks) + prm[4:5, :]
    text, lay = norm(h, prm, 1, 5, d, n2, inv)
    y[:, 0:d] = text.astype(BF)
    y[:, d:] = lay.astype(BF)


def wait_body(ids):
    pass


def norm_project_body(d, ids, s, r, n1, prm, wct, bc, n2, inv, y, q, kv):
    second_norm(d, s, r, n1, prm, n2, inv, y)
    project(y[...], wct, bc, q, kv)


def norm_back(dy, normed, inv, prm, gain_row, d, n, dh, dhb, small):
    small[...] = jnp.zeros_like(small)
    block = dy.shape[0] // (2 * n)

    def total(value):
        return sum(
            jnp.sum(value[2 * k * block : (2 * k + 1) * block], axis=0, keepdims=True) for k in range(n)
        )

    for a0, a1, lane in ((0, d, 0), (d, dy.shape[1], HEAD)):
        up = dy[:, a0:a1]
        x = normed[:, a0:a1]
        scaled = up * prm[gain_row : gain_row + 1, a0:a1]
        inner = (
            scaled
            - jnp.mean(scaled, axis=-1, keepdims=True)
            - x * jnp.mean(scaled * x, axis=-1, keepdims=True)
        )
        g = inner * inv[:, lane : lane + 1]
        dh[:, a0:a1] = g
        dhb[:, a0:a1] = g.astype(BF)
        small[0:1, a0:a1] = total(up * x)
        small[1:2, a0:a1] = total(up)
        small[2:3, a0:a1] = total(g)


def ffn_back(dhb, slopes, own, mate, w1l, w2l, dpre, out, sents):
    d = out.shape[1] - w1l.shape[0]
    f, fl = own.shape[1], w1l.shape[1] // 2
    parts = []
    for a0, a1, f0, f1, w1, w2 in hidden_parts(own, mate, w1l, w2l):
        dact = mm(dhb[:, a0:a1], w2[...], NT)
        dp = (dact * cat(slopes, f0, f1).astype(F32)).astype(BF)
        dpre[:, f0:f1] = dp
        parts.append(mm(dp, w1[...], NT))
    out[:, 0:d] = (parts[0] + parts[1]).astype(BF)
    out[:, d:] = parts[2].astype(BF)
    rows = sents[0].shape[0]
    for k, sent in enumerate(sents):
        a, b = k * rows, (k + 1) * rows
        for_mate(dhb[a:b, :], dpre[a:b, :], d, f, fl, sent)


def turn_body(n, ids, prm, own, mate, w1l, w2l, cot0, cot1, *refs):
    s, r, n1, slopes = (refs[i * n : (i + 1) * n] for i in range(4))
    y, dh, dhb, small, dpre, out = refs[4 * n : 4 * n + 6]
    sents = refs[4 * n + 6 : 5 * n + 6]
    n2, inv = refs[5 * n + 6 :]
    width = n2.shape[1]
    d = width - w1l.shape[0]
    second_norm(d, cat(s), cat(r), cat(n1), prm, n2, inv, y, n)
    parts = []
    step = cot0.shape[0] // n
    for k in range(n):
        for cot in (cot0, cot1):
            c = cot[k * step : (k + 1) * step, :].astype(F32)
            lane = lax.broadcasted_iota(jnp.int32, (c.shape[0], width), 1)
            w = jnp.where(lane < d, c[:, width : width + 1], c[:, width + 32 : width + 33])
            parts.append(c[:, 0:width] * w)
    norm_back(jnp.concatenate(parts, axis=0), n2, inv, prm, 1, d, n, dh, dhb, small)
    ffn_back(dhb, slopes, own, mate, w1l, w2l, dpre, out, sents)


def back_next_body(n, ids, dh_up, s, r, prm, own, mate, w1l, w2l, *refs):
    n2, inv, slopes = (refs[i * n : (i + 1) * n] for i in range(3))
    dxin, dh, dhb, small, dpre, out = refs[3 * n : 3 * n + 6]
    sents = refs[3 * n + 6 :]
    d = dh.shape[1] - w1l.shape[0]
    dx = (dh_up[...] + crossed(s, r, n)).astype(BF)
    dxin[...] = dx
    norm_back(dx.astype(F32), cat(n2), cat(inv), prm, 1, d, n, dh, dhb, small)
    ffn_back(dhb, slopes, own, mate, w1l, w2l, dpre, out, sents)


def attn_back_body(n, d, ids, dh2, s1, r1, prm, segc, segr, woc, lse, *refs):
    n1, inv, qs, own, peer = (refs[i * n : (i + 1) * n] for i in range(5))
    dh, dhb, small, dq, mine = refs[5 * n : 5 * n + 5]
    fars = refs[5 * n + 5 : 6 * n + 5]
    sents = refs[6 * n + 5 :]
    norm_back(dh2[...] + crossed(s1, r1, n), cat(n1), cat(inv), prm, 0, d, n, dh, dhb, small)
    rows = dq.shape[0]
    step = rows // n
    for k, sent in enumerate(sents):
        sent[...] = dhb[k * step : (k + 1) * step, :]
    heads = dq.shape[1] // TILE
    total = 2 * rows
    doc = mm(dhb[...], woc[...], NT).astype(BF)
    same = same_doc(segc, segr, 0, rows)
    text_t = lax.broadcasted_iota(jnp.int32, (total, TILE), 1) < HEAD
    text_q = lax.broadcasted_iota(jnp.int32, (rows, TILE), 1) < HEAD
    for h in range(heads):
        hc = slice(h * TILE, (h + 1) * TILE)
        vc = slice((heads + h) * TILE, (heads + h + 1) * TILE)
        key = heads_columns(own, peer, h, heads, False)
        val = heads_columns(own, peer, h, heads, True)
        zero = jnp.zeros_like(key)
        query = cat(qs, h * TILE, (h + 1) * TILE)
        up = doc[:, hc]
        zero_q = jnp.zeros_like(query)
        s = mm(key, query, NT)
        p = jnp.where(same, jnp.exp(s - lse[h : h + 1, :]), 0.0)
        dp_all = mm(val, up, NT)
        dp_text = mm(val, jnp.where(text_q, up, zero_q), NT)
        ds_all = (p * (dp_all - jnp.sum(dp_all * p, axis=0, keepdims=True))).astype(BF)
        ds_text = (p * (dp_text - jnp.sum(dp_text * p, axis=0, keepdims=True))).astype(BF)
        dval = mm(p.astype(BF), up)
        dkey = mm(ds_text, jnp.where(text_q, query, zero_q)) + mm(ds_all, jnp.where(text_q, zero_q, query))
        dq_t = mm(jnp.where(text_t, key, zero).T, ds_text) + mm(jnp.where(text_t, zero, key).T, ds_all)
        dq[:, hc] = dq_t.T.astype(BF)
        for col, value in ((hc, dkey), (vc, dval)):
            mine[:, col] = value[0:rows]
            for k, far in enumerate(fars):
                far[:, col] = value[rows + k * step : rows + (k + 1) * step].astype(BF)


def dx_body(n, ids, dq, mine, wct, *refs):
    fars = refs[0:n]
    out, dkv = refs[n : n + 2]
    sents = refs[n + 2 :]
    rows, split = dq.shape
    half = split // 2
    far = cat(fars)
    far = jnp.concatenate(
        [far[:, half:split], far[:, 0:half], far[:, split + half :], far[:, split : split + half]], axis=1
    )
    dkv[...] = (mine[...] + far.astype(F32)).astype(BF)
    out[...] = (mm(dq[...], wct[0:split, :]) + mm(dkv[...], wct[split:, :])).astype(BF)
    step = rows // n
    for k, sent in enumerate(sents):
        a, b = k * step, (k + 1) * step
        for i, part in enumerate((dq[a:b, half:], dkv[a:b, half:split], dkv[a:b, split + half :])):
            sent[:, i * half : (i + 1) * half] = part


def back_last_body(n, ids, dh, s, r, dxin):
    dxin[...] = (dh[...] + crossed(s, r, n)).astype(BF)


def put_halves(text, lay, pages, ids, keep, send, i, n):
    tr = text.shape[0] // (2 * pages)
    ll = lay.shape[0] // (2 * pages)
    lanes = lay.shape[1]
    lr = 8 if ll % 8 == 0 else ll
    rows = tr + lr
    blank = keep.shape[1] - ll // lr * lanes

    def put(order):
        for ref, half in zip((keep, send), order):
            for z in range(pages):
                at = (z * n + i) * rows
                a = (2 * z + half) * tr
                ref[at : at + tr, :] = text[a : a + tr]
                for g in range(ll // lr):
                    b = (2 * z + half) * ll + g * lr
                    ref[at + tr : at + rows, g * lanes : (g + 1) * lanes] = lay[b : b + lr]
                if blank:
                    ref[at + tr : at + rows, ref.shape[1] - blank :] = jnp.zeros((lr, blank), ref.dtype)

    @pl.when(ids[0] == 0)
    def _():
        put((0, 1))

    @pl.when(ids[0] != 0)
    def _():
        put((1, 0))


def both_cores(own, mate, parts, at):
    left = jnp.concatenate([jnp.concatenate([ref[:, a:b] for a, b in parts], axis=1) for ref in own], axis=0)
    size = left.shape[1]
    return jnp.concatenate([left] + [ref[:, at : at + size] for ref in mate], axis=0)


def ffn_grad_body(d, f, fl, n, pages, ids, *refs):
    up, dpre = refs[0:1], refs[1:2]
    act, x, sent, sent_up = (refs[2 + i * n : 2 + (i + 1) * n] for i in range(4))
    keep, send, total = refs[2 + 4 * n :]
    width = x[0].shape[1]
    hidden = ((0, f), (2 * f, 2 * f + fl))
    for i, (a, b, a_mate) in enumerate(((up, act, sent_up), (x, dpre, sent))):
        left = both_cores(a, a_mate, ((0, width),), 0)
        right = both_cores(b, (sent, sent_up)[i], hidden, width)
        text = mm(left[:, 0:d], right[:, 0:f], TN).astype(BF)
        lay = mm(left[:, d:], right[:, f:], TN).astype(BF)
        put_halves(text, lay, pages, ids, keep, send, i, 2)
    total[...] = jnp.broadcast_to(jnp.sum(right.astype(F32), axis=0, keepdims=True), total.shape)


def attn_grad_body(d, n, pages, ids, *refs):
    ups, dqs, dkvs = refs[0:1], refs[1:2], refs[2:3]
    xs, ups_mate, sent_up = (refs[3 + i * n : 3 + (i + 1) * n] for i in range(3))
    oc, sent, keep, send, qb = refs[3 + 3 * n :]
    width = xs[0].shape[1]
    half = dqs[0].shape[1] // 2
    hs = half // TILE
    x = both_cores(xs, (sent,), ((0, width),), 0)
    up = both_cores(ups, ups_mate, ((0, width),), 0)
    o = both_cores((oc,), (sent,), ((0, half),), width)
    grads = (
        both_cores(dqs, sent_up, ((0, half),), 0),
        both_cores(dkvs, sent_up, ((0, half),), half),
        both_cores(dkvs, sent_up, ((2 * half, 3 * half),), 2 * half),
    )

    def lanes(value, a, size):
        return [value[:, h * TILE + a : h * TILE + a + size] for h in range(hs)]

    tq = jnp.concatenate([v for g in grads for v in lanes(g, 0, HEAD)], axis=1)
    lq = jnp.concatenate([v for g in grads for v in lanes(g, HEAD, LHEAD)], axis=1)
    to = jnp.concatenate(lanes(o, 0, HEAD), axis=1)
    lo = jnp.concatenate(lanes(o, HEAD, LHEAD), axis=1)
    et, el = hs * HEAD, hs * LHEAD

    def scaled(value, size, width):
        lane = lax.broadcasted_iota(jnp.int32, value.shape, 1)
        return jnp.where(lane < size, value * width**-0.5, value)

    text = jnp.concatenate(
        [scaled(mm(x[:, 0:d], tq, TN), et, HEAD).astype(BF), mm(up[:, 0:d], to, TN).astype(BF)], axis=1
    )
    lay = jnp.concatenate(
        [scaled(mm(x[:, d:], lq, TN), el, LHEAD).astype(BF), mm(up[:, d:], lo, TN).astype(BF)], axis=1
    )
    put_halves(text, lay, pages, ids, keep, send, 0, 1)
    qb[...] = jnp.zeros_like(qb)
    sums = jnp.sum(tq.astype(F32), axis=0, keepdims=True)
    qb[0:1, 0 : 3 * et] = scaled(sums, et, HEAD)
    sums = jnp.sum(lq.astype(F32), axis=0, keepdims=True)
    qb[0:1, d : d + 3 * el] = scaled(sums, el, LHEAD)


def smalls_body(ids, *refs):
    one, two, fb, qb, out = refs
    rows = (one[0:1], two[0:1], one[2:3], one[1:2], two[2:3], two[1:2], fb[0:1, :], qb[0:1, :])
    for i, row in enumerate(rows):
        out[i : i + 1, :] = row


def own_block(refs, rows, n):
    value = cat(refs)
    return jnp.concatenate([value[2 * k * rows : (2 * k + 1) * rows] for k in range(n)], axis=0)


def away_body(n, cut, ids, *refs):
    out = refs[-1]
    rows = out.shape[0] // n

    @pl.when(ids[0] == 0)
    def _():
        out[...] = own_block(refs[cut:-1], rows, n)

    @pl.when(ids[0] != 0)
    def _():
        out[...] = own_block(refs[0:cut], rows, n)


def both_body(n, cut, d, ids, *refs):
    got, text, lay = refs[-3:]
    parts = refs[:-3]
    s = ids[0]
    rows = got.shape[0] // n
    text[1 - s] = got[:, 0:d]
    lay[1 - s] = got[:, d:].astype(F32).T.astype(BF)

    def put(refs):
        mine = own_block(refs, rows, n)
        text[s] = mine[:, 0:d]
        lay[s] = mine[:, d:].astype(F32).T.astype(BF)

    @pl.when(s == 0)
    def _():
        put(parts[0:cut])

    @pl.when(s != 0)
    def _():
        put(parts[cut:])


def add_body(ids, keep, got, out):
    out[...] = (keep[...].astype(F32) + got[...].astype(F32)).astype(BF)


def halve_body(bit, size, ids, a, b, keep, send):
    mine = lax.rem(ids[2] // bit, 2)
    for i in range(keep.shape[0] // size):
        for ref, side in ((keep, mine), (send, 1 - mine)):
            at = pl.ds(pl.multiple_of((2 * i + side) * size, 8), size)
            ref[i * size : (i + 1) * size, :] = (a[at, :].astype(F32) + b[at, :].astype(F32)).astype(BF)


def swap_body(ids, a, b, away):
    @pl.when(ids[0] == 0)
    def _():
        away[...] = b[...]

    @pl.when(ids[0] != 0)
    def _():
        away[...] = a[...]


def small_halves_body(ids, both, shared, mine, away):
    n = shared.shape[0] // 2

    def put(layer, ref):
        ref[0:n, :] = shared[layer * n : (layer + 1) * n, :]
        ref[n:, :] = both[layer * 8 + n : (layer + 1) * 8, :]

    @pl.when(ids[0] == 0)
    def _():
        put(0, mine)
        put(1, away)

    @pl.when(ids[0] != 0)
    def _():
        put(1, mine)
        put(0, away)


def own_rows(ids, a, b, got, tr, ll, lanes):
    own = jnp.where(ids[0] == 0, a.astype(F32), b.astype(F32))
    oth = got.astype(F32)
    first = jnp.where(ids[0] == 0, own, oth)
    second = jnp.where(ids[0] == 0, oth, own)
    text = jnp.concatenate([first[0:tr], second[0:tr]], axis=0)
    lay = jnp.concatenate(
        [
            half[tr:, g * lanes : (g + 1) * lanes]
            for half in (first, second)
            for g in range(ll // (first.shape[0] - tr))
        ],
        axis=0,
    )
    return text, lay


def matrices_body(tr, ll, ids, a, b, got, *outs):
    rows = a.shape[0] // (len(outs) // 2)
    for i in range(len(outs) // 2):
        at = slice(i * rows, (i + 1) * rows)
        text, lay = outs[2 * i : 2 * i + 2]
        text[...], lay[...] = own_rows(ids, a[at, :], b[at, :], got[at, :], tr, ll, lay.shape[1])


def proj_body(tr, ll, ids, a, b, got, qkv, out, lqkv, lout):
    et = qkv.shape[2]
    el = lqkv.shape[2]
    t, l = own_rows(ids, a[...], b[...], got[...], tr, ll, 4 * el)
    for c in range(3):
        qkv[c] = t[:, c * et : (c + 1) * et]
        lqkv[c] = l[:, c * el : (c + 1) * el]
    out[...] = t[:, 3 * et :].T
    lout[...] = l[:, 3 * el :].T


def swap(value, axis, bit):
    size = lax.axis_size(axis)
    return lax.ppermute(value, axis, [(i, i ^ bit) for i in range(size)])


def core_swap(value):
    return swap(value, "tensor", 1)


def chip_swap(value):
    return swap(value, "tensor", 2)


def other_section(value):
    return swap(value, "section", 1)


def around(value, axis):
    size = lax.axis_size(axis)
    return lax.ppermute(value, axis, [(i, (i + 1) % size) for i in range(size)])


def per_device(
    text_in,
    layout_in,
    text_cot,
    layout_cot,
    token_mask,
    box_mask,
    segments,
    text_qkv,
    text_qv_bias,
    text_out_w,
    text_ffn_in,
    text_ffn_bias,
    text_ffn_out,
    text_gains,
    text_biases,
    layout_qkv,
    layout_qv_bias,
    layout_out_w,
    layout_ffn_in,
    layout_ffn_bias,
    layout_ffn_out,
    layout_gains,
    layout_biases,
):
    sections = lax.axis_size("section")
    section = lax.axis_index("section")
    pages = lax.axis_size("dp")
    micro, mine, d = text_in.shape
    assert micro == sections == 2 and lax.axis_size("tensor") == 4 and segments.shape[1] == 1
    n = CHUNKS
    dl = layout_in.shape[2]
    width = d + dl
    rows = 4 * mine
    mine_rows = mine
    own = 2 * mine
    cb = mine // n
    hk = 2 * cb
    hs = text_qkv.shape[-1] // HEAD
    heads = 2 * hs
    f = text_ffn_in.shape[-1]
    fl = layout_ffn_in.shape[-1]
    fw = 2 * (f + fl)
    et, el = hs * HEAD, hs * LHEAD
    wq = heads * TILE
    part = functools.partial
    ids = Turn(
        jnp.stack([section, lax.axis_index("tensor"), lax.axis_index("dp")]).astype(jnp.int32)
    )

    pieces = pages if pages <= 4 else 1
    arows = 3 * et + el + et + LHEAD
    attn_own, piece = call(
        part(attn_send_body, pieces),
        [((arows, d), BF), ((arows // 2 // pieces, d), BF)],
        "attn_send",
    )(
        ids,
        jnp.swapaxes(text_qkv[0], 1, 2),
        jnp.swapaxes(layout_qkv[0], 1, 2),
        text_out_w[0],
        layout_out_w[0],
        loose=range(4),
    )

    def spread(value):
        out = [other_section(value)]
        for k in range(1, pieces):
            out.append(lax.ppermute(out[0], "dp", [(i, (i + k) % pages) for i in range(pages)]))
        return out

    attn_got = spread(piece)
    x_mine = call(inputs_body, [((mine, width), BF)], "inputs")(
        ids, text_in, jnp.swapaxes(layout_in, 1, 2), loose=(0, 1)
    )[0]
    x_mate = chip_swap(x_mine)
    prm_own = call(params_body, [((16, width), F32)], "params")(
        ids,
        text_gains[0],
        text_biases[0],
        text_ffn_bias,
        text_qv_bias[0],
        layout_gains[0],
        layout_biases[0],
        layout_ffn_bias,
        layout_qv_bias[0],
        loose=range(8),
    )[0]
    prm_oth = other_section(prm_own)
    x_all = jnp.concatenate(
        [v[k * cb : (k + 1) * cb] for k in range(n) for v in (x_mine, x_mate)], axis=0
    )
    x_own = [x_all[k * hk : (k + 1) * hk] for k in range(n)]
    cot, segr, segc = call(
        part(side_body, n),
        [((mine, width + 64), BF), ((1, rows), jnp.int32), ((rows, TILE), F32)],
        "side",
    )(
        ids,
        text_cot,
        jnp.swapaxes(layout_cot, 1, 2),
        token_mask,
        box_mask,
        segments.reshape(micro, 4, mine),
        loose=range(5),
    )

    x_peer = core_swap(x_all)
    cot_mate = chip_swap(cot)
    lead = call(first_half_body, [((arows // 2, d), BF)], "attn_lead", us=0.6)(
        ids, attn_own, after=attn_got[0:1]
    )[0]
    attn_direct = other_section(lead)
    frows = 2 * d + 2 * dl * dl // d
    ffn_own, piece = call(
        part(ffn_send_body, pieces),
        [((frows, d), BF), ((d // pieces, d), BF)],
        "ffn_send",
    )(
        ids, text_ffn_in[0], text_ffn_out[0], layout_ffn_in[0], layout_ffn_out[0],
        loose=range(4), after=[attn_direct, *attn_got],
    )
    ffn_got = spread(piece)
    weights = []

    def attn_weights(j, after=()):
        q_own, prm = call(
            part(pick_attn_body, j, pieces), [((arows, d), BF), ((16, width), F32)], "pick_attn", us=0.8
        )(ids, attn_own, attn_direct, prm_own, prm_oth, *attn_got, after=after)
        return q_own, prm

    def attn_packed(q_own, prm):
        wct, woc, bc, fb = call(
            part(pack_body, et, el, f, fl),
            [((3 * wq, width), BF), ((wq, width), BF), ((8, 3 * wq), F32), ((8, fw), F32)],
            "pack",
            us=1.5,
        )(ids, q_own, core_swap(q_own), prm, core_swap(prm))
        return wct, woc, bc, prm, fb

    def ffn_weights(j, after=()):
        w_own = call(part(pick_ffn_body, j, pieces, d), [((frows, d), BF)], "pick_ffn", us=1)(
            ids, ffn_own, ffn_direct, *ffn_got, after=after
        )[0]
        w_mate = core_swap(w_own)
        w1l, w2l = call(
            part(unfold_body, d), [((dl, 2 * fl), BF), ((2 * fl, dl), BF)], "unfold", us=0.6
        )(ids, w_own, w_mate)
        return w_own, w_mate, w1l, w2l

    picked = attn_weights(0, [x_peer])
    ffn_lead = call(part(ffn_lead_body, d), [((frows - d, d), BF)], "ffn_lead", us=0.6)(
        ids, ffn_own, after=ffn_got[0:1]
    )[0]
    ffn_direct = other_section(ffn_lead)
    attn_w = attn_packed(*picked)

    qkv_outs = [((hk, wq), BF), ((hk, 2 * wq), BF)]
    norm_outs = [((hk, width), F32), ((hk, TILE), F32)]
    row_out = ((hk, width), BF)
    mate_out = ((hk, width + f + fl), BF)
    outs = call(part(project_body, n), qkv_outs[0:1] * n + qkv_outs[1:2] * (2 * n), "project", us=3)(
        ids, attn_w[0], attn_w[2], x_all, x_peer
    )
    q, kv, peer = outs[0:n], outs[n : 2 * n], outs[2 * n :]

    own_row = ((own, width), BF)
    back_outs = [((own, width), F32), own_row, ((8, width), F32)]
    kept = []
    hidden = []
    for j in range(sections):
        wct, woc, bc, prm, fb = attn_w
        *s, oc, lse, xa = call(
            part(attn_body, n),
            [row_out] * n + [((own, wq), BF), ((8, own), F32), ((own, up_to_tile(width + wq // 2)), BF)],
            "attn",
            us=4,
            hbm=(n + 2,),
        )(ids, segc, segr, woc, *x_own, *q, *kv, *peer, after=[cot_mate] if j == 0 else mates_up)
        r = [chip_swap(v) for v in s]
        xa = core_swap(xa)
        attn_next = attn_packed(*attn_weights(j + 1, ffn_got[1:])) if j + 1 < sections else None
        ffn_w = ffn_weights(j, r[0:1] if j == 0 else ())
        weights.append((wct, woc, bc, prm, fb, ffn_w))
        s2, n1, inv1, xb, act, slope, xf = ([] for _ in range(7))
        for k in range(n):
            outs = call(
                ffn_body,
                [row_out] + norm_outs + [row_out] + [((hk, fw), BF)] * 2 + [mate_out],
                "ffn",
                us=2 if j + 1 < sections else 60,
                hbm=(6,),
            )(ids, s[k], r[k], x_own[k], prm, fb, *ffn_w, after=[xa] if k == n - 1 else [])
            for got, value in zip((s2, n1, inv1, xb, act, slope, xf), outs):
                got.append(value)
        r2 = [chip_swap(v) for v in s2]
        xf = [core_swap(v) for v in xf]
        mates_up = xf
        kept.append((x_own, q, kv, peer, oc, lse, n1, inv1, xb, act, slope, xa, xf))
        y, n2, inv2 = ([] for _ in range(3))
        if j + 1 < sections:
            q, kv, peer = [], [], []
            for k in range(n):
                outs = call(
                    part(norm_project_body, d), norm_outs + [row_out] + qkv_outs, "norm_project", us=2
                )(
                    ids, s2[k], r2[k], n1[k], prm, attn_next[0], attn_next[2],
                )
                for got, value in zip((n2, inv2, y, q, kv), outs):
                    got.append(value)
                peer.append(core_swap(kv[k]))
            kept[j] = kept[j] + (n2, inv2)
            x_own = y
            attn_w = attn_next
        else:
            call(wait_body, [], "wait", us=1)(ids, after=[r2[0], xf[0]])
            last, dh2, dh2b, small2, dpre, s1, *xt = call(
                part(turn_body, n),
                [own_row] + back_outs + [((own, fw), BF), own_row] + [mate_out] * n,
                "turn",
                (pltpu.VMEM((own, width), F32), pltpu.VMEM((own, TILE), F32)),
                us=5,
                vmem=14,
            )(ids, prm, *ffn_w, cot, cot_mate, *s2, *r2, *n1, *slope)
            y = [last]
        hidden.append(y)

    tr = d // (2 * pages)
    ll = dl // (2 * pages)
    grows = tr + (8 if ll % 8 == 0 else ll)

    def grad_outs(count):
        return [((count * pages * grows, d), BF)] * 2 + [((8, width), F32)]

    def over_pages(keep, got):
        value = call(add_body, [(keep.shape, BF)], "add", hbm=True)(ids, keep, got)[0]
        return lax.psum_scatter(value, "dp", scatter_dimension=0, tiled=True)

    class OverPages:
        def __init__(self, keep, got):
            self.a, self.b, self.bit = keep, got, 1
            self.size = keep.shape[0] // pages

        def step(self):
            if pages > 4:
                if self.bit == 1:
                    self.out = over_pages(self.a, self.b)
                    self.bit = pages
            elif self.bit < pages:
                rows = self.a.shape[0] // 2
                self.a, send = call(
                    part(halve_body, self.bit, self.size), [((rows, d), BF)] * 2, "halve", us=0.7
                )(ids, self.a, self.b)
                self.b = swap(send, "dp", self.bit)
                self.bit *= 2
            else:
                self.out = call(add_body, [(self.a.shape, BF)], "add", us=0.7)(ids, self.a, self.b)[0]

    def collect(layers):
        parts = list(layers[0]) + list(layers[1])
        cut = len(layers[0])
        away = call(part(away_body, n, cut), [((mine_rows, width), BF)], "away", us=0.6)(ids, *parts)[0]
        return parts, cut, other_section(away)

    def both(parts, cut, got):
        text, lay = call(
            part(both_body, n, cut, d),
            [((micro, mine_rows, d), BF), ((micro, dl, mine_rows), BF)],
            "both",
            hbm=True,
        )(ids, *parts, got)
        return text[None], jnp.swapaxes(lay, 1, 2)[None]

    ffn_grad = call(part(ffn_grad_body, d, f, fl, n, pages), grad_outs(2), "ffn_grad", us=5, vmem=16)
    attn_grad = call(part(attn_grad_body, d, n, pages), grad_outs(1), "attn_grad", us=4)
    hid = collect(hidden)
    input_grads = [None] * sections
    small_sums = [None] * sections
    for j in reversed(range(sections)):
        x_own, q, kv, peer, oc, lse, n1, inv1, xb, act, slope, xa, xf = kept[j][0:13]
        wct, woc, bc, prm, fb, ffn_w = weights[j]
        if j + 1 < sections:
            n2, inv2 = kept[j][13:]
            dxin, dh2, dh2b, small2, dpre, s1, *xt = call(
                part(back_next_body, n),
                [own_row] + back_outs + [((own, fw), BF), own_row] + [mate_out] * n,
                "back_next",
                us=5,
                vmem=14,
            )(ids, dh, s, r, prm, *ffn_w, *n2, *inv2, *slope)
            input_grads[j + 1] = [dxin]
        r1 = chip_swap(s1)
        if j == 0:
            attn_up = OverPages(*attn_pair)
            attn_up.step()
        keep, send, hsum = ffn_grad(
            ids, dh2b, dpre, *act, *xb, *xf, *[core_swap(v) for v in xt]
        )
        ffn_pair = (keep, other_section(send))
        if j == 0:
            ffn_up.step()
        dh, dhb, small1, dq, mine, *more = call(
            part(attn_back_body, n, d),
            back_outs + [((own, wq), BF), ((own, 2 * wq), F32)] + [((hk, 2 * wq), BF)] * n + [row_out] * n,
            "attn_back",
            us=7,
            vmem=14,
        )(ids, dh2, s1, r1, prm, segc, segr, woc, lse, *n1, *inv1, *q, *kv, *peer)
        far = [core_swap(v) for v in more[0:n]]
        ups = [core_swap(v) for v in more[n:]]
        s, dkv, *xd = call(
            part(dx_body, n),
            [own_row, ((own, 2 * wq), BF)] + [((hk, 3 * wq // 2), BF)] * n,
            "dx",
            us=2.5,
        )(ids, dq, mine, wct, *far)
        r = chip_swap(s)
        keep, send, hq = attn_grad(
            ids, dhb, dq, dkv, *x_own, *ups, *[core_swap(v) for v in xd], oc, xa
        )
        attn_pair = (keep, other_section(send))
        if j:
            ffn_up = OverPages(*ffn_pair)
            ffn_up.step()
        if j:
            small_sums[j] = call(smalls_body, [((8, width), F32)], "smalls", us=0.6)(
                ids, small1, small2, hsum, hq
            )[0]
    input_grads[0] = call(part(back_last_body, n), [own_row], "back_last", us=0.6)(ids, dh, s, r)

    ing = collect(input_grads)
    small_sums[0] = call(smalls_body, [((8, width), F32)], "smalls", us=0.6)(
        ids, small1, small2, hsum, hq
    )[0]
    both_sums = jnp.concatenate(small_sums, axis=0)
    bit = 1
    while bit < pages:
        both_sums = both_sums + swap(both_sums, "dp", bit)
        bit *= 2
    shared_sums = jnp.concatenate([both_sums[0:6], both_sums[8:14]], axis=0)
    shared_sums = shared_sums + core_swap(shared_sums)
    shared_sums = shared_sums + chip_swap(shared_sums)
    attn_up.step()
    ffn_up.step()
    ffn_last = OverPages(*ffn_pair)
    ffn_last.step()
    ffn_last.step()
    attn_last = OverPages(*attn_pair)
    attn_last.step()
    small_mine, small_away = call(small_halves_body, [((8, width), F32)] * 2, "small_halves", us=0.6)(
        ids, both_sums, shared_sums
    )
    small_got = other_section(small_away)
    hid_t, hid_l = both(*hid)
    attn_last.step()
    ing_t, ing_l = both(*ing)
    attn_up.step()
    def away_half(a, b, loose):
        away = call(swap_body, [(a.shape, BF)], "swap", us=0.6)(ids, a, b, loose=loose)[0]
        return a, b, other_section(away)

    rs = (1,) if pages <= 4 else (0, 1)
    rs = () if pages <= 4 else (0, 1)
    ffn_last.step()
    ffn_parts = away_half(ffn_last.out, ffn_up.out, rs)
    attn_last.step()
    attn_parts = away_half(attn_last.out, attn_up.out, rs)
    g2, lg2, g1, lg1 = call(
        part(matrices_body, tr, ll),
        [((2 * tr, f), F32), ((2 * ll, fl), F32)] * 2,
        "matrices",
        hbm=True,
    )(ids, *ffn_parts, loose=rs)
    g_qkv, g_out, g_lqkv, g_lout = call(
        part(proj_body, tr, ll),
        [((3, 2 * tr, et), F32), ((et, 2 * tr), F32), ((3, 2 * ll, el), F32), ((el, 2 * ll), F32)],
        "proj",
        hbm=True,
    )(ids, *attn_parts, loose=rs)

    total = small_mine + small_got
    shared = total[0:6]
    qv = total[7, 0 : 3 * et].reshape(3, et)
    lqv = total[7, d : d + 3 * el].reshape(3, el)
    return (
        hid_t,
        hid_l,
        ing_t,
        ing_l,
        g_qkv[None],
        jnp.stack([qv[0], qv[2]])[None],
        g_out[None],
        g1[None],
        total[6:7, 0:f],
        g2.T[None],
        shared[None, 0:2, 0:d],
        shared[None, 2:6, 0:d],
        g_lqkv[None],
        jnp.stack([lqv[0], lqv[2]])[None],
        g_lout[None],
        lg1[None],
        total[6:7, f:fw],
        lg2.T[None],
        shared[None, 0:2, d:],
        shared[None, 2:6, d:],
    )


def solution(mesh):
    in_specs = (
        P(None, ("dp", "tensor"), None),
        P(None, ("dp", "tensor"), None),
        P(None, ("dp", "tensor"), None),
        P(None, ("dp", "tensor"), None),
        P(None, ("dp", "tensor")),
        P(None, ("dp", "tensor")),
        P(None, "dp", None),
        P("section", None, None, "tensor"),
        P("section", None, "tensor"),
        P("section", "tensor", None),
        P("section", None, "tensor"),
        P("section", "tensor"),
        P("section", "tensor", None),
        P("section", None, None),
        P("section", None, None),
        P("section", None, None, "tensor"),
        P("section", None, "tensor"),
        P("section", "tensor", None),
        P("section", None, "tensor"),
        P("section", "tensor"),
        P("section", "tensor", None),
        P("section", None, None),
        P("section", None, None),
    )
    out_specs = (
        P("section", None, ("dp", "tensor"), None),
        P("section", None, ("dp", "tensor"), None),
        P("section", None, ("dp", "tensor"), None),
        P("section", None, ("dp", "tensor"), None),
        P("section", None, "dp", "tensor"),
        P("section", None, "tensor"),
        P("section", "tensor", "dp"),
        P("section", "dp", "tensor"),
        P("section", "tensor"),
        P("section", "tensor", "dp"),
        P("section", None, None),
        P("section", None, None),
        P("section", None, "dp", "tensor"),
        P("section", None, "tensor"),
        P("section", "tensor", "dp"),
        P("section", "dp", "tensor"),
        P("section", "tensor"),
        P("section", "tensor", "dp"),
        P("section", None, None),
        P("section", None, None),
    )
    return jax.shard_map(
        per_device, mesh=mesh, in_specs=in_specs, out_specs=out_specs, check_vma=False
    )
```
